32 devices in a mesh: fsdp: 32 (over z, y, x, core).
Axes of the slice: x: 2, y: 2, z: 4, core: 2. Of those that a mesh axis runs over, the one named last changes fastest.
Arguments:
- tokens: bfloat16 [32768, 768], P('fsdp'), may hold values from -6 to 6
- cotangent: bfloat16 [32768, 768], P('fsdp'), may hold values from -6 to 6
- packed_slot: int32 [32768], replicated, may hold values from 0 to 32767, as said below
- seq_lengths: int32 [32, 4], P('fsdp'), may hold values from 1 to 512, 1024 in all within a row
- query_weight: bfloat16 [589824], P('fsdp'), may hold values from -0.21875 to 0.21875
- query_bias: bfloat16 [768], P('fsdp'), may hold values from -3 to 3
- key_weight: bfloat16 [589824], P('fsdp'), may hold values from -0.21875 to 0.21875
- value_weight: bfloat16 [589824], P('fsdp'), may hold values from -0.21875 to 0.21875
- value_bias: bfloat16 [768], P('fsdp'), may hold values from -3 to 3
- output_weight: bfloat16 [589824], P('fsdp'), may hold values from -0.875 to 0.875
- output_bias: bfloat16 [768], P('fsdp'), may hold values from -3 to 3
- attention_gain: bfloat16 [768], P('fsdp'), may hold values from 0.5 to 1.5
- attention_shift: bfloat16 [768], P('fsdp'), may hold values from -3 to 3
- inner_weight: bfloat16 [2359296], P('fsdp'), may hold values from -0.21875 to 0.21875
- inner_bias: bfloat16 [3072], P('fsdp'), may hold values from -3 to 3
- outer_weight: bfloat16 [2359296], P('fsdp'), may hold values from -0.109375 to 0.109375
- outer_bias: bfloat16 [768], P('fsdp'), may hold values from -3 to 3
- final_gain: bfloat16 [768], P('fsdp'), may hold values from 0.5 to 1.5
- final_shift: bfloat16 [768], P('fsdp'), may hold values from -3 to 3
Outputs:
- layer_out: bfloat16 [32768, 768], P('fsdp')
- tokens_grad: bfloat16 [32768, 768], P('fsdp')
- query_weight_grad: float32 [589824], P('fsdp')
- query_bias_grad: float32 [768], P('fsdp')
- key_weight_grad: float32 [589824], P('fsdp')
- value_weight_grad: float32 [589824], P('fsdp')
- value_bias_grad: float32 [768], P('fsdp')
- output_weight_grad: float32 [589824], P('fsdp')
- output_bias_grad: float32 [768], P('fsdp')
- attention_gain_grad: float32 [768], P('fsdp')
- attention_shift_grad: float32 [768], P('fsdp')
- inner_weight_grad: float32 [2359296], P('fsdp')
- inner_bias_grad: float32 [3072], P('fsdp')
- outer_weight_grad: float32 [2359296], P('fsdp')
- outer_bias_grad: float32 [768], P('fsdp')
- final_gain_grad: float32 [768], P('fsdp')
- final_shift_grad: float32 [768], P('fsdp')
The draws below stay inside these ranges and needn't reach their ends.
Inputs may be any that keep to these rules, and one draw needn't show every extreme that they name: `packed_slot`: a permutation of the 32768 rows; of each aligned block of 1024 given rows exactly 32 have their packed row in each aligned block of 1024 packed rows. `seq_lengths`: each row sums to 1024 and its largest entry is 512.
All inputs are finite; a program needn't handle non-finite values.
Results may differ from the reference program's by a relative error of at most 0.013.
Values may be sent and summed in bfloat16 or wider, within the bound.
A program may use at most 192 MiB of HBM per device.

```python
import math
import jax
import jax.numpy as jnp
import numpy as np
from jax import lax

D = 768
H = 12
HD = 64
FF = 3072
TOK_DEV = 1024
SEQ_DEV = 4
SEQ_MAX = 512
TOKENS = 32768
PEER_ROWS = 32
N_FSDP = 32


def draw_packed_slot(key, part):
    first_key = jax.random.fold_in(key, 11)
    second_key = jax.random.fold_in(key, 23)
    targets = jax.vmap(lambda sub: jax.random.permutation(sub, TOK_DEV))(jax.random.split(first_key, N_FSDP))
    targets = targets.astype(jnp.int32).reshape(N_FSDP, N_FSDP, PEER_ROWS)
    offsets = (jnp.arange(N_FSDP, dtype=jnp.int32) * TOK_DEV)[:, None, None]
    targets = (targets + offsets).transpose(1, 0, 2).reshape(N_FSDP, TOK_DEV)
    orders = jax.vmap(lambda sub: jax.random.permutation(sub, TOK_DEV))(jax.random.split(second_key, N_FSDP))
    orders = orders.astype(jnp.int32)
    placed = jax.vmap(lambda vals, rows: jnp.zeros((TOK_DEV,), jnp.int32).at[rows].set(vals))(targets, orders)
    return placed.reshape(TOKENS).astype(jnp.int32)


def shard_levels(stream_key, shape, pieces, smallest, largest):
    level = 1.0
    for axis_at, parts in pieces:
        draws = jax.random.uniform(jax.random.fold_in(jax.random.fold_in(stream_key, 6), axis_at), (parts,), jnp.float32, smallest / len(pieces), largest / len(pieces))
        level = level * jnp.repeat(jnp.exp(draws), shape[axis_at] // parts).reshape((-1,) + (1,) * (len(shape) - 1 - axis_at))
    return level


def split_up(amount, total, most, slope):
    loads = [(1 << 20) // math.isqrt(rank ** slope) + 1 for rank in range(2, amount + 1)]
    rest, given = total - most - (amount - 1), [1] * (amount - 1)
    while rest > 0:
        movable = [i for i in range(amount - 1) if given[i] < most]
        mass, remaining = sum([loads[i] for i in movable]), rest
        for i in movable:
            extra = min(most - given[i], max(1, remaining * loads[i] // mass), rest)
            given[i] = given[i] + extra
            rest = rest - extra
    return np.array([most] + given)


def uneven(stream_key, count, total, most, slope):
    if count == 2:
        one = jax.random.randint(stream_key, (), max(1, total - most), min(most, total - 1) + 1)
        return jnp.stack([one, total - one])
    sizes = jnp.asarray(split_up(count, total, most, slope), jnp.int32)
    twos = (count - 1) // 2
    source_of, sink = sizes[1:1 + 2 * twos:2], sizes[2:2 + 2 * twos:2]
    room = jnp.minimum(source_of - 1, most - sink)
    shifted = jax.random.randint(jax.random.fold_in(stream_key, 1), (twos,), 0, 1 << 20) % (room + 1)
    sizes = sizes.at[1:1 + 2 * twos:2].set(source_of - shifted).at[2:2 + 2 * twos:2].set(sink + shifted)
    return sizes[jax.random.permutation(jax.random.fold_in(stream_key, 2), count)]


def normal_values(own_key, extent, deviation, reach, cuts=(), kind=jnp.bfloat16):
    factor_of = shard_levels(own_key, extent, cuts, -0.22, 0.18) if cuts else 1.0
    entries = jax.random.normal(own_key, extent, jnp.float32) * deviation * factor_of
    return jnp.minimum(jnp.maximum(entries, -reach), reach).astype(kind)


def setup_inputs(seed: int = 0) -> dict:
    splits = jax.random.split(jax.random.key(seed), 20)
    return {
        "tokens": normal_values(splits[0], (TOKENS, D), 1.0, 6.0, ((0, 32),)),
        "cotangent": normal_values(splits[1], (TOKENS, D), 1.0, 6.0, ((0, 32),)),
        "packed_slot": draw_packed_slot(jax.random.fold_in(splits[19], 71), 0),
        "seq_lengths": jax.vmap(lambda own: uneven(own, SEQ_DEV, TOK_DEV, SEQ_MAX, 2))(jax.random.split(splits[3], N_FSDP)).reshape((N_FSDP, SEQ_DEV)).astype(jnp.int32),
        "query_weight": normal_values(splits[4], (D * D,), D ** -0.5, 0.21875, ((0, 32),)),
        "query_bias": normal_values(splits[5], (D,), 0.5, 3.0, ((0, 32),)),
        "key_weight": normal_values(splits[6], (D * D,), D ** -0.5, 0.21875, ((0, 32),)),
        "value_weight": normal_values(splits[7], (D * D,), D ** -0.5, 0.21875, ((0, 32),)),
        "value_bias": normal_values(splits[8], (D,), 0.5, 3.0, ((0, 32),)),
        "output_weight": normal_values(splits[9], (D * D,), (D // 16) ** -0.5, 0.875, ((0, 32),)),
        "output_bias": normal_values(splits[10], (D,), 0.5, 3.0, ((0, 32),)),
        "attention_gain": jnp.clip(1.0 + 0.1 * jax.random.normal(splits[11], (D,), jnp.float32), 0.5, 1.5).astype(jnp.bfloat16),
        "attention_shift": normal_values(splits[12], (D,), 0.5, 3.0, ((0, 32),)),
        "inner_weight": normal_values(splits[13], (D * FF,), D ** -0.5, 0.21875, ((0, 32),)),
        "inner_bias": normal_values(splits[14], (FF,), 0.5, 3.0, ((0, 32),)),
        "outer_weight": normal_values(splits[15], (FF * D,), FF ** -0.5, 0.109375, ((0, 32),)),
        "outer_bias": normal_values(splits[16], (D,), 0.5, 3.0, ((0, 32),)),
        "final_gain": jnp.clip(1.0 + 0.1 * jax.random.normal(splits[17], (D,), jnp.float32), 0.5, 1.5).astype(jnp.bfloat16),
        "final_shift": normal_values(splits[18], (D,), 0.5, 3.0, ((0, 32),)),
    }


@jax.custom_vjp
def low(v):
    return lax.optimization_barrier(v.astype(jnp.bfloat16)).astype(jnp.float32)

@jax.custom_vjp
def low_back(v):
    return v

def low_keep(v):
    return (low(v), None)

def low_pass(kept, grad):
    return (grad,)

def back_keep(v):
    return (v, None)

def back_low(kept, grad):
    return (low(grad),)
low.defvjp(low_keep, low_pass)
low_back.defvjp(back_keep, back_low)
EPSILON = 1e-12
NEG_LARGE = -1e+30

def exact_dot(left, right):
    return jnp.dot(left, right, precision=lax.Precision.HIGHEST)

def layer_norm(hidden, norm_gain, norm_shift):
    centered = hidden - lax.optimization_barrier(jnp.mean(hidden, axis=-1, keepdims=True))
    variance = lax.optimization_barrier(jnp.mean(centered * centered, axis=-1, keepdims=True))
    return centered * lax.rsqrt(variance + EPSILON) * norm_gain + norm_shift

def head_attention(inputs, visible):
    query_head, key_head, value_head = inputs
    scores = low_back(exact_dot(query_head, key_head.T) * 0.125)
    scores = jnp.where(visible, scores, NEG_LARGE)
    row_max = lax.optimization_barrier(jnp.max(scores, axis=-1, keepdims=True))
    raised = jnp.exp(scores - row_max)
    probs = raised / lax.optimization_barrier(jnp.sum(raised, axis=-1, keepdims=True))
    return exact_dot(low(probs), value_head)

def layer_forward(packed_rows, params, visible):
    query_weight, query_bias, key_weight, value_weight, value_bias, output_weight, output_bias, attention_gain, attention_shift, inner_weight, inner_bias, outer_weight, outer_bias, final_gain, final_shift = params
    row_count = packed_rows.shape[0]
    queries = low(low_back(exact_dot(packed_rows, query_weight) + query_bias))
    key_rows = low(low_back(exact_dot(packed_rows, key_weight)))
    values = low(low_back(exact_dot(packed_rows, value_weight) + value_bias))

    def split_heads(matrix):
        return matrix.reshape(row_count, H, HD).transpose(1, 0, 2)
    per_head = jax.checkpoint(lambda inputs: head_attention(inputs, visible))
    attended = lax.map(per_head, (split_heads(queries), split_heads(key_rows), split_heads(values)))
    attended = low(low_back(attended.transpose(1, 0, 2).reshape(row_count, D)))
    branch = low_back(exact_dot(attended, output_weight) + output_bias)
    normed = layer_norm(packed_rows + branch, attention_gain, attention_shift)
    inner_pre = low_back(exact_dot(low(normed), inner_weight) + inner_bias)
    activated = low(jax.nn.gelu(inner_pre, approximate=False))
    feed_out = low_back(exact_dot(activated, outer_weight) + outer_bias)
    return layer_norm(normed + feed_out, final_gain, final_shift)

def reference(tokens, cotangent, packed_slot, seq_lengths, query_weight, query_bias, key_weight, value_weight, value_bias, output_weight, output_bias, attention_gain, attention_shift, inner_weight, inner_bias, outer_weight, outer_bias, final_gain, final_shift):
    flats = (query_weight, query_bias, key_weight, value_weight, value_bias, output_weight, output_bias, attention_gain, attention_shift, inner_weight, inner_bias, outer_weight, outer_bias, final_gain, final_shift)
    shapes = ((D, D), (D,), (D, D), (D, D), (D,), (D, D), (D,), (D,), (D,), (D, FF), (FF,), (FF, D), (D,), (D,), (D,))
    params = tuple((flat.astype(jnp.float32).reshape(shape) for flat, shape in zip(flats, shapes)))
    packed_tokens = jnp.zeros((TOKENS, D), tokens.dtype).at[packed_slot].set(tokens).reshape(N_FSDP, TOK_DEV, D)
    packed_cot = jnp.zeros((TOKENS, D), cotangent.dtype).at[packed_slot].set(cotangent).reshape(N_FSDP, TOK_DEV, D)
    positions = jnp.arange(TOK_DEV, dtype=jnp.int32)

    def one_device(totals, inputs):
        packed_rows, rows_cot, lengths_row = inputs
        ends = jnp.cumsum(lengths_row, dtype=jnp.int32)
        segment = lax.optimization_barrier(jnp.sum((positions[:, None] >= ends[None, :]).astype(jnp.int32), axis=1, dtype=jnp.int32))
        visible = segment[:, None] == segment[None, :]
        result, pullback = jax.vjp(lambda rows, prm: layer_forward(rows, prm, visible), packed_rows.astype(jnp.float32), params)
        rows_grad, param_grads = pullback(rows_cot.astype(jnp.float32))
        totals = tuple((total + grad for total, grad in zip(totals, param_grads)))
        return (totals, (result.astype(jnp.bfloat16), rows_grad.astype(jnp.bfloat16)))
    initial = tuple((jnp.zeros_like(param) for param in params))
    totals, (results, grads) = lax.scan(one_device, initial, (packed_tokens, packed_cot, seq_lengths))
    layer_out = results.reshape(TOKENS, D)[packed_slot]
    tokens_grad = grads.reshape(TOKENS, D)[packed_slot]
    flat_grads = tuple((total.reshape(-1) for total in totals))
    return (layer_out, tokens_grad, flat_grads[0], flat_grads[1], flat_grads[2], flat_grads[3], flat_grads[4], flat_grads[5], flat_grads[6], flat_grads[7], flat_grads[8], flat_grads[9], flat_grads[10], flat_grads[11], flat_grads[12], flat_grads[13], flat_grads[14])
```

```python
from functools import partial

import jax
import jax.numpy as jnp
from jax import lax
from jax.experimental import pallas as pl
from jax.experimental.pallas import tpu as pltpu
from jax.sharding import PartitionSpec as P

HD = 64
LANES = 128
EPSILON = 1e-12
NEG_LARGE = -1e30
MIB = 1 << 20
F32 = jnp.float32
BF16 = jnp.bfloat16
MESH = pl.DeviceIdType.MESH


def dot_nn(a, b):
    return lax.dot_general(a, b, (((1,), (0,)), ((), ())), preferred_element_type=F32)


def dot_nt(a, b):
    return lax.dot_general(a, b, (((1,), (1,)), ((), ())), preferred_element_type=F32)


def dot_tn(a, b):
    return lax.dot_general(a, b, (((0,), (0,)), ((), ())), preferred_element_type=F32)


def full_spec(shape, **kw):
    return pl.BlockSpec(shape, lambda *_: (0,) * len(shape), **kw)


def held_spec(shape):
    return full_spec(shape, pipeline_mode=pl.Buffered(1))


def params(mib, *axes, **kw):
    return pltpu.CompilerParams(
        dimension_semantics=axes or None, vmem_limit_bytes=mib * MIB, **kw
    )


def grid_of(devices):
    return {32: (4, 2, 2, 2), 128: (4, 4, 4, 2)}.get(devices, (devices, 1, 1, 1))


def gather_kernel(sizes, half, w4, wi, wu, vec, g4, gi, gu, gv, local_sem, sa, ra, sb, rb, sc, rc, sk, rk):
    na, nb, nc, nk = sizes
    me = lax.axis_index("fsdp")
    k = me % nk
    c = (me // nk) % nc
    b = (me // (nk * nc)) % nb
    a = me // (nk * nc * nb)

    def at(ja, jb, jc, jk=0):
        aa = (a + na - ja) % na
        bb = (b + nb - jb) % nb
        cc = (c + nc - jc) % nc
        kk = (k + nk - jk) % nk
        return ((aa * nb + bb) * nc + cc) * nk + kk

    rest = wu.shape[0] - half
    own = (w4, wi, wu.at[pl.ds(0, half)], wu.at[pl.ds(half, rest)], vec)

    def slot(dev):
        return (
            g4.at[:, dev],
            gi.at[dev],
            gu.at[dev, pl.ds(0, half)],
            gu.at[dev, pl.ds(half, rest)],
            gv.at[dev],
        )

    peers = [at(-j, 0, 0) for j in range(1, na)]
    peers += [at(0, -j, 0) for j in range(1, nb)]
    peers += [at(0, 0, -j) for j in range(1, nc)]
    peers += [at(0, 0, 0, -j) for j in range(1, nk)]
    barrier = pltpu.get_barrier_semaphore()
    for peer in peers:
        pl.semaphore_signal(barrier, inc=1, device_id=(peer,), device_id_type=MESH)
    pl.semaphore_wait(barrier, len(peers))

    started = []

    def send(source, target, send_sem, recv_sem, peer):
        copy = pltpu.make_async_remote_copy(
            src_ref=source, dst_ref=target, send_sem=send_sem, recv_sem=recv_sem,
            device_id=(peer,), device_id_type=MESH,
        )
        copy.start()
        started.append(copy)

    def arrive(piece, send_sem, recv_sem):
        pltpu.make_async_remote_copy(
            src_ref=piece, dst_ref=piece, send_sem=send_sem, recv_sem=recv_sem,
            device_id=(me,), device_id_type=MESH,
        ).wait_recv()

    mine = slot(me)
    local = []
    for p in range(5):
        for j in range(1, na):
            send(own[p], mine[p], sa.at[p, j], ra.at[p, j], at(-j, 0, 0))
    for p in range(5):
        copy = pltpu.make_async_copy(own[p], mine[p], local_sem.at[p])
        copy.start()
        local.append(copy)
    first = (0, 4, 2)
    second = (1, 3)

    def source_of(p, ja, jb, jc):
        if ja == 0 and jb == 0 and jc == 0:
            return own[p], mine[p]
        piece = slot(at(ja, jb, jc))[p]
        return piece, piece

    def to_b(p, ja, jc):
        source, target = source_of(p, ja, 0, jc)
        for j in range(1, nb):
            send(source, target, sb.at[p, ja, jc, j], rb.at[p, ja, jc, j], at(0, -j, 0))

    def to_c(p, ja, jb):
        source, target = source_of(p, ja, jb, 0)
        for j in range(1, nc):
            send(source, target, sc.at[p, ja, jb, j], rc.at[p, ja, jb, j], at(0, 0, -j))

    def to_k(p, ja, jb, jc):
        source, target = source_of(p, ja, jb, jc)
        for j in range(1, nk):
            send(source, target, sk.at[p, ja, jb, jc, j], rk.at[p, ja, jb, jc, j], at(0, 0, 0, -j))

    for ja in range(na):
        for p in first + second:
            if ja:
                arrive(slot(at(ja, 0, 0))[p], sa.at[p, ja], ra.at[p, ja])
            if p in first:
                to_b(p, ja, 0)
                to_c(p, ja, 0)
            else:
                to_c(p, ja, 0)
                to_b(p, ja, 0)
            to_k(p, ja, 0, 0)
    for ja in range(na):
        for p in first + second:
            if p in first:
                for j in range(1, nb):
                    arrive(slot(at(ja, j, 0))[p], sb.at[p, ja, 0, j], rb.at[p, ja, 0, j])
                    to_c(p, ja, j)
                    to_k(p, ja, j, 0)
            else:
                for j in range(1, nc):
                    arrive(slot(at(ja, 0, j))[p], sc.at[p, ja, 0, j], rc.at[p, ja, 0, j])
                    to_b(p, ja, j)
                    to_k(p, ja, 0, j)
    for ja in range(na):
        for p in first + second:
            if p in first:
                for j in range(nb):
                    for i in range(1, nc):
                        arrive(slot(at(ja, j, i))[p], sc.at[p, ja, j, i], rc.at[p, ja, j, i])
                        to_k(p, ja, j, i)
            else:
                for i in range(nc):
                    for j in range(1, nb):
                        arrive(slot(at(ja, j, i))[p], sb.at[p, ja, i, j], rb.at[p, ja, i, j])
                        to_k(p, ja, j, i)
    for ja in range(na):
        for jb in range(nb):
            for jc in range(nc):
                for p in first + second:
                    for j in range(1, nk):
                        arrive(
                            slot(at(ja, jb, jc, j))[p],
                            sk.at[p, ja, jb, jc, j],
                            rk.at[p, ja, jb, jc, j],
                        )
    for copy in local:
        copy.wait()
    for copy in started:
        copy.wait_send()


def gather_parameters(devices, w4, wi, wu, vec):
    sizes = grid_of(devices)
    na, nb, nc, nk = sizes
    rows = w4.shape[1]
    dma = pltpu.SemaphoreType.DMA
    anywhere = pl.BlockSpec(memory_space=pl.ANY)
    return pl.pallas_call(
        partial(gather_kernel, sizes, wu.shape[0] // 16 * 8),
        out_shape=(
            jax.ShapeDtypeStruct((4, devices) + w4.shape[1:], BF16),
            jax.ShapeDtypeStruct((devices,) + wi.shape, BF16),
            jax.ShapeDtypeStruct((devices,) + wu.shape, BF16),
            jax.ShapeDtypeStruct((devices,) + vec.shape, BF16),
        ),
        in_specs=[anywhere] * 4,
        out_specs=[anywhere] * 4,
        scratch_shapes=[dma((5,))]
        + [dma((5, na))] * 2
        + [dma((5, na, nc, nb))] * 2
        + [dma((5, na, nb, nc))] * 2
        + [dma((5, na, nb, nc, nk))] * 2,
        compiler_params=pltpu.CompilerParams(collective_id=1, has_side_effects=True),
    )(w4, wi, wu, vec)


def permute_kernel(tile, where_ref, rows_ref, out_ref):
    count = where_ref.shape[1]
    target = lax.broadcasted_iota(jnp.int32, (tile, count), 0) + pl.program_id(0) * tile
    chosen = jnp.where(where_ref[...] == target, 1.0, 0.0).astype(BF16)
    out_ref[...] = dot_nn(chosen, rows_ref[...]).astype(BF16)


def permute_rows(where_row, rows):
    count, width = rows.shape
    tile = count // 4
    return pl.pallas_call(
        partial(permute_kernel, tile),
        grid=(4,),
        out_shape=jax.ShapeDtypeStruct(rows.shape, BF16),
        in_specs=[full_spec((1, count)), full_spec((count, width))],
        out_specs=pl.BlockSpec((tile, width), lambda i: (i, 0)),
        compiler_params=params(32, "arbitrary"),
        name="permute_rows",
    )(where_row, rows)


def unpermute_kernel(from_ref, rows_ref, out_ref):
    tile, count = out_ref.shape[0], rows_ref.shape[0]
    lane = lax.broadcasted_iota(jnp.int32, (tile, count), 1)
    chosen = jnp.where(from_ref[...] == lane, 1.0, 0.0).astype(BF16)
    out_ref[...] = dot_nn(chosen, rows_ref[...]).astype(BF16)


def unpermute_rows(from_col, rows):
    count, width = rows.shape
    tile = count // 4
    return pl.pallas_call(
        unpermute_kernel,
        grid=(4,),
        out_shape=jax.ShapeDtypeStruct(rows.shape, BF16),
        in_specs=[pl.BlockSpec((tile, 1), lambda i: (i, 0)), full_spec((count, width))],
        out_specs=pl.BlockSpec((tile, width), lambda i: (i, 0)),
        compiler_params=params(32, "arbitrary"),
        name="unpermute_rows",
    )(from_col, rows)


LOW = 32


def source_kernel(slots_ref, out_ref):
    devices, count = slots_ref.shape
    high = out_ref.shape[0]

    def body(s, total):
        local = slots_ref[pl.ds(s, 1), :]
        in_high = lax.broadcasted_iota(jnp.int32, (high, count), 0) == (local >> 5)
        in_low = lax.broadcasted_iota(jnp.int32, (LOW, count), 0) == (local & (LOW - 1))
        weight = jnp.where(in_high, s.astype(F32), 0.0).astype(BF16)
        return total + dot_nt(weight, jnp.where(in_low, 1.0, 0.0).astype(BF16))

    out_ref[...] = lax.fori_loop(0, devices, body, jnp.zeros((high, LOW), F32))


def source_devices(local_slots, count):
    return pl.pallas_call(
        source_kernel,
        out_shape=jax.ShapeDtypeStruct((count // LOW, LOW), F32),
        in_specs=[pl.BlockSpec(memory_space=pltpu.VMEM)],
        out_specs=pl.BlockSpec(memory_space=pltpu.VMEM),
        name="source_devices",
    )(local_slots)


def project_kernel(place_ref, arrived_ref, wq_ref, wk_ref, wv_ref, vec_ref, rows_ref, q_ref, k_ref, v_ref):
    tile, count = rows_ref.shape[0], arrived_ref.shape[0]
    lane = lax.broadcasted_iota(jnp.int32, (tile, count), 1)
    chosen = jnp.where(place_ref[...] == lane, 1.0, 0.0).astype(BF16)
    rows = dot_nn(chosen, arrived_ref[...]).astype(BF16)
    rows_ref[...] = rows
    vec = vec_ref[...]
    q_ref[...] = ((dot_nn(rows, wq_ref[...]) + vec[0:1]).astype(BF16).astype(F32) * 0.125).astype(BF16)
    k_ref[...] = dot_nn(rows, wk_ref[...]).astype(BF16)
    v_ref[...] = (dot_nn(rows, wv_ref[...]) + vec[1:2]).astype(BF16)


def project(place_col, arrived, w4, vec):
    count, width = arrived.shape
    tile = count // 4
    row_spec = pl.BlockSpec((tile, width), lambda i: (i, 0))

    def weight(n):
        return pl.BlockSpec((pl.Squeezed(), width, width), lambda i: (n, 0, 0), pipeline_mode=pl.Buffered(1))

    return pl.pallas_call(
        project_kernel,
        grid=(4,),
        out_shape=[jax.ShapeDtypeStruct((count, width), BF16)] * 4,
        in_specs=[pl.BlockSpec((tile, 1), lambda i: (i, 0)), held_spec((count, width)),
                  weight(0), weight(1), weight(2), held_spec(vec.shape)],
        out_specs=[row_spec] * 4,
        compiler_params=params(40, "arbitrary"),
        cost_estimate=pl.CostEstimate(flops=8 * count * width * width, bytes_accessed=14 * MIB, transcendentals=0),
        name="project",
    )(place_col, arrived, w4, w4, w4, vec)


def split3(column):
    high = column.astype(BF16).astype(F32)
    rest = column - high
    mid = rest.astype(BF16).astype(F32)
    return high, mid, rest - mid


def feature_lanes(rows):
    lane = lax.broadcasted_iota(jnp.int32, (rows, LANES), 1)
    return lane < HD, lane & (HD - 1)


def key_features(lane, segment, segments):
    return jnp.where(lane == segment, 1.0, jnp.where((lane >= segments) & (lane < segments + 3), 1.0, 0.0))


def query_features(lane, segment, segments):
    return jnp.where((lane < segments) & (lane != segment), NEG_LARGE, 0.0)


def with_column(features, lane, start, column):
    high, mid, last = split3(column)
    features = jnp.where(lane == start, high, features)
    features = jnp.where(lane == start + 1, mid, features)
    return jnp.where(lane == start + 2, last, features)


def attend_kernel(segments, seg_ref, q_ref, seg_all_ref, k_ref, v_ref, out_ref, lse_ref, k0, k1):
    count, tile = k_ref.shape[0], q_ref.shape[0]
    first_all, lane_all = feature_lanes(count)

    @pl.when(pl.program_id(1) == 0)
    def _():
        extra = key_features(lane_all, seg_all_ref[...], segments).astype(BF16)
        k0[...] = jnp.where(first_all, k_ref[...], extra)
        k1[...] = jnp.where(first_all, extra, k_ref[...])

    first, lane = feature_lanes(tile)
    extra = query_features(lane, seg_ref[...], segments).astype(BF16)
    queries = q_ref[...]
    values = v_ref[...]
    outs, logs = [], []
    for mask, keys in ((first, k0), (~first, k1)):
        scores = dot_nt(jnp.where(mask, queries, extra), keys[...])
        top = jnp.max(scores, axis=1, keepdims=True)
        raised = jnp.exp(scores - top)
        total = jnp.sum(raised, axis=1, keepdims=True)
        outs.append(dot_nn(raised.astype(BF16), values) * (1.0 / total))
        logs.append(top + jnp.log(total))
    out_ref[...] = jnp.where(first, outs[0], outs[1]).astype(BF16)
    lse_ref[...] = jnp.where(first, logs[0], logs[1])


def attend(segments, segment_col, q, k, v):
    count, width = q.shape
    pairs = width // LANES
    tile = count // 4
    tile_spec = pl.BlockSpec((tile, LANES), lambda h, i: (i, h))
    all_spec = pl.BlockSpec((count, LANES), lambda h, i: (0, h))
    return pl.pallas_call(
        partial(attend_kernel, segments),
        grid=(pairs, 4),
        out_shape=[jax.ShapeDtypeStruct((count, width), BF16), jax.ShapeDtypeStruct((count, width), F32)],
        in_specs=[pl.BlockSpec((tile, 1), lambda h, i: (i, 0)), tile_spec, held_spec((count, 1)), all_spec, all_spec],
        out_specs=[tile_spec, tile_spec],
        scratch_shapes=[pltpu.VMEM((count, LANES), BF16)] * 2,
        compiler_params=params(40, "arbitrary", "arbitrary"),
        cost_estimate=pl.CostEstimate(flops=8 * count * count * width, bytes_accessed=10 * MIB, transcendentals=count * count * 12),
        name="attend",
    )(segment_col, q, segment_col, k, v)


def attend_back_kernel(segments, seg_ref, q_ref, o_ref, g_ref, lse_ref, seg_all_ref, k_ref, v_ref,
                       dq_ref, dk_ref, dv_ref, sums_ref, k0, k1, v0, v1, dk_sum, dv_sum):
    count, tile = k_ref.shape[0], q_ref.shape[0]
    first_all, lane_all = feature_lanes(count)
    step, last = pl.program_id(1), pl.num_programs(1) - 1

    @pl.when(step == 0)
    def _():
        extra = key_features(lane_all, seg_all_ref[...], segments).astype(BF16)
        k0[...] = jnp.where(first_all, k_ref[...], extra)
        k1[...] = jnp.where(first_all, extra, k_ref[...])
        v0[...] = jnp.where(first_all, v_ref[...], extra)
        v1[...] = jnp.where(first_all, extra, v_ref[...])
        dk_sum[...] = jnp.zeros_like(dk_sum)
        dv_sum[...] = jnp.zeros_like(dv_sum)
        sums_ref[...] = jnp.zeros_like(sums_ref)

    first, lane = feature_lanes(tile)
    hidden = query_features(lane, seg_ref[...], segments)
    queries, grads = q_ref[...], g_ref[...]
    product = grads.astype(F32) * o_ref[...].astype(F32)
    lses = lse_ref[...]
    dqs, dks, dvs = [], [], []
    for mask, keys, values, at in ((first, k0, v0, 0), (~first, k1, v1, HD)):
        lse = lses[:, at:at + 1]
        delta = jnp.sum(jnp.where(mask, product, 0.0), axis=1, keepdims=True)
        query = jnp.where(mask, queries, with_column(hidden, lane, segments, -lse).astype(BF16))
        grad = jnp.where(mask, grads, with_column(jnp.zeros_like(hidden), lane, segments, -delta).astype(BF16))
        probs = jnp.exp(dot_nt(keys[...], query))
        score = (probs * dot_nt(values[...], grad)).astype(BF16)
        dvs.append(dot_nn(probs.astype(BF16), grad))
        dks.append(dot_nn(score, query))
        dqs.append(dot_tn(score, keys[...]))
    dq = (jnp.where(first, dqs[0], dqs[1]) * 0.125).astype(BF16)
    dq_ref[...] = dq
    dk_sum[...] += jnp.where(first_all, dks[0], dks[1])
    dv_sum[...] += jnp.where(first_all, dvs[0], dvs[1])
    sums_ref[0:1, :] += jnp.sum(dq.astype(F32), axis=0, keepdims=True)

    @pl.when(step == last)
    def _():
        dk_ref[...] = dk_sum[...].astype(BF16)
        dv = dv_sum[...].astype(BF16)
        dv_ref[...] = dv
        sums_ref[1:2, :] += jnp.sum(dv.astype(F32), axis=0, keepdims=True)


def attend_back(segments, segment_col, q, out, grad, lse, k, v):
    count, width = q.shape
    pairs = width // LANES
    tile = count // 4
    tile_spec = pl.BlockSpec((tile, LANES), lambda h, i: (i, h))
    all_spec = pl.BlockSpec((count, LANES), lambda h, i: (0, h))
    return pl.pallas_call(
        partial(attend_back_kernel, segments),
        grid=(pairs, 4),
        out_shape=[jax.ShapeDtypeStruct((count, width), BF16)] * 3 + [jax.ShapeDtypeStruct((8, width), F32)],
        in_specs=[pl.BlockSpec((tile, 1), lambda h, i: (i, 0))] + [tile_spec] * 4 + [held_spec((count, 1)), all_spec, all_spec],
        out_specs=[tile_spec, all_spec, all_spec, pl.BlockSpec((8, LANES), lambda h, i: (0, h))],
        scratch_shapes=[pltpu.VMEM((count, LANES), BF16)] * 4 + [pltpu.VMEM((count, LANES), F32)] * 2,
        compiler_params=params(48, "arbitrary", "arbitrary"),
        cost_estimate=pl.CostEstimate(flops=20 * count * count * width, bytes_accessed=16 * MIB, transcendentals=count * count * 12),
        name="attend_back",
    )(segment_col, q, out, grad, lse, segment_col, k, v)


def normalize(hidden):
    centered = hidden - jnp.mean(hidden, axis=1, keepdims=True)
    variance = jnp.mean(centered * centered, axis=1, keepdims=True)
    inverse = lax.rsqrt(variance + EPSILON)
    return centered * inverse, inverse


def normalize_back(grad, normal, inverse):
    return inverse * (
        grad
        - jnp.mean(grad, axis=1, keepdims=True)
        - normal * jnp.mean(grad * normal, axis=1, keepdims=True)
    )


def column_sum(matrix):
    return jnp.sum(matrix.astype(F32), axis=0, keepdims=True)


def feed_kernel(chunk, place_ref, rows_ref, att_ref, cot_ref, wo_ref, wi_ref, wu_ref, vec_ref, bi_ref,
                out_ref, act_ref, inner_ref, normed_ref, outer_ref, low_ref, first_ref, agrad_ref,
                sums_ref, bisum_ref, slope_ref):
    tile, count = rows_ref.shape[0], cot_ref.shape[0]
    hidden_width = wi_ref.shape[1]
    step = pl.program_id(0)

    @pl.when(step == 0)
    def _():
        sums_ref[...] = jnp.zeros_like(sums_ref)
        bisum_ref[...] = jnp.zeros_like(bisum_ref)

    vec = vec_ref[...]
    bo, ga, sa, bu, gf, sf = (vec[i:i + 1] for i in range(2, 8))
    first_sum = rows_ref[...].astype(F32) + dot_nn(att_ref[...], wo_ref[...]) + bo
    normal1, inverse1 = normalize(first_sum)
    normed = normal1 * ga + sa
    normed_low = normed.astype(BF16)
    normed_ref[...] = normed_low
    second = normed + bu
    for at in range(0, hidden_width, chunk):
        pre = dot_nn(normed_low, wi_ref[:, at:at + chunk]) + bi_ref[:, at:at + chunk]
        share = 0.5 + 0.5 * lax.erf(pre * 0.7071067811865476)
        act = (pre * share).astype(BF16)
        act_ref[:, at:at + chunk] = act
        slope_ref[:, at:at + chunk] = share + pre * (jnp.exp(pre * pre * -0.5) * 0.3989422804014327)
        second = second + dot_nn(act, wu_ref[at:at + chunk, :])
    normal2, inverse2 = normalize(second)
    out_ref[...] = (normal2 * gf + sf).astype(BF16)
    lane = lax.broadcasted_iota(jnp.int32, (tile, count), 1)
    chosen = jnp.where(place_ref[...] == lane, 1.0, 0.0).astype(BF16)
    cot = dot_nn(chosen, cot_ref[...])
    second_grad = normalize_back(cot * gf, normal2, inverse2)
    outer_low = second_grad.astype(BF16)
    outer_ref[...] = outer_low
    normed_grad = second_grad
    for at in range(0, hidden_width, chunk):
        act_grad = dot_nt(outer_low, wu_ref[at:at + chunk, :])
        inner_low = (act_grad * slope_ref[:, at:at + chunk]).astype(BF16)
        inner_ref[:, at:at + chunk] = inner_low
        bisum_ref[0:1, at:at + chunk] += column_sum(inner_low)
        normed_grad = normed_grad + dot_nt(inner_low, wi_ref[:, at:at + chunk])
    first_grad = normalize_back(normed_grad * ga, normal1, inverse1)
    first_ref[...] = first_grad
    branch_low = first_grad.astype(BF16)
    low_ref[...] = branch_low
    agrad_ref[...] = dot_nt(branch_low, wo_ref[...]).astype(BF16)
    sums_ref[2:3, :] += column_sum(branch_low)
    sums_ref[3:4, :] += column_sum(normed_grad * normal1)
    sums_ref[4:5, :] += column_sum(normed_grad)
    sums_ref[5:6, :] += column_sum(outer_low)
    sums_ref[6:7, :] += column_sum(cot * normal2)
    sums_ref[7:8, :] += column_sum(cot)


def feed_forward(place_col, rows, attended, arrived_cot, w4, wi, wu, vec, bi):
    count, width = rows.shape
    hidden_width = wi.shape[1]
    tile = count // 4
    row_spec = pl.BlockSpec((tile, width), lambda i: (i, 0))
    wide_spec = pl.BlockSpec((tile, hidden_width), lambda i: (i, 0))

    def rows_of(n, dtype):
        return jax.ShapeDtypeStruct((count, n), dtype)

    return pl.pallas_call(
        partial(feed_kernel, 512),
        grid=(4,),
        out_shape=[
            rows_of(width, BF16), rows_of(hidden_width, BF16), rows_of(hidden_width, BF16), rows_of(width, BF16),
            rows_of(width, BF16), rows_of(width, BF16), rows_of(width, F32), rows_of(width, BF16),
            jax.ShapeDtypeStruct((8, width), F32), jax.ShapeDtypeStruct((8, hidden_width), F32),
        ],
        in_specs=[
            pl.BlockSpec((tile, 1), lambda i: (i, 0)), row_spec, row_spec, held_spec((count, width)),
            pl.BlockSpec((pl.Squeezed(), width, width), lambda i: (3, 0, 0), pipeline_mode=pl.Buffered(1)),
            held_spec(wi.shape), held_spec(wu.shape), held_spec(vec.shape), held_spec(bi.shape),
        ],
        out_specs=[row_spec, wide_spec, wide_spec] + [row_spec] * 5
        + [full_spec((8, width)), full_spec((8, hidden_width))],
        scratch_shapes=[pltpu.VMEM((tile, hidden_width), F32)],
        compiler_params=params(56, "arbitrary"),
        cost_estimate=pl.CostEstimate(flops=12 * count * width * hidden_width, bytes_accessed=36 * MIB, transcendentals=2 * count * hidden_width),
        name="feed_forward",
    )(place_col, rows, attended, arrived_cot, w4, wi, wu, vec, bi)


def rows_grad_kernel(tile, where_ref, first_ref, dq_ref, dk_ref, dv_ref, wq_ref, wk_ref, wv_ref, out_ref, total_ref):
    step = pl.program_id(0)
    tiles = total_ref.shape[0] // tile

    @pl.when(step < tiles)
    def _():
        total = (
            first_ref[...]
            + dot_nt(dq_ref[...], wq_ref[...])
            + dot_nt(dk_ref[...], wk_ref[...])
            + dot_nt(dv_ref[...], wv_ref[...])
        )
        total_ref[pl.ds(pl.multiple_of(step * tile, tile), tile), :] = total.astype(BF16)

    @pl.when(step >= tiles)
    def _():
        count = where_ref.shape[1]
        target = lax.broadcasted_iota(jnp.int32, (tile, count), 0) + (step - tiles) * tile
        chosen = jnp.where(where_ref[...] == target, 1.0, 0.0).astype(BF16)
        out_ref[...] = dot_nn(chosen, total_ref[...]).astype(BF16)


def rows_grad(where_row, first_grad, dq, dk, dv, w4):
    count, width = dq.shape
    tiles = 4
    tile = count // tiles
    row_spec = pl.BlockSpec((tile, width), lambda i: (jnp.minimum(i, tiles - 1), 0))

    def weight(n):
        return pl.BlockSpec((pl.Squeezed(), width, width), lambda i: (n, 0, 0), pipeline_mode=pl.Buffered(1))

    return pl.pallas_call(
        partial(rows_grad_kernel, tile),
        grid=(2 * tiles,),
        out_shape=jax.ShapeDtypeStruct((count, width), BF16),
        in_specs=[held_spec((1, count)), row_spec, row_spec, row_spec, row_spec, weight(0), weight(1), weight(2)],
        out_specs=pl.BlockSpec((tile, width), lambda i: (jnp.maximum(i - tiles, 0), 0)),
        scratch_shapes=[pltpu.VMEM((count, width), BF16)],
        compiler_params=params(40, "arbitrary"),
        name="rows_grad",
    )(where_row, first_grad, dq, dk, dv, w4, w4, w4)


def scatter_sum(pieces):
    return lax.psum_scatter(pieces, "fsdp", scatter_dimension=0, tiled=True)


def on_device(tokens, cotangent, packed_slot, seq_lengths, query_weight, query_bias, key_weight, value_weight,
              value_bias, output_weight, output_bias, attention_gain, attention_shift, inner_weight, inner_bias,
              outer_weight, outer_bias, final_gain, final_shift):
    devices = lax.axis_size("fsdp")
    me = lax.axis_index("fsdp")
    count, width = tokens.shape
    hidden_width = inner_bias.shape[0] * devices
    peer_rows = count // devices
    segments = seq_lengths.shape[1]
    share = width // devices
    counting = jnp.arange(count, dtype=jnp.int32)

    def exchange(rows):
        pieces = rows.reshape(devices, peer_rows, width)
        return lax.all_to_all(pieces, "fsdp", split_axis=0, concat_axis=0, tiled=True).reshape(count, width)

    own_slots = lax.dynamic_slice_in_dim(packed_slot, me * count, count)
    rank = jnp.sum((own_slots[None, :] < own_slots[:, None]).astype(jnp.int32), axis=1)
    rank_row, rank_col = rank.reshape(1, count), rank.reshape(count, 1)
    arrived = exchange(permute_rows(rank_row, tokens))
    arrived_cot = exchange(permute_rows(rank_row, cotangent))

    w4 = jnp.stack([w.reshape(share, width) for w in (query_weight, key_weight, value_weight, output_weight)])
    small = (query_bias, value_bias, output_bias, attention_gain, attention_shift, outer_bias, final_gain, final_shift)
    vec = jnp.concatenate(small + (inner_bias,))
    used = vec.shape[0]
    vec = jnp.pad(vec, (0, 8 * LANES - used)).reshape(8, LANES)
    g4, gi, gu, gv = gather_parameters(
        devices, w4, inner_weight.reshape(share, hidden_width), outer_weight.reshape(hidden_width // devices, width), vec
    )
    w4 = g4.reshape(4, width, width)
    wi = gi.reshape(width, hidden_width)
    wu = gu.reshape(hidden_width, width)
    flat = gv.reshape(devices, 8 * LANES).astype(F32)
    vec = flat[:, : 8 * share].reshape(devices, 8, share).transpose(1, 0, 2).reshape(8, width)
    bi = flat[:, 8 * share : used].reshape(1, hidden_width)

    local_slots = packed_slot.reshape(devices, count) - me * count
    source = source_devices(local_slots, count).astype(jnp.int32).reshape(count)
    same = (source[:, None] == source[None, :]) & (counting[None, :] < counting[:, None])
    place = source * peer_rows + jnp.sum(same.astype(jnp.int32), axis=1)
    place_row, place_col = place.reshape(1, count), place.reshape(count, 1)
    ends = jnp.cumsum(seq_lengths[0], dtype=jnp.int32)
    segment = jnp.sum((counting[:, None] >= ends[None, :]).astype(jnp.int32), axis=1)
    segment_col = segment.reshape(count, 1)

    rows, q, k, v = project(place_col, arrived, w4, vec)
    attended, lse = attend(segments, segment_col, q, k, v)
    (result, activated, inner_low, normed_low, outer_low, branch_low, first_grad, attended_grad, sums, bi_sum) = feed_forward(
        place_col, rows, attended, arrived_cot, w4, wi, wu, vec, bi
    )
    layer_out = unpermute_rows(rank_col, exchange(permute_rows(place_row, result)))

    def weight_grad(left, right):
        return dot_tn(left, right).astype(BF16)

    def pieces_of(grad):
        return grad.reshape(devices, -1, grad.shape[-1])

    inner_grad = scatter_sum(pieces_of(weight_grad(normed_low, inner_low)))
    outer_grad = scatter_sum(pieces_of(weight_grad(activated, outer_low)))
    wo_grad = weight_grad(attended, branch_low)

    dq, dk, dv, more = attend_back(segments, segment_col, q, attended, attended_grad, lse, k, v)
    tokens_grad = unpermute_rows(rank_col, exchange(rows_grad(place_row, first_grad, dq, dk, dv, w4)))
    sums = sums + more
    sums = sums.reshape(8, devices, share).transpose(1, 0, 2).reshape(devices, 8 * share)
    sums = jnp.concatenate([sums, bi_sum[0].reshape(devices, hidden_width // devices)], axis=1)
    sums = jnp.pad(sums, ((0, 0), (0, width - used))).reshape(devices, 1, width).astype(BF16)
    late = jnp.concatenate(
        [pieces_of(weight_grad(rows, dq)), pieces_of(weight_grad(rows, dk)), pieces_of(weight_grad(rows, dv)),
         pieces_of(wo_grad), sums],
        axis=1,
    )
    late = scatter_sum(late)[0].astype(F32)
    wq_grad, wk_grad, wv_grad, wo_grad = (late[i * share:(i + 1) * share].reshape(-1) for i in range(4))
    sums = late[4 * share]
    small = [sums[i * share:(i + 1) * share] for i in range(8)]
    return (
        layer_out, tokens_grad, wq_grad, small[0], wk_grad, wv_grad, small[1], wo_grad, small[2], small[3], small[4],
        inner_grad.astype(F32).reshape(-1), sums[8 * share:used], outer_grad.astype(F32).reshape(-1), small[5], small[6], small[7],
    )


def solution(mesh):
    split, rows = P("fsdp"), P("fsdp", None)
    return jax.shard_map(
        on_device,
        mesh=mesh,
        in_specs=(rows, rows, P(), rows) + (split,) * 15,
        out_specs=(rows, rows) + (split,) * 15,
        check_vma=False,
    )
```

```python
from functools import partial

import jax
import jax.numpy as jnp
from jax import lax
from jax.experimental import pallas as pl
from jax.experimental.pallas import tpu as pltpu
from jax.sharding import PartitionSpec as P

HD = 64
LANES = 128
EPSILON = 1e-12
NEG_LARGE = -1e30
MIB = 1 << 20
F32 = jnp.float32
BF16 = jnp.bfloat16
MESH = pl.DeviceIdType.MESH


def dot_nn(a, b):
    return lax.dot_general(a, b, (((1,), (0,)), ((), ())), preferred_element_type=F32)


def dot_nt(a, b):
    return lax.dot_general(a, b, (((1,), (1,)), ((), ())), preferred_element_type=F32)


def dot_tn(a, b):
    return lax.dot_general(a, b, (((0,), (0,)), ((), ())), preferred_element_type=F32)


def full_spec(shape, **kw):
    return pl.BlockSpec(shape, lambda *_: (0,) * len(shape), **kw)


def held_spec(shape):
    return full_spec(shape, pipeline_mode=pl.Buffered(1))


def params(mib, *axes, **kw):
    return pltpu.CompilerParams(
        dimension_semantics=axes or None, vmem_limit_bytes=mib * MIB, **kw
    )


def grid_of(devices):
    return {32: (4, 2, 2, 2), 128: (4, 4, 4, 2)}.get(devices, (devices, 1, 1, 1))


def gather_kernel(sizes, half, w4, wi, wu, vec, g4, gi, gu, gv, local_sem, sa, ra, sb, rb, sc, rc, sk, rk):
    na, nb, nc, nk = sizes
    me = lax.axis_index("fsdp")
    k = me % nk
    c = (me // nk) % nc
    b = (me // (nk * nc)) % nb
    a = me // (nk * nc * nb)

    def at(ja, jb, jc, jk=0):
        aa = (a + na - ja) % na
        bb = (b + nb - jb) % nb
        cc = (c + nc - jc) % nc
        kk = (k + nk - jk) % nk
        return ((aa * nb + bb) * nc + cc) * nk + kk

    rest = wu.shape[0] - half
    own = (w4, wi, wu.at[pl.ds(0, half)], wu.at[pl.ds(half, rest)], vec)

    def slot(dev):
        return (
            g4.at[:, dev],
            gi.at[dev],
            gu.at[dev, pl.ds(0, half)],
            gu.at[dev, pl.ds(half, rest)],
            gv.at[dev],
        )

    peers = [at(-j, 0, 0) for j in range(1, na)]
    peers += [at(0, -j, 0) for j in range(1, nb)]
    peers += [at(0, 0, -j) for j in range(1, nc)]
    peers += [at(0, 0, 0, -j) for j in range(1, nk)]
    barrier = pltpu.get_barrier_semaphore()
    for peer in peers:
        pl.semaphore_signal(barrier, inc=1, device_id=(peer,), device_id_type=MESH)
    pl.semaphore_wait(barrier, len(peers))

    started = []

    def send(source, target, send_sem, recv_sem, peer):
        copy = pltpu.make_async_remote_copy(
            src_ref=source, dst_ref=target, send_sem=send_sem, recv_sem=recv_sem,
            device_id=(peer,), device_id_type=MESH,
        )
        copy.start()
        started.append(copy)

    def arrive(piece, send_sem, recv_sem):
        pltpu.make_async_remote_copy(
            src_ref=piece, dst_ref=piece, send_sem=send_sem, recv_sem=recv_sem,
            device_id=(me,), device_id_type=MESH,
        ).wait_recv()

    mine = slot(me)
    local = []
    for p in range(5):
        for j in range(1, na):
            send(own[p], mine[p], sa.at[p, j], ra.at[p, j], at(-j, 0, 0))
    for p in range(5):
        copy = pltpu.make_async_copy(own[p], mine[p], local_sem.at[p])
        copy.start()
        local.append(copy)
    first = (0, 4, 2)
    second = (1, 3)

    def source_of(p, ja, jb, jc):
        if ja == 0 and jb == 0 and jc == 0:
            return own[p], mine[p]
        piece = slot(at(ja, jb, jc))[p]
        return piece, piece

    def to_b(p, ja, jc):
        source, target = source_of(p, ja, 0, jc)
        for j in range(1, nb):
            send(source, target, sb.at[p, ja, jc, j], rb.at[p, ja, jc, j], at(0, -j, 0))

    def to_c(p, ja, jb):
        source, target = source_of(p, ja, jb, 0)
        for j in range(1, nc):
            send(source, target, sc.at[p, ja, jb, j], rc.at[p, ja, jb, j], at(0, 0, -j))

    def to_k(p, ja, jb, jc):
        source, target = source_of(p, ja, jb, jc)
        for j in range(1, nk):
            send(source, target, sk.at[p, ja, jb, jc, j], rk.at[p, ja, jb, jc, j], at(0, 0, 0, -j))

    for ja in range(na):
        for p in first + second:
            if ja:
                arrive(slot(at(ja, 0, 0))[p], sa.at[p, ja], ra.at[p, ja])
            if p in first:
                to_b(p, ja, 0)
                to_c(p, ja, 0)
            else:
                to_c(p, ja, 0)
                to_b(p, ja, 0)
            to_k(p, ja, 0, 0)
    for ja in range(na):
        for p in first + second:
            if p in first:
                for j in range(1, nb):
                    arrive(slot(at(ja, j, 0))[p], sb.at[p, ja, 0, j], rb.at[p, ja, 0, j])
                    to_c(p, ja, j)
                    to_k(p, ja, j, 0)
            else:
                for j in range(1, nc):
                    arrive(slot(at(ja, 0, j))[p], sc.at[p, ja, 0, j], rc.at[p, ja, 0, j])
                    to_b(p, ja, j)
                    to_k(p, ja, 0, j)
    for ja in range(na):
        for p in first + second:
            if p in first:
                for j in range(nb):
                    for i in range(1, nc):
                        arrive(slot(at(ja, j, i))[p], sc.at[p, ja, j, i], rc.at[p, ja, j, i])
                        to_k(p, ja, j, i)
            else:
                for i in range(nc):
                    for j in range(1, nb):
                        arrive(slot(at(ja, j, i))[p], sb.at[p, ja, i, j], rb.at[p, ja, i, j])
                        to_k(p, ja, j, i)
    for ja in range(na):
        for jb in range(nb):
            for jc in range(nc):
                for p in first + second:
                    for j in range(1, nk):
                        arrive(
                            slot(at(ja, jb, jc, j))[p],
                            sk.at[p, ja, jb, jc, j],
                            rk.at[p, ja, jb, jc, j],
                        )
    for copy in local:
        copy.wait()
    for copy in started:
        copy.wait_send()


def gather_parameters(devices, w4, wi, wu, vec):
    sizes = grid_of(devices)
    na, nb, nc, nk = sizes
    rows = w4.shape[1]
    dma = pltpu.SemaphoreType.DMA
    anywhere = pl.BlockSpec(memory_space=pl.ANY)
    return pl.pallas_call(
        partial(gather_kernel, sizes, wu.shape[0] // 16 * 8),
        out_shape=(
            jax.ShapeDtypeStruct((4, devices) + w4.shape[1:], BF16),
            jax.ShapeDtypeStruct((devices,) + wi.shape, BF16),
            jax.ShapeDtypeStruct((devices,) + wu.shape, BF16),
            jax.ShapeDtypeStruct((devices,) + vec.shape, BF16),
        ),
        in_specs=[anywhere] * 4,
        out_specs=[anywhere] * 4,
        scratch_shapes=[dma((5,))]
        + [dma((5, na))] * 2
        + [dma((5, na, nc, nb))] * 2
        + [dma((5, na, nb, nc))] * 2
        + [dma((5, na, nb, nc, nk))] * 2,
        compiler_params=pltpu.CompilerParams(collective_id=1, has_side_effects=True),
    )(w4, wi, wu, vec)


class Place:
    def __init__(self, sizes):
        na, nb, nc, nk = self.sizes = sizes
        self.me = me = lax.axis_index("fsdp")
        self.k = me % nk
        self.c = (me // nk) % nc
        self.b = (me // (nk * nc)) % nb
        self.a = me // (nk * nc * nb)

    def ahead(self, axis, step):
        own = (self.a, self.b, self.c, self.k)[axis]
        return (own + step) % self.sizes[axis]

    def device(self, axis, step):
        na, nb, nc, nk = self.sizes
        where = [self.a, self.b, self.c, self.k]
        where[axis] = self.ahead(axis, step)
        return ((where[0] * nb + where[1]) * nc + where[2]) * nk + where[3]


def remote(source, target, send_sem, recv_sem, peer):
    return pltpu.make_async_remote_copy(
        src_ref=source, dst_ref=target, send_sem=send_sem, recv_sem=recv_sem,
        device_id=(peer,), device_id_type=MESH,
    )


def greet_all(devices):
    me = lax.axis_index("fsdp")
    barrier = pltpu.get_barrier_semaphore()

    def signal(j, carry):
        pl.semaphore_signal(barrier, inc=1, device_id=((me + j) % devices,), device_id_type=MESH)
        return carry

    lax.fori_loop(1, devices, signal, 0)
    pl.semaphore_wait(barrier, devices - 1)


class Exchange:
    def __init__(self, devices, source, target, sems, local_sem):
        self.devices, self.source, self.target, self.sems, self.local_sem = devices, source, target, sems, local_sem
        self.rows = source.shape[0] // devices
        self.me = lax.axis_index("fsdp")

    def block(self, ref, device):
        return ref.at[pl.ds(pl.multiple_of(device * self.rows, self.rows), self.rows)]

    def own(self):
        return pltpu.make_async_copy(self.block(self.source, self.me), self.block(self.target, self.me), self.local_sem)

    def outgoing(self, j):
        peer = (self.me + j) % self.devices
        return remote(self.block(self.source, peer), self.block(self.target, self.me), self.sems.at[0, j], self.sems.at[1, j], peer)

    def incoming(self, j):
        peer = (self.me + self.devices - j) % self.devices
        block = self.block(self.target, peer)
        return remote(block, block, self.sems.at[0, j], self.sems.at[1, j], peer)

    def over(self, act):
        def body(j, carry):
            act(j)
            return carry

        lax.fori_loop(1, self.devices, body, 0)

    def start(self):
        self.own().start()
        self.over(lambda j: self.outgoing(j).start())

    def wait(self):
        self.over(lambda j: self.incoming(j).wait_recv())
        self.over(lambda j: self.outgoing(j).wait_send())
        self.own().wait()


def tree_scratch(sizes, flip, rows, columns):
    na, nb, nc, nk = sizes
    one, two = (nb, nc) if flip else (nc, nb)
    shapes = [(na, nb, nc), (nk - 1, na, nb, nc), (one - 1, na, two), (two - 1, na), (na - 1,)]
    return [pltpu.VMEM(shape + (rows, columns), BF16) for shape in shapes] + [
        pltpu.SemaphoreType.DMA((2, 4, max(sizes))),
        pltpu.SemaphoreType.DMA(()),
    ]


class Tree:
    def __init__(self, place, flip, parts, scratch):
        self.place, self.flip, self.parts = place, flip, parts
        self.held, *self.landing, self.sems, self.local_sem = scratch
        order = (3, 1, 2, 0) if flip else (3, 2, 1, 0)
        self.axes = order

    def own(self):
        return pltpu.make_async_copy(self.parts.at[:, :, :, self.place.k], self.held, self.local_sem)

    def outgoing(self, stage):
        place, held = self.place, self.held
        axis = self.axes[stage]
        copies = []
        for j in range(1, place.sizes[axis]):
            other = place.ahead(axis, j)
            if stage == 0:
                source = self.parts.at[:, :, :, other]
            elif stage == 1:
                source = held.at[:, other] if self.flip else held.at[:, :, other]
            elif stage == 2:
                source = held.at[:, place.b, other] if self.flip else held.at[:, other, place.c]
            else:
                source = held.at[other, place.b, place.c]
            copies.append(
                remote(source, self.landing[stage].at[j - 1], self.sems.at[0, stage, j], self.sems.at[1, stage, j], place.device(axis, j))
            )
        return copies

    def start(self, stage):
        if stage == 0:
            self.own().start()
        for copy in self.outgoing(stage):
            copy.start()

    def settle(self, stage, out=None):
        place, held, landing = self.place, self.held, self.landing[stage]
        na, nb, nc, nk = place.sizes
        if stage == 0:
            self.own().wait()
        for copy in self.outgoing(stage):
            copy.wait_recv()
        count = place.sizes[self.axes[stage]] - 1

        def total(own, index):
            value = own.astype(F32)
            for j in range(count):
                value = value + landing[(j,) + index].astype(F32)
            return value

        if stage == 0:
            def add(i, carry):
                held[i] = total(held[i], (i,)).astype(BF16)
                return carry
            lax.fori_loop(0, na, add, 0)
        elif stage == 1:
            two = nc if self.flip else nb
            def add(i, carry):
                for t in range(two):
                    at = (i, place.b, t) if self.flip else (i, t, place.c)
                    held[at] = total(held[at], (i, t)).astype(BF16)
                return carry
            lax.fori_loop(0, na, add, 0)
        elif stage == 2:
            def add(i, carry):
                at = (i, place.b, place.c)
                held[at] = total(held[at], (i,)).astype(BF16)
                return carry
            lax.fori_loop(0, na, add, 0)
        else:
            out[...] = total(held[place.a, place.b, place.c], ())

    def drain(self):
        for stage in range(4):
            for copy in self.outgoing(stage):
                copy.wait_send()


def permute_kernel(tile, where_ref, rows_ref, out_ref):
    count = where_ref.shape[1]
    target = lax.broadcasted_iota(jnp.int32, (tile, count), 0) + pl.program_id(0) * tile
    chosen = jnp.where(where_ref[...] == target, 1.0, 0.0).astype(BF16)
    out_ref[...] = dot_nn(chosen, rows_ref[...]).astype(BF16)


def permute_rows(where_row, rows):
    count, width = rows.shape
    tile = count // 4
    return pl.pallas_call(
        partial(permute_kernel, tile),
        grid=(4,),
        out_shape=jax.ShapeDtypeStruct(rows.shape, BF16),
        in_specs=[full_spec((1, count)), full_spec((count, width))],
        out_specs=pl.BlockSpec((tile, width), lambda i: (i, 0)),
        compiler_params=params(32, "arbitrary"),
        name="permute_rows",
    )(where_row, rows)


def unpermute_kernel(from_ref, rows_ref, out_ref):
    tile, count = out_ref.shape[0], rows_ref.shape[0]
    lane = lax.broadcasted_iota(jnp.int32, (tile, count), 1)
    chosen = jnp.where(from_ref[...] == lane, 1.0, 0.0).astype(BF16)
    out_ref[...] = dot_nn(chosen, rows_ref[...]).astype(BF16)


def unpermute_rows(from_col, rows):
    count, width = rows.shape
    tile = count // 4
    return pl.pallas_call(
        unpermute_kernel,
        grid=(4,),
        out_shape=jax.ShapeDtypeStruct(rows.shape, BF16),
        in_specs=[pl.BlockSpec((tile, 1), lambda i: (i, 0)), full_spec((count, width))],
        out_specs=pl.BlockSpec((tile, width), lambda i: (i, 0)),
        compiler_params=params(32, "arbitrary"),
        name="unpermute_rows",
    )(from_col, rows)


LOW = 32


def source_kernel(slots_ref, out_ref):
    devices, count = slots_ref.shape
    high = out_ref.shape[0]

    def body(s, total):
        local = slots_ref[pl.ds(s, 1), :]
        in_high = lax.broadcasted_iota(jnp.int32, (high, count), 0) == (local >> 5)
        in_low = lax.broadcasted_iota(jnp.int32, (LOW, count), 0) == (local & (LOW - 1))
        weight = jnp.where(in_high, s.astype(F32), 0.0).astype(BF16)
        return total + dot_nt(weight, jnp.where(in_low, 1.0, 0.0).astype(BF16))

    out_ref[...] = lax.fori_loop(0, devices, body, jnp.zeros((high, LOW), F32))


def source_devices(local_slots, count):
    return pl.pallas_call(
        source_kernel,
        out_shape=jax.ShapeDtypeStruct((count // LOW, LOW), F32),
        in_specs=[pl.BlockSpec(memory_space=pltpu.VMEM)],
        out_specs=pl.BlockSpec(memory_space=pltpu.VMEM),
        name="source_devices",
    )(local_slots)


def project_kernel(place_ref, arrived_ref, wq_ref, wk_ref, wv_ref, vec_ref, rows_ref, q_ref, k_ref, v_ref):
    tile, count = rows_ref.shape[0], arrived_ref.shape[0]
    lane = lax.broadcasted_iota(jnp.int32, (tile, count), 1)
    chosen = jnp.where(place_ref[...] == lane, 1.0, 0.0).astype(BF16)
    rows = dot_nn(chosen, arrived_ref[...]).astype(BF16)
    rows_ref[...] = rows
    vec = vec_ref[...]
    q_ref[...] = ((dot_nn(rows, wq_ref[...]) + vec[0:1]).astype(BF16).astype(F32) * 0.125).astype(BF16)
    k_ref[...] = dot_nn(rows, wk_ref[...]).astype(BF16)
    v_ref[...] = (dot_nn(rows, wv_ref[...]) + vec[1:2]).astype(BF16)


def project(place_col, arrived, w4, vec):
    count, width = arrived.shape
    tile = count // 4
    row_spec = pl.BlockSpec((tile, width), lambda i: (i, 0))

    def weight(n):
        return pl.BlockSpec((pl.Squeezed(), width, width), lambda i: (n, 0, 0), pipeline_mode=pl.Buffered(1))

    return pl.pallas_call(
        project_kernel,
        grid=(4,),
        out_shape=[jax.ShapeDtypeStruct((count, width), BF16)] * 4,
        in_specs=[pl.BlockSpec((tile, 1), lambda i: (i, 0)), held_spec((count, width)),
                  weight(0), weight(1), weight(2), held_spec(vec.shape)],
        out_specs=[row_spec] * 4,
        compiler_params=params(40, "arbitrary"),
        cost_estimate=pl.CostEstimate(flops=8 * count * width * width, bytes_accessed=14 * MIB, transcendentals=0),
        name="project",
    )(place_col, arrived, w4, w4, w4, vec)


def split3(column):
    high = column.astype(BF16).astype(F32)
    rest = column - high
    mid = rest.astype(BF16).astype(F32)
    return high, mid, rest - mid


def feature_lanes(rows):
    lane = lax.broadcasted_iota(jnp.int32, (rows, LANES), 1)
    return lane < HD, lane & (HD - 1)


def key_features(lane, segment, segments):
    return jnp.where(lane == segment, 1.0, jnp.where((lane >= segments) & (lane < segments + 3), 1.0, 0.0))


def query_features(lane, segment, segments):
    return jnp.where((lane < segments) & (lane != segment), NEG_LARGE, 0.0)


def with_column(features, lane, start, column):
    high, mid, last = split3(column)
    features = jnp.where(lane == start, high, features)
    features = jnp.where(lane == start + 1, mid, features)
    return jnp.where(lane == start + 2, last, features)


def attend_kernel(segments, seg_ref, q_ref, seg_all_ref, k_ref, v_ref, out_ref, lse_ref, k0, k1):
    count, tile = k_ref.shape[0], q_ref.shape[0]
    first_all, lane_all = feature_lanes(count)

    @pl.when(pl.program_id(1) == 0)
    def _():
        extra = key_features(lane_all, seg_all_ref[...], segments).astype(BF16)
        k0[...] = jnp.where(first_all, k_ref[...], extra)
        k1[...] = jnp.where(first_all, extra, k_ref[...])

    first, lane = feature_lanes(tile)
    extra = query_features(lane, seg_ref[...], segments).astype(BF16)
    queries = q_ref[...]
    values = v_ref[...]
    outs, logs = [], []
    for mask, keys in ((first, k0), (~first, k1)):
        scores = dot_nt(jnp.where(mask, queries, extra), keys[...])
        top = jnp.max(scores, axis=1, keepdims=True)
        raised = jnp.exp(scores - top)
        total = jnp.sum(raised, axis=1, keepdims=True)
        outs.append(dot_nn(raised.astype(BF16), values) * (1.0 / total))
        logs.append(top + jnp.log(total))
    out_ref[...] = jnp.where(first, outs[0], outs[1]).astype(BF16)
    lse_ref[...] = jnp.where(first, logs[0], logs[1])


def attend(segments, segment_col, q, k, v):
    count, width = q.shape
    pairs = width // LANES
    tile = count // 4
    tile_spec = pl.BlockSpec((tile, LANES), lambda h, i: (i, h))
    all_spec = pl.BlockSpec((count, LANES), lambda h, i: (0, h))
    return pl.pallas_call(
        partial(attend_kernel, segments),
        grid=(pairs, 4),
        out_shape=[jax.ShapeDtypeStruct((count, width), BF16), jax.ShapeDtypeStruct((count, width), F32)],
        in_specs=[pl.BlockSpec((tile, 1), lambda h, i: (i, 0)), tile_spec, held_spec((count, 1)), all_spec, all_spec],
        out_specs=[tile_spec, tile_spec],
        scratch_shapes=[pltpu.VMEM((count, LANES), BF16)] * 2,
        compiler_params=params(40, "arbitrary", "arbitrary"),
        cost_estimate=pl.CostEstimate(flops=8 * count * count * width, bytes_accessed=10 * MIB, transcendentals=count * count * 12),
        name="attend",
    )(segment_col, q, segment_col, k, v)


def attend_back_kernel(segments, sizes, seg_ref, q_ref, o_ref, g_ref, lse_ref, seg_all_ref, k_ref, v_ref,
                       leaving_ref, wi_ref, wu_ref, wo_ref,
                       dq_ref, dk_ref, dv_ref, sums_ref, returned_ref, wi_out, wu_out, wo_out,
                       k0, k1, v0, v1, dk_sum, dv_sum, swap_sems, swap_local, *tree_refs):
    count, tile = k_ref.shape[0], q_ref.shape[0]
    first_all, lane_all = feature_lanes(count)
    step, last = pl.program_id(1), pl.num_programs(1) - 1
    now = pl.program_id(0) * pl.num_programs(1) + step

    place = Place(sizes)
    devices = sizes[0] * sizes[1] * sizes[2] * sizes[3]
    swap = Exchange(devices, leaving_ref, returned_ref, swap_sems, swap_local)
    trees = [
        Tree(place, flip, parts, tree_refs[7 * i:7 * i + 7])
        for i, (flip, parts) in enumerate(((False, wi_ref), (True, wu_ref), (False, wo_ref)))
    ]
    outs = (wi_out, wu_out, wo_out)

    @pl.when(now == 0)
    def _():
        greet_all(devices)
        for tree in trees:
            tree.start(0)
        swap.start()

    for i, tree in enumerate(trees):
        for stage, at in enumerate(((3, 16, 22), (5, 17, 22), (6, 18, 22))[i]):
            @pl.when(now == at)
            def _(tree=tree, stage=stage):
                tree.settle(stage)
                tree.start(stage + 1)

    @pl.when(step == 0)
    def _():
        extra = key_features(lane_all, seg_all_ref[...], segments).astype(BF16)
        k0[...] = jnp.where(first_all, k_ref[...], extra)
        k1[...] = jnp.where(first_all, extra, k_ref[...])
        v0[...] = jnp.where(first_all, v_ref[...], extra)
        v1[...] = jnp.where(first_all, extra, v_ref[...])
        dk_sum[...] = jnp.zeros_like(dk_sum)
        dv_sum[...] = jnp.zeros_like(dv_sum)
        sums_ref[...] = jnp.zeros_like(sums_ref)

    first, lane = feature_lanes(tile)
    hidden = query_features(lane, seg_ref[...], segments)
    queries, grads = q_ref[...], g_ref[...]
    product = grads.astype(F32) * o_ref[...].astype(F32)
    lses = lse_ref[...]
    dqs, dks, dvs = [], [], []
    for mask, keys, values, at in ((first, k0, v0, 0), (~first, k1, v1, HD)):
        lse = lses[:, at:at + 1]
        delta = jnp.sum(jnp.where(mask, product, 0.0), axis=1, keepdims=True)
        query = jnp.where(mask, queries, with_column(hidden, lane, segments, -lse).astype(BF16))
        grad = jnp.where(mask, grads, with_column(jnp.zeros_like(hidden), lane, segments, -delta).astype(BF16))
        probs = jnp.exp(dot_nt(keys[...], query))
        score = (probs * dot_nt(values[...], grad)).astype(BF16)
        dvs.append(dot_nn(probs.astype(BF16), grad))
        dks.append(dot_nn(score, query))
        dqs.append(dot_tn(score, keys[...]))
    dq = (jnp.where(first, dqs[0], dqs[1]) * 0.125).astype(BF16)
    dq_ref[...] = dq
    dk_sum[...] += jnp.where(first_all, dks[0], dks[1])
    dv_sum[...] += jnp.where(first_all, dvs[0], dvs[1])
    sums_ref[0:1, :] += jnp.sum(dq.astype(F32), axis=0, keepdims=True)

    @pl.when(step == last)
    def _():
        dk_ref[...] = dk_sum[...].astype(BF16)
        dv = dv_sum[...].astype(BF16)
        dv_ref[...] = dv
        sums_ref[1:2, :] += jnp.sum(dv.astype(F32), axis=0, keepdims=True)

    @pl.when(now == pl.num_programs(0) * pl.num_programs(1) - 1)
    def _():
        for tree, out in zip(trees, outs):
            tree.settle(3, out)
        swap.wait()
        for tree in trees:
            tree.drain()


def attend_back(segments, segment_col, q, out, grad, lse, k, v, leaving, wi, wu, wo):
    count, width = q.shape
    pairs = width // LANES
    tile = count // 4
    devices = wi.shape[0]
    sizes = grid_of(devices)
    tile_spec = pl.BlockSpec((tile, LANES), lambda h, i: (i, h))
    all_spec = pl.BlockSpec((count, LANES), lambda h, i: (0, h))
    anywhere = pl.BlockSpec(memory_space=pl.ANY)
    parts = [x.reshape(sizes + x.shape[1:]) for x in (wi, wu, wo)]
    trees = []
    for flip, x in zip((False, True, False), (wi, wu, wo)):
        trees += tree_scratch(sizes, flip, *x.shape[1:])
    return pl.pallas_call(
        partial(attend_back_kernel, segments, sizes),
        grid=(pairs, 4),
        out_shape=[jax.ShapeDtypeStruct((count, width), BF16)] * 3
        + [jax.ShapeDtypeStruct((8, width), F32), jax.ShapeDtypeStruct((count, width), BF16)]
        + [jax.ShapeDtypeStruct(x.shape[1:], F32) for x in (wi, wu, wo)],
        in_specs=[pl.BlockSpec((tile, 1), lambda h, i: (i, 0))] + [tile_spec] * 4 + [held_spec((count, 1)), all_spec, all_spec]
        + [anywhere] * 4,
        out_specs=[tile_spec, all_spec, all_spec, pl.BlockSpec((8, LANES), lambda h, i: (0, h)), anywhere]
        + [full_spec(x.shape[1:]) for x in (wi, wu, wo)],
        scratch_shapes=[pltpu.VMEM((count, LANES), BF16)] * 4 + [pltpu.VMEM((count, LANES), F32)] * 2
        + [pltpu.SemaphoreType.DMA((2, devices)), pltpu.SemaphoreType.DMA(())] + trees,
        compiler_params=params(60, "arbitrary", "arbitrary", collective_id=2, has_side_effects=True),
        cost_estimate=pl.CostEstimate(flops=20 * count * count * width, bytes_accessed=16 * MIB, transcendentals=count * count * 12),
        name="attend_back",
    )(segment_col, q, out, grad, lse, segment_col, k, v, leaving, *parts)


def normalize(hidden):
    centered = hidden - jnp.mean(hidden, axis=1, keepdims=True)
    variance = jnp.mean(centered * centered, axis=1, keepdims=True)
    inverse = lax.rsqrt(variance + EPSILON)
    return centered * inverse, inverse


def normalize_back(grad, normal, inverse):
    return inverse * (
        grad
        - jnp.mean(grad, axis=1, keepdims=True)
        - normal * jnp.mean(grad * normal, axis=1, keepdims=True)
    )


def column_sum(matrix):
    return jnp.sum(matrix.astype(F32), axis=0, keepdims=True)


def feed_kernel(chunk, place_ref, rows_ref, att_ref, cot_ref, wo_ref, wi_ref, wu_ref, vec_ref, bi_ref,
                out_ref, act_ref, inner_ref, normed_ref, outer_ref, low_ref, first_ref, agrad_ref,
                sums_ref, bisum_ref, slope_ref):
    tile, count = rows_ref.shape[0], cot_ref.shape[0]
    hidden_width = wi_ref.shape[1]
    step = pl.program_id(0)

    @pl.when(step == 0)
    def _():
        sums_ref[...] = jnp.zeros_like(sums_ref)
        bisum_ref[...] = jnp.zeros_like(bisum_ref)

    vec = vec_ref[...]
    bo, ga, sa, bu, gf, sf = (vec[i:i + 1] for i in range(2, 8))
    first_sum = rows_ref[...].astype(F32) + dot_nn(att_ref[...], wo_ref[...]) + bo
    normal1, inverse1 = normalize(first_sum)
    normed = normal1 * ga + sa
    normed_low = normed.astype(BF16)
    normed_ref[...] = normed_low
    second = normed + bu
    for at in range(0, hidden_width, chunk):
        pre = dot_nn(normed_low, wi_ref[:, at:at + chunk]) + bi_ref[:, at:at + chunk]
        share = 0.5 + 0.5 * lax.erf(pre * 0.7071067811865476)
        act = (pre * share).astype(BF16)
        act_ref[:, at:at + chunk] = act
        slope_ref[:, at:at + chunk] = share + pre * (jnp.exp(pre * pre * -0.5) * 0.3989422804014327)
        second = second + dot_nn(act, wu_ref[at:at + chunk, :])
    normal2, inverse2 = normalize(second)
    out_ref[...] = (normal2 * gf + sf).astype(BF16)
    lane = lax.broadcasted_iota(jnp.int32, (tile, count), 1)
    chosen = jnp.where(place_ref[...] == lane, 1.0, 0.0).astype(BF16)
    cot = dot_nn(chosen, cot_ref[...])
    second_grad = normalize_back(cot * gf, normal2, inverse2)
    outer_low = second_grad.astype(BF16)
    outer_ref[...] = outer_low
    normed_grad = second_grad
    for at in range(0, hidden_width, chunk):
        act_grad = dot_nt(outer_low, wu_ref[at:at + chunk, :])
        inner_low = (act_grad * slope_ref[:, at:at + chunk]).astype(BF16)
        inner_ref[:, at:at + chunk] = inner_low
        bisum_ref[0:1, at:at + chunk] += column_sum(inner_low)
        normed_grad = normed_grad + dot_nt(inner_low, wi_ref[:, at:at + chunk])
    first_grad = normalize_back(normed_grad * ga, normal1, inverse1)
    first_ref[...] = first_grad
    branch_low = first_grad.astype(BF16)
    low_ref[...] = branch_low
    agrad_ref[...] = dot_nt(branch_low, wo_ref[...]).astype(BF16)
    sums_ref[2:3, :] += column_sum(branch_low)
    sums_ref[3:4, :] += column_sum(normed_grad * normal1)
    sums_ref[4:5, :] += column_sum(normed_grad)
    sums_ref[5:6, :] += column_sum(outer_low)
    sums_ref[6:7, :] += column_sum(cot * normal2)
    sums_ref[7:8, :] += column_sum(cot)


def feed_forward(place_col, rows, attended, arrived_cot, w4, wi, wu, vec, bi):
    count, width = rows.shape
    hidden_width = wi.shape[1]
    tile = count // 4
    row_spec = pl.BlockSpec((tile, width), lambda i: (i, 0))
    wide_spec = pl.BlockSpec((tile, hidden_width), lambda i: (i, 0))

    def rows_of(n, dtype):
        return jax.ShapeDtypeStruct((count, n), dtype)

    return pl.pallas_call(
        partial(feed_kernel, 512),
        grid=(4,),
        out_shape=[
            rows_of(width, BF16), rows_of(hidden_width, BF16), rows_of(hidden_width, BF16), rows_of(width, BF16),
            rows_of(width, BF16), rows_of(width, BF16), rows_of(width, F32), rows_of(width, BF16),
            jax.ShapeDtypeStruct((8, width), F32), jax.ShapeDtypeStruct((8, hidden_width), F32),
        ],
        in_specs=[
            pl.BlockSpec((tile, 1), lambda i: (i, 0)), row_spec, row_spec, held_spec((count, width)),
            pl.BlockSpec((pl.Squeezed(), width, width), lambda i: (3, 0, 0), pipeline_mode=pl.Buffered(1)),
            held_spec(wi.shape), held_spec(wu.shape), held_spec(vec.shape), held_spec(bi.shape),
        ],
        out_specs=[row_spec, wide_spec, wide_spec] + [row_spec] * 5
        + [full_spec((8, width)), full_spec((8, hidden_width))],
        scratch_shapes=[pltpu.VMEM((tile, hidden_width), F32)],
        compiler_params=params(56, "arbitrary"),
        cost_estimate=pl.CostEstimate(flops=12 * count * width * hidden_width, bytes_accessed=36 * MIB, transcendentals=2 * count * hidden_width),
        name="feed_forward",
    )(place_col, rows, attended, arrived_cot, w4, wi, wu, vec, bi)


def finish_kernel(sizes, share, where_ref, rank_ref, first_hbm, dq_hbm, dk_hbm, dv_hbm, w4_hbm, rows_hbm, returned_hbm, small_ref,
                  layer_ref, tokens_ref, wq_out, wk_out, wv_out, small_out,
                  first_ref, dq_ref, dk_ref, dv_ref, w_ref, rows_ref, returned_ref, load_sems,
                  total_ref, leaving_ref, back_ref, wq_ref, wk_ref, wv_ref, swap_sems, swap_local, *tree_refs):
    count, width = total_ref.shape
    devices = count and sizes[0] * sizes[1] * sizes[2] * sizes[3]
    na, nb, nc, nk = sizes
    tile = count // 4
    loads = [
        pltpu.make_async_copy(source, target, load_sems.at[i])
        for i, (source, target) in enumerate((
            (first_hbm, first_ref), (dq_hbm, dq_ref), (w4_hbm.at[pl.ds(0, 3)], w_ref), (dk_hbm, dk_ref), (dv_hbm, dv_ref),
            (rows_hbm, rows_ref), (returned_hbm, returned_ref),
        ))
    ]
    for load in loads:
        load.start()
    place = Place(sizes)
    swap = Exchange(devices, leaving_ref, back_ref, swap_sems, swap_local)
    parts = (wq_ref, wk_ref, wv_ref, small_ref)
    trees = [Tree(place, flip, ref, tree_refs[7 * i:7 * i + 7]) for i, (flip, ref) in enumerate(zip((False, True, False, True), parts))]
    greet_all(devices)
    for load in loads[:5]:
        load.wait()
    trees[3].start(0)
    for at in range(0, count, tile):
        cut = slice(at, at + tile)
        total_ref[cut] = (
            first_ref[cut] + dot_nt(dq_ref[cut], w_ref[0]) + dot_nt(dk_ref[cut], w_ref[1]) + dot_nt(dv_ref[cut], w_ref[2])
        ).astype(BF16)
    for at in range(0, count, tile):
        target = lax.broadcasted_iota(jnp.int32, (tile, count), 0) + at
        chosen = jnp.where(where_ref[...] == target, 1.0, 0.0).astype(BF16)
        leaving_ref[at:at + tile] = dot_nn(chosen, total_ref[...]).astype(BF16)
    swap.start()
    loads[5].wait()
    group = 3 * LANES
    for grad_ref, out_ref, tree in zip((dq_ref, dk_ref, dv_ref), parts, trees):
        for at in range(0, width, group):
            value = dot_tn(rows_ref[:, at:at + group], grad_ref[...])
            for i in range(group // share):
                d = at // share + i
                index = (d // (nk * nc * nb), d // (nk * nc) % nb, d // nk % nc, d % nk)
                out_ref[index] = value[i * share:(i + 1) * share].astype(BF16)
        tree.start(0)
    loads[6].wait()

    def restore(out_ref, from_ref):
        for at in range(0, count, tile):
            lane = lax.broadcasted_iota(jnp.int32, (tile, count), 1)
            chosen = jnp.where(rank_ref[at:at + tile] == lane, 1.0, 0.0).astype(BF16)
            out_ref[at:at + tile] = dot_nn(chosen, from_ref[...]).astype(BF16)

    for stage in range(3):
        for tree in trees:
            tree.settle(stage)
            tree.start(stage + 1)
        if stage == 0:
            restore(layer_ref, returned_ref)
    for tree, out in zip(trees, (wq_out, wk_out, wv_out, small_out)):
        tree.settle(3, out)
    swap.wait()
    restore(tokens_ref, back_ref)
    for tree in trees:
        tree.drain()


def finish(place_row, rank_col, first_grad, dq, dk, dv, w4, rows, returned, small):
    count, width = dq.shape
    devices = small.shape[0]
    sizes = grid_of(devices)
    share = width // devices
    anywhere = pl.BlockSpec(memory_space=pl.ANY)
    in_vmem = pl.BlockSpec(memory_space=pltpu.VMEM)
    whole = pltpu.VMEM((count, width), BF16)
    trees = []
    for flip, shape in zip((False, True, False, True), ((share, width),) * 3 + (small.shape[1:],)):
        trees += tree_scratch(sizes, flip, *shape)
    return pl.pallas_call(
        partial(finish_kernel, sizes, share),
        out_shape=[jax.ShapeDtypeStruct((count, width), BF16)] * 2
        + [jax.ShapeDtypeStruct((share, width), F32)] * 3 + [jax.ShapeDtypeStruct(small.shape[1:], F32)],
        in_specs=[in_vmem] * 2 + [anywhere] * 7 + [in_vmem],
        out_specs=[in_vmem] * 6,
        scratch_shapes=[pltpu.VMEM((count, width), F32)] + [whole] * 3 + [pltpu.VMEM((3, width, width), BF16)] + [whole] * 2
        + [pltpu.SemaphoreType.DMA((7,))] + [whole] * 3 + [pltpu.VMEM(sizes + (share, width), BF16)] * 3
        + [pltpu.SemaphoreType.DMA((2, devices)), pltpu.SemaphoreType.DMA(())] + trees,
        compiler_params=pltpu.CompilerParams(collective_id=3, has_side_effects=True, vmem_limit_bytes=60 * MIB),
        name="finish",
    )(place_row, rank_col, first_grad, dq, dk, dv, w4, rows, returned, small.reshape(sizes + small.shape[1:]))


def on_device(tokens, cotangent, packed_slot, seq_lengths, query_weight, query_bias, key_weight, value_weight,
              value_bias, output_weight, output_bias, attention_gain, attention_shift, inner_weight, inner_bias,
              outer_weight, outer_bias, final_gain, final_shift):
    devices = lax.axis_size("fsdp")
    me = lax.axis_index("fsdp")
    count, width = tokens.shape
    hidden_width = inner_bias.shape[0] * devices
    peer_rows = count // devices
    segments = seq_lengths.shape[1]
    share = width // devices
    counting = jnp.arange(count, dtype=jnp.int32)

    def exchange(rows):
        pieces = rows.reshape(devices, peer_rows, width)
        return lax.all_to_all(pieces, "fsdp", split_axis=0, concat_axis=0, tiled=True).reshape(count, width)

    own_slots = lax.dynamic_slice_in_dim(packed_slot, me * count, count)
    rank = jnp.sum((own_slots[None, :] < own_slots[:, None]).astype(jnp.int32), axis=1)
    rank_row, rank_col = rank.reshape(1, count), rank.reshape(count, 1)
    arrived = exchange(permute_rows(rank_row, tokens))
    arrived_cot = exchange(permute_rows(rank_row, cotangent))

    w4 = jnp.stack([w.reshape(share, width) for w in (query_weight, key_weight, value_weight, output_weight)])
    small = (query_bias, value_bias, output_bias, attention_gain, attention_shift, outer_bias, final_gain, final_shift)
    vec = jnp.concatenate(small + (inner_bias,))
    used = vec.shape[0]
    vec = jnp.pad(vec, (0, 8 * LANES - used)).reshape(8, LANES)
    g4, gi, gu, gv = gather_parameters(
        devices, w4, inner_weight.reshape(share, hidden_width), outer_weight.reshape(hidden_width // devices, width), vec
    )
    w4 = g4.reshape(4, width, width)
    wi = gi.reshape(width, hidden_width)
    wu = gu.reshape(hidden_width, width)
    flat = gv.reshape(devices, 8 * LANES).astype(F32)
    vec = flat[:, : 8 * share].reshape(devices, 8, share).transpose(1, 0, 2).reshape(8, width)
    bi = flat[:, 8 * share : used].reshape(1, hidden_width)

    local_slots = packed_slot.reshape(devices, count) - me * count
    source = source_devices(local_slots, count).astype(jnp.int32).reshape(count)
    same = (source[:, None] == source[None, :]) & (counting[None, :] < counting[:, None])
    place = source * peer_rows + jnp.sum(same.astype(jnp.int32), axis=1)
    place_row, place_col = place.reshape(1, count), place.reshape(count, 1)
    ends = jnp.cumsum(seq_lengths[0], dtype=jnp.int32)
    segment = jnp.sum((counting[:, None] >= ends[None, :]).astype(jnp.int32), axis=1)
    segment_col = segment.reshape(count, 1)

    rows, q, k, v = project(place_col, arrived, w4, vec)
    attended, lse = attend(segments, segment_col, q, k, v)
    (result, activated, inner_low, normed_low, outer_low, branch_low, first_grad, attended_grad, sums, bi_sum) = feed_forward(
        place_col, rows, attended, arrived_cot, w4, wi, wu, vec, bi
    )
    leaving = permute_rows(place_row, result)

    def weight_grad(left, right):
        grad = dot_tn(left, right).astype(BF16)
        return grad.reshape(devices, -1, grad.shape[-1])

    inner_grad = weight_grad(normed_low, inner_low)
    outer_grad = weight_grad(activated, outer_low)
    wo_grad = weight_grad(attended, branch_low)
    dq, dk, dv, more, returned, inner_grad, outer_grad, wo_grad = attend_back(
        segments, segment_col, q, attended, attended_grad, lse, k, v, leaving, inner_grad, outer_grad, wo_grad
    )
    sums = sums + more
    sums = sums.reshape(8, devices, share).transpose(1, 0, 2).reshape(devices, 8 * share)
    sums = jnp.concatenate([sums, bi_sum[0].reshape(devices, hidden_width // devices)], axis=1)
    sums = jnp.pad(sums, ((0, 0), (0, 8 * LANES - used))).reshape(devices, 8, LANES).astype(BF16)
    layer_out, tokens_grad, wq_grad, wk_grad, wv_grad, sums = finish(
        place_row, rank_col, first_grad, dq, dk, dv, w4, rows, returned, sums
    )
    wq_grad, wk_grad, wv_grad, wo_grad = (x.reshape(-1) for x in (wq_grad, wk_grad, wv_grad, wo_grad))
    sums = sums.reshape(-1)
    small = [sums[i * share:(i + 1) * share] for i in range(8)]
    return (
        layer_out, tokens_grad, wq_grad, small[0], wk_grad, wv_grad, small[1], wo_grad, small[2], small[3], small[4],
        inner_grad.reshape(-1), sums[8 * share:used], outer_grad.reshape(-1), small[5], small[6], small[7],
    )


def solution(mesh):
    split, rows = P("fsdp"), P("fsdp", None)
    return jax.shard_map(
        on_device,
        mesh=mesh,
        in_specs=(rows, rows, P(), rows) + (split,) * 15,
        out_specs=(rows, rows) + (split,) * 15,
        check_vma=False,
    )
```

```python
from functools import partial

import jax
import jax.numpy as jnp
from jax import lax
from jax.experimental import pallas as pl
from jax.experimental.pallas import tpu as pltpu
from jax.sharding import PartitionSpec as P

HD = 64
LANES = 128
EPSILON = 1e-12
NEG_LARGE = -1e30
MIB = 1 << 20
F32 = jnp.float32
BF16 = jnp.bfloat16
MESH = pl.DeviceIdType.MESH


def dot_nn(a, b):
    return lax.dot_general(a, b, (((1,), (0,)), ((), ())), preferred_element_type=F32)


def dot_nt(a, b):
    return lax.dot_general(a, b, (((1,), (1,)), ((), ())), preferred_element_type=F32)


def dot_tn(a, b):
    return lax.dot_general(a, b, (((0,), (0,)), ((), ())), preferred_element_type=F32)


def full_spec(shape, **kw):
    return pl.BlockSpec(shape, lambda *_: (0,) * len(shape), **kw)


def held_spec(shape):
    return full_spec(shape, pipeline_mode=pl.Buffered(1))


def params(mib, *axes, **kw):
    return pltpu.CompilerParams(
        dimension_semantics=axes or None, vmem_limit_bytes=mib * MIB, **kw
    )


def grid_of(devices):
    return {32: (4, 2, 2, 2), 128: (4, 4, 4, 2)}.get(devices, (devices, 1, 1, 1))


class Place:
    def __init__(self, sizes):
        na, nb, nc, nk = self.sizes = sizes
        self.me = me = lax.axis_index("fsdp")
        self.k = me % nk
        self.c = (me // nk) % nc
        self.b = (me // (nk * nc)) % nb
        self.a = me // (nk * nc * nb)

    def ahead(self, axis, step):
        own = (self.a, self.b, self.c, self.k)[axis]
        return (own + step) % self.sizes[axis]

    def device(self, axis, step):
        na, nb, nc, nk = self.sizes
        where = [self.a, self.b, self.c, self.k]
        where[axis] = self.ahead(axis, step)
        return ((where[0] * nb + where[1]) * nc + where[2]) * nk + where[3]


def remote(source, target, send_sem, recv_sem, peer):
    return pltpu.make_async_remote_copy(
        src_ref=source, dst_ref=target, send_sem=send_sem, recv_sem=recv_sem,
        device_id=(peer,), device_id_type=MESH,
    )


def greet_all(devices):
    me = lax.axis_index("fsdp")
    barrier = pltpu.get_barrier_semaphore()

    def signal(j, carry):
        pl.semaphore_signal(barrier, inc=1, device_id=((me + j) % devices,), device_id_type=MESH)
        return carry

    lax.fori_loop(1, devices, signal, 0)
    pl.semaphore_wait(barrier, devices - 1)


class Exchange:
    def __init__(self, devices, source, target, sems, local_sem, turns=None):
        self.devices, self.source, self.target, self.sems, self.local_sem = devices, source, target, sems, local_sem
        self.turns = turns or (1, devices)
        self.rows = source.shape[0] // devices
        self.me = lax.axis_index("fsdp")

    def block(self, ref, device):
        return ref.at[pl.ds(pl.multiple_of(device * self.rows, self.rows), self.rows)]

    def own(self):
        return pltpu.make_async_copy(self.block(self.source, self.me), self.block(self.target, self.me), self.local_sem)

    def outgoing(self, j):
        peer = (self.me + j) % self.devices
        return remote(self.block(self.source, peer), self.block(self.target, self.me), self.sems.at[0, j], self.sems.at[1, j], peer)

    def incoming(self, j):
        peer = (self.me + self.devices - j) % self.devices
        block = self.block(self.target, peer)
        return remote(block, block, self.sems.at[0, j], self.sems.at[1, j], peer)

    def over(self, act):
        def body(j, carry):
            act((j * 13) % self.devices)
            return carry

        lax.fori_loop(*self.turns, body, 0)

    def start(self):
        self.own().start()
        self.start_remote()

    def start_remote(self):
        self.over(lambda j: self.outgoing(j).start())

    def wait(self):
        self.wait_remote()
        self.own().wait()

    def wait_remote(self):
        self.over(lambda j: self.incoming(j).wait_recv())
        self.over(lambda j: self.outgoing(j).wait_send())


def greet_peers(place):
    barrier = pltpu.get_barrier_semaphore()
    count = 0
    for axis, size in enumerate(place.sizes):
        for j in range(1, size):
            pl.semaphore_signal(barrier, inc=1, device_id=(place.device(axis, j),), device_id_type=MESH)
            count += 1
    pl.semaphore_wait(barrier, count)


def spread_scratch(sizes):
    return [pltpu.SemaphoreType.DMA((2, 4, max(sizes))), pltpu.SemaphoreType.DMA(())]


class Spread:
    def __init__(self, place, flip, own, out, scratch, lead=()):
        self.place, self.flip, self.mine, self.out, self.lead = place, flip, own, out, lead
        self.sems, self.local_sem = scratch
        self.axes = (0, 1, 2, 3) if flip else (0, 2, 1, 3)

    def region(self, stage, step=0):
        place, every = self.place, slice(None)
        where = [place.a, place.b, place.c, place.k]
        axis = self.axes[stage]
        where[axis] = place.ahead(axis, step)
        for done in self.axes[:stage]:
            where[done] = every
        return self.out.at[self.lead + tuple(where)]

    def local(self):
        return pltpu.make_async_copy(self.mine, self.region(0), self.local_sem)

    def outgoing(self, stage):
        axis = self.axes[stage]
        source = self.mine if stage == 0 else self.region(stage)
        return [
            remote(source, self.region(stage), self.sems.at[0, stage, j], self.sems.at[1, stage, j], self.place.device(axis, j))
            for j in range(1, self.place.sizes[axis])
        ]

    def start(self, stage):
        for copy in self.outgoing(stage):
            copy.start()
        if stage == 0:
            self.local().start()

    def settle(self, stage):
        axis = self.axes[stage]
        if stage == 0:
            self.local().wait()
        for j in range(1, self.place.sizes[axis]):
            block = self.region(stage, self.place.sizes[axis] - j)
            remote(block, block, self.sems.at[0, stage, j], self.sems.at[1, stage, j], self.place.device(axis, j)).wait_recv()

    def drain(self):
        for stage in range(4):
            for copy in self.outgoing(stage):
                copy.wait_send()


def store_flat(ref, base, value):
    rows, columns = value.shape
    width = ref.shape[0] // rows
    for j in range(columns // LANES):
        ref[pl.ds(base + j, rows, stride=width), :] = value[:, j * LANES:(j + 1) * LANES]


def tree_scratch(sizes, flip, rows, columns):
    na, nb, nc, nk = sizes
    one, two = (nb, nc) if flip else (nc, nb)
    shapes = [(na, nb, nc), (nk - 1, na, nb, nc), (one - 1, na, two), (two - 1, na), (na - 1,)]
    return [pltpu.VMEM(shape + (rows, columns), BF16) for shape in shapes] + [
        pltpu.SemaphoreType.DMA((2, 4, max(sizes))),
        pltpu.SemaphoreType.DMA(()),
    ]


class Tree:
    def __init__(self, place, flip, parts, scratch):
        self.place, self.flip, self.parts = place, flip, parts
        self.held, *self.landing, self.sems, self.local_sem = scratch
        order = (3, 1, 2, 0) if flip else (3, 2, 1, 0)
        self.axes = order

    def own(self):
        return pltpu.make_async_copy(self.parts.at[:, :, :, self.place.k], self.held, self.local_sem)

    def outgoing(self, stage):
        place, held = self.place, self.held
        axis = self.axes[stage]
        copies = []
        for j in range(1, place.sizes[axis]):
            other = place.ahead(axis, j)
            if stage == 0:
                source = self.parts.at[:, :, :, other]
            elif stage == 1:
                source = held.at[:, other] if self.flip else held.at[:, :, other]
            elif stage == 2:
                source = held.at[:, place.b, other] if self.flip else held.at[:, other, place.c]
            else:
                source = held.at[other, place.b, place.c]
            copies.append(
                remote(source, self.landing[stage].at[j - 1], self.sems.at[0, stage, j], self.sems.at[1, stage, j], place.device(axis, j))
            )
        return copies

    def start(self, stage):
        if stage == 0:
            self.own().start()
        for copy in self.outgoing(stage):
            copy.start()

    def settle(self, stage, out=None):
        place, held, landing = self.place, self.held, self.landing[stage]
        na, nb, nc, nk = place.sizes
        if stage == 0:
            self.own().wait()
        for copy in self.outgoing(stage):
            copy.wait_recv()
        count = place.sizes[self.axes[stage]] - 1

        def total(own, index):
            value = own.astype(F32)
            for j in range(count):
                value = value + landing[(j,) + index].astype(F32)
            return value

        if stage == 0:
            def add(i, carry):
                held[i] = total(held[i], (i,)).astype(BF16)
                return carry
            lax.fori_loop(0, na, add, 0)
        elif stage == 1:
            two = nc if self.flip else nb
            def add(i, carry):
                for t in range(two):
                    at = (i, place.b, t) if self.flip else (i, t, place.c)
                    held[at] = total(held[at], (i, t)).astype(BF16)
                return carry
            lax.fori_loop(0, na, add, 0)
        elif stage == 2:
            def add(i, carry):
                at = (i, place.b, place.c)
                held[at] = total(held[at], (i,)).astype(BF16)
                return carry
            lax.fori_loop(0, na, add, 0)
        else:
            out(total(held[place.a, place.b, place.c], ()))

    def drain(self):
        for stage in range(4):
            for copy in self.outgoing(stage):
                copy.wait_send()


LOW = 32


def select_rows(chosen, rows_ref):
    return dot_nn(jnp.where(chosen, 1.0, 0.0).astype(BF16), rows_ref[...]).astype(BF16)


def count_true(mask, axis):
    return jnp.sum(jnp.where(mask, 1.0, 0.0), axis=axis, keepdims=True)


def load_flat(ref, base_ref, width, store):
    total = ref.shape[0]
    base_ref[0:total, :] = ref[...].astype(F32)
    per_row = width // LANES
    for j in range(per_row):
        store(j * LANES, base_ref[pl.ds(j, total // per_row, stride=per_row), :].astype(BF16))


def arrive_kernel(sizes, lengths_ref, *refs):
    given, outs, held = refs[:18], refs[18:28], refs[28:46]
    leaving_ref, flat_ref, w4_hbm, wi_own, lines_ref, vec_hbm, load_sems, swap_sems, swap_local, *spread_refs = refs[46:]
    arrived_ref, cot_out, g4, gv, gi, place_row, place_col, rank_out, segment_out, wu_out = outs
    w4_refs, small_refs = held[:4], held[4:13]
    slots_ref, tokens_ref, cot_ref, wi_ref, wu_ref = held[13:]
    loads = [pltpu.make_async_copy(source, target, load_sems.at[i]) for i, (source, target) in enumerate(zip(given, held))]
    for load in loads:
        load.start()
    for load in loads:
        load.wait()
    count = tokens_ref.shape[0]
    devices = slots_ref.shape[0]
    peer_rows = count // devices
    tile = count // 4
    place = Place(sizes)
    me = place.me
    spreads = [
        Spread(place, False, w4_hbm.at[pl.ds(0, 2)], g4, spread_refs[0:2], (pl.ds(0, 2),)),
        Spread(place, True, w4_hbm.at[pl.ds(2, 2)], g4, spread_refs[2:4], (pl.ds(2, 2),)),
        Spread(place, True, vec_hbm, gv, spread_refs[4:6]),
    ]
    half = wi_own.shape[1] // 2
    for i in range(2):
        cut = pl.ds(i * half, half)
        spreads.append(Spread(place, i == 1, wi_own.at[:, cut], gi.at[:, :, :, :, :, cut], spread_refs[6 + 2 * i:8 + 2 * i]))
    swap = Exchange(devices, leaving_ref, arrived_ref, swap_sems, swap_local)
    width = tokens_ref.shape[1]
    for i, ref in enumerate(w4_refs):
        def put(at, value, i=i):
            w4_hbm[i, :, at:at + LANES] = value
        load_flat(ref, flat_ref, width, put)
    def put_inner(at, value):
        wi_own[:, at:at + LANES] = value

    load_flat(wi_ref, flat_ref, wi_own.shape[1], put_inner)
    lines_ref[...] = jnp.zeros_like(lines_ref)
    for i, ref in enumerate(small_refs):
        lines_ref[i:i + 1, 0:ref.shape[1]] = ref[...].astype(F32)
    vec_hbm[...] = lines_ref[...].astype(BF16)
    greet_all(devices)
    for spread in spreads:
        spread.start(0)

    cuts = [(at, slice(at, at + tile)) for at in range(0, count, tile)]
    row_at = [lax.broadcasted_iota(jnp.int32, (tile, count), 0) + at for at, _ in cuts]
    lane = lax.broadcasted_iota(jnp.int32, (tile, count), 1)
    own_row = slots_ref[pl.ds(me, 1), :]
    own_float = own_row.astype(F32)
    own_col = [jnp.sum(jnp.where(lane == row, own_float, 0.0), axis=1, keepdims=True) for row in row_at]
    rank_row = sum(count_true(col < own_float, 0) for col in own_col).astype(jnp.int32)
    for (_, cut), row in zip(cuts, row_at):
        leaving_ref[cut] = select_rows(rank_row == row, tokens_ref)
    swap.start()
    for (_, cut), row, col in zip(cuts, row_at, own_col):
        cot_out[cut] = select_rows(rank_row == row, cot_ref)
        rank_out[cut] = count_true(own_float < col, 1).astype(jnp.int32)

    def put_outer(at, value):
        wu_out[:, at:at + LANES] = value

    load_flat(wu_ref, flat_ref, width, put_outer)
    row = lax.broadcasted_iota(jnp.int32, (count, 1), 0)
    end, segment = 0, jnp.zeros((count, 1), jnp.int32)
    for i in range(lengths_ref.shape[1]):
        end = end + lengths_ref[0, i]
        segment = segment + jnp.where(row >= end, 1, 0)
    segment_out[...] = segment

    high = count // LOW

    def body(s, total):
        local = slots_ref[pl.ds(s, 1), :] - me * count
        in_high = lax.broadcasted_iota(jnp.int32, (high, count), 0) == (local >> 5)
        in_low = lax.broadcasted_iota(jnp.int32, (LOW, count), 0) == (local & (LOW - 1))
        weight = jnp.where(in_high, s.astype(F32), 0.0).astype(BF16)
        return total + dot_nt(weight, jnp.where(in_low, 1.0, 0.0).astype(BF16))

    source = lax.fori_loop(0, devices, body, jnp.zeros((high, LOW), F32)).astype(BF16)
    wide = lax.broadcasted_iota(jnp.int32, (high, count), 1)
    picked = dot_tn(source, jnp.where((wide >> 5) == lax.broadcasted_iota(jnp.int32, (high, count), 0), 1.0, 0.0).astype(BF16))
    low_row = lax.broadcasted_iota(jnp.int32, (LOW, count), 0)
    low_wide = lax.broadcasted_iota(jnp.int32, (LOW, count), 1) & (LOW - 1)
    source_row = jnp.sum(jnp.where(low_row == low_wide, picked, 0.0), axis=0, keepdims=True)
    places = source_row * peer_rows
    for (_, cut), row in zip(cuts, row_at):
        source_col = jnp.sum(jnp.where(lane == row, source_row, 0.0), axis=1, keepdims=True)
        same = source_col == source_row
        place_col[cut] = (source_col * peer_rows + count_true(same & (lane < row), 1)).astype(jnp.int32)
        places = places + count_true(same & (row < lane), 0)
    place_row[...] = places.astype(jnp.int32)

    for stage in range(4):
        for spread in spreads:
            spread.settle(stage)
            if stage < 3:
                spread.start(stage + 1)
    swap.wait()
    for spread in spreads:
        spread.drain()


def arrive(seq_lengths, packed_slot, tokens, cotangent, w4, wi, wu, small):
    devices, count = packed_slot.shape
    width = tokens.shape[1]
    hidden_width = small[-1].shape[0] * devices
    sizes = grid_of(devices)
    share = width // devices
    anywhere = pl.BlockSpec(memory_space=pl.ANY)
    in_vmem = pl.BlockSpec(memory_space=pltpu.VMEM)

    def shape(*dims, dtype=BF16):
        return jax.ShapeDtypeStruct(dims, dtype)

    flat = [w.reshape(-1, LANES) for w in w4]
    given = flat + [x.reshape(1, -1) for x in small] + [packed_slot, tokens, cotangent, wi.reshape(-1, LANES), wu.reshape(-1, LANES)]
    return pl.pallas_call(
        partial(arrive_kernel, sizes),
        out_shape=[shape(count, width), shape(count, width), shape(4, *sizes, share, width), shape(*sizes, 16, LANES),
                   shape(*sizes, share, hidden_width), shape(1, count, dtype=jnp.int32)] + [shape(count, 1, dtype=jnp.int32)] * 3
        + [shape(hidden_width // devices, width)],
        in_specs=[pl.BlockSpec(memory_space=pltpu.SMEM)] + [anywhere] * len(given),
        out_specs=[in_vmem] * 2 + [anywhere] * 3 + [in_vmem] * 5,
        scratch_shapes=[pltpu.VMEM(x.shape, x.dtype) for x in given]
        + [pltpu.VMEM((count, width), BF16), pltpu.VMEM(given[-1].shape, F32), pltpu.VMEM((4, share, width), BF16),
           pltpu.VMEM((share, hidden_width), BF16), pltpu.VMEM((16, LANES), F32), pltpu.VMEM((16, LANES), BF16), pltpu.SemaphoreType.DMA((len(given),)),
           pltpu.SemaphoreType.DMA((2, devices)), pltpu.SemaphoreType.DMA(())] + spread_scratch(sizes) * 5,
        compiler_params=pltpu.CompilerParams(collective_id=1, has_side_effects=True, vmem_limit_bytes=56 * MIB),
        name="arrive",
    )(seq_lengths, *given)


def split3(column):
    high = column.astype(BF16).astype(F32)
    rest = column - high
    mid = rest.astype(BF16).astype(F32)
    return high, mid, rest - mid


def feature_lanes(rows):
    lane = lax.broadcasted_iota(jnp.int32, (rows, LANES), 1)
    return lane < HD, lane & (HD - 1)


def key_features(lane, segment, segments):
    return jnp.where(lane == segment, 1.0, jnp.where((lane >= segments) & (lane < segments + 3), 1.0, 0.0))


def query_features(lane, segment, segments):
    return jnp.where((lane < segments) & (lane != segment), NEG_LARGE, 0.0)


def with_column(features, lane, start, column):
    high, mid, last = split3(column)
    features = jnp.where(lane == start, high, features)
    features = jnp.where(lane == start + 1, mid, features)
    return jnp.where(lane == start + 2, last, features)


def attend_kernel(segments, sizes, cuts, tiles, place_ref, arrived_ref, w4_hbm, vec_ref, seg_ref, wu_hbm, cot_hbm,
                  out_ref, lse_ref, rows_hbm, q_hbm, k_hbm, v_hbm, gu, cot_out,
                  w_ref, rows_ref, q_ref, k_ref, v_ref, k0, k1, load_sem, save_sems, swap_sems, swap_local, *spread_refs):
    count = arrived_ref.shape[0]
    tile = count // tiles
    now, last = pl.program_id(0), pl.num_programs(0) - 1
    place = Place(sizes)
    every = (slice(None),) * 5
    spreads = []
    for i, (base, columns, flip) in enumerate(cuts):
        cut = pl.ds(base, columns)
        spreads.append(Spread(place, flip, wu_hbm.at[:, cut], gu.at[every + (cut,)], spread_refs[2 * i:2 * i + 2]))
    devices = sizes[0] * sizes[1] * sizes[2] * sizes[3]
    swap = Exchange(devices, cot_hbm, cot_out, swap_sems, swap_local, (1, devices // 2))
    load = pltpu.make_async_copy(w4_hbm.at[pl.ds(0, 3)], w_ref, load_sem)
    saves = [
        pltpu.make_async_copy(source, target, save_sems.at[i])
        for i, (source, target) in enumerate(((rows_ref, rows_hbm), (q_ref, q_hbm), (k_ref, k_hbm), (v_ref, v_hbm)))
    ]

    @pl.when(now == 0)
    def _():
        load.start()
        greet_all(devices)
        for spread in spreads[:2]:
            spread.start(0)
        load.wait()

    def hook(at, act):
        @pl.when(now == at)
        def _():
            act()

    def onward(pair, stage, then=None):
        for spread in spreads[2 * pair:2 * pair + 2]:
            spread.settle(stage)
        if then is not None:
            for spread in spreads[2 * then:2 * then + 2]:
                spread.start(0)
        for spread in spreads[2 * pair:2 * pair + 2]:
            if stage < 3:
                spread.start(stage + 1)

    hook(4, lambda: (onward(0, 0, 1), swap.start_remote()))
    hook(9, lambda: (onward(0, 1), onward(1, 0)))
    hook(16, lambda: (onward(0, 2), onward(1, 1)))
    hook(21, lambda: onward(1, 2))

    @pl.when(now < tiles)
    def _():
        cut = pl.ds(pl.multiple_of(now * tile, tile), tile)
        lane = lax.broadcasted_iota(jnp.int32, (tile, count), 1)
        rows = select_rows(place_ref[cut, :] == lane, arrived_ref)
        rows_ref[cut, :] = rows
        vec = vec_ref[...]
        q_ref[cut, :] = ((dot_nn(rows, w_ref[0]) + vec[0:1]).astype(BF16).astype(F32) * 0.125).astype(BF16)
        k_ref[cut, :] = dot_nn(rows, w_ref[1]).astype(BF16)
        v_ref[cut, :] = (dot_nn(rows, w_ref[2]) + vec[1:2]).astype(BF16)

    @pl.when(now == tiles)
    def _():
        for save in saves:
            save.start()

    work = now - tiles
    columns = pl.ds(pl.multiple_of(jnp.maximum(work, 0) // tiles * LANES, LANES), LANES)

    @pl.when((now >= tiles) & (work % tiles == 0))
    def _():
        first_all, lane_all = feature_lanes(count)
        extra = key_features(lane_all, seg_ref[...], segments).astype(BF16)
        keys = k_ref[:, columns]
        k0[...] = jnp.where(first_all, keys, extra)
        k1[...] = jnp.where(first_all, extra, keys)

    @pl.when(now >= tiles)
    def _():
        cut = pl.ds(pl.multiple_of(work % tiles * tile, tile), tile)
        first, lane = feature_lanes(tile)
        extra = query_features(lane, seg_ref[cut, :], segments).astype(BF16)
        queries = q_ref[cut, columns]
        values = v_ref[:, columns]
        outs, logs = [], []
        for mask, keys in ((first, k0), (~first, k1)):
            scores = dot_nt(jnp.where(mask, queries, extra), keys[...])
            top = jnp.max(scores, axis=1, keepdims=True)
            raised = jnp.exp(scores - top)
            total = jnp.sum(raised, axis=1, keepdims=True)
            outs.append(dot_nn(raised.astype(BF16), values) * (1.0 / total))
            logs.append(top + jnp.log(total))
        out_ref[...] = jnp.where(first, outs[0], outs[1]).astype(BF16)
        lse_ref[...] = jnp.where(first, logs[0], logs[1])

    @pl.when(now == last)
    def _():
        onward(0, 3)
        onward(1, 3)
        for spread in spreads:
            spread.drain()
        swap.wait_remote()
        for save in saves:
            save.wait()


def attend(devices, segments, place_col, arrived, w4, vec, segment_col, wu, leaving_cot):
    count, width = arrived.shape
    pairs = width // LANES
    tiles = 4
    tile = count // tiles
    sizes = grid_of(devices)
    anywhere = pl.BlockSpec(memory_space=pl.ANY)
    part = wu.shape[1] // 6
    cuts = [(0, 2 * part, False), (2 * part, 2 * part, True), (4 * part, part, False), (5 * part, part, True)]

    def tile_at(i):
        work = jnp.maximum(i - tiles, 0)
        return work % tiles, work // tiles

    tile_spec = pl.BlockSpec((tile, LANES), tile_at)
    whole = jax.ShapeDtypeStruct((count, width), BF16)
    held = pltpu.VMEM((count, width), BF16)
    return pl.pallas_call(
        partial(attend_kernel, segments, sizes, cuts, tiles),
        grid=(tiles + pairs * tiles,),
        out_shape=[whole, jax.ShapeDtypeStruct((count, width), F32)] + [whole] * 4
        + [jax.ShapeDtypeStruct(sizes + wu.shape, BF16), whole],
        in_specs=[held_spec((count, 1)), held_spec((count, width)), anywhere, held_spec(vec.shape), held_spec((count, 1))] + [anywhere] * 2,
        out_specs=[tile_spec, tile_spec] + [anywhere] * 6,
        scratch_shapes=[pltpu.VMEM((3, width, width), BF16)] + [held] * 4 + [pltpu.VMEM((count, LANES), BF16)] * 2
        + [pltpu.SemaphoreType.DMA(()), pltpu.SemaphoreType.DMA((4,)),
           pltpu.SemaphoreType.DMA((2, devices)), pltpu.SemaphoreType.DMA(())] + spread_scratch(sizes) * len(cuts),
        compiler_params=params(56, "arbitrary", collective_id=4, has_side_effects=True),
        cost_estimate=pl.CostEstimate(flops=8 * count * count * width, bytes_accessed=10 * MIB, transcendentals=count * count * 12),
        name="attend",
    )(place_col, arrived, w4, vec, segment_col, wu, leaving_cot)


def attend_back_kernel(segments, sizes, cuts, seg_ref, q_ref, o_ref, g_ref, lse_ref, seg_all_ref, k_ref, v_ref,
                       wi_ref, wu_ref, wo_ref,
                       dq_ref, dk_ref, dv_ref, sums_ref, wi_out, wu_out, wo_out,
                       k0, k1, v0, v1, dk_sum, dv_sum, *tree_refs):
    count, tile = k_ref.shape[0], q_ref.shape[0]
    first_all, lane_all = feature_lanes(count)
    step, last = pl.program_id(1), pl.num_programs(1) - 1
    now = pl.program_id(0) * pl.num_programs(1) + step

    place = Place(sizes)
    outs = {0: wi_out, 1: wu_out, 2: wo_out}
    every = (slice(None),) * 5
    trees, ends = [], []
    for i, (which, base, columns, flip) in enumerate(cuts):
        parts = (wi_ref, wu_ref, wo_ref)[which].at[every + (pl.ds(base, columns),)]
        trees.append(Tree(place, flip, parts, tree_refs[7 * i:7 * i + 7]))
        ends.append(partial(store_flat, outs[which], base // LANES))

    @pl.when(now == 0)
    def _():
        greet_peers(place)
        for tree in trees[:3]:
            tree.start(0)

    groups = (slice(0, 3), slice(3, 5), slice(5, 7))

    def onward(group, stage, then=None):
        for tree, end in zip(trees[groups[group]], ends[groups[group]]):
            tree.settle(stage, end)
            if stage < 3:
                tree.start(stage + 1)
        if then is not None:
            for tree in trees[groups[then]]:
                tree.start(0)

    def hook(at, act):
        @pl.when(now == at)
        def _():
            act()

    hook(2, lambda: onward(0, 0, 1))
    hook(7, lambda: (onward(0, 1), onward(1, 0, 2)))
    hook(10, lambda: onward(0, 2))
    hook(15, lambda: (onward(1, 1), onward(2, 0)))
    hook(18, lambda: onward(0, 3))
    hook(19, lambda: (onward(1, 2), onward(2, 1)))
    hook(22, lambda: onward(2, 2))

    @pl.when(step == 0)
    def _():
        extra = key_features(lane_all, seg_all_ref[...], segments).astype(BF16)
        k0[...] = jnp.where(first_all, k_ref[...], extra)
        k1[...] = jnp.where(first_all, extra, k_ref[...])
        v0[...] = jnp.where(first_all, v_ref[...], extra)
        v1[...] = jnp.where(first_all, extra, v_ref[...])
        dk_sum[...] = jnp.zeros_like(dk_sum)
        dv_sum[...] = jnp.zeros_like(dv_sum)
        sums_ref[...] = jnp.zeros_like(sums_ref)

    first, lane = feature_lanes(tile)
    hidden = query_features(lane, seg_ref[...], segments)
    queries, grads = q_ref[...], g_ref[...]
    product = grads.astype(F32) * o_ref[...].astype(F32)
    lses = lse_ref[...]
    dqs, dks, dvs = [], [], []
    for mask, keys, values, at in ((first, k0, v0, 0), (~first, k1, v1, HD)):
        lse = lses[:, at:at + 1]
        delta = jnp.sum(jnp.where(mask, product, 0.0), axis=1, keepdims=True)
        query = jnp.where(mask, queries, with_column(hidden, lane, segments, -lse).astype(BF16))
        grad = jnp.where(mask, grads, with_column(jnp.zeros_like(hidden), lane, segments, -delta).astype(BF16))
        probs = jnp.exp(dot_nt(keys[...], query))
        score = (probs * dot_nt(values[...], grad)).astype(BF16)
        dvs.append(dot_nn(probs.astype(BF16), grad))
        dks.append(dot_nn(score, query))
        dqs.append(dot_tn(score, keys[...]))
    dq = (jnp.where(first, dqs[0], dqs[1]) * 0.125).astype(BF16)
    dq_ref[...] = dq
    dk_sum[...] += jnp.where(first_all, dks[0], dks[1])
    dv_sum[...] += jnp.where(first_all, dvs[0], dvs[1])
    sums_ref[0:1, :] += jnp.sum(dq.astype(F32), axis=0, keepdims=True)

    @pl.when(step == last)
    def _():
        dk_ref[...] = dk_sum[...].astype(BF16)
        dv = dv_sum[...].astype(BF16)
        dv_ref[...] = dv
        sums_ref[1:2, :] += jnp.sum(dv.astype(F32), axis=0, keepdims=True)

    @pl.when(now == pl.num_programs(0) * pl.num_programs(1) - 1)
    def _():
        onward(1, 3)
        onward(2, 3)
        for tree in trees:
            tree.drain()


def attend_back(segments, segment_col, q, out, grad, lse, k, v, wi, wu, wo):
    count, width = q.shape
    pairs = width // LANES
    tile = count // 4
    devices = wi.shape[0]
    sizes = grid_of(devices)
    tile_spec = pl.BlockSpec((tile, LANES), lambda h, i: (i, h))
    all_spec = pl.BlockSpec((count, LANES), lambda h, i: (0, h))
    anywhere = pl.BlockSpec(memory_space=pl.ANY)
    parts = [x.reshape(sizes + x.shape[1:]) for x in (wi, wu, wo)]
    cuts, part = [], wi.shape[2] // 6
    for base, size in ((0, 2), (2, 3), (5, 1)):
        cuts.append((0, base * part, size * part, False))
        cuts.append((1, base * wu.shape[2] // 6, size * wu.shape[2] // 6, True))
        if base == 0:
            cuts.append((2, 0, wo.shape[2], False))
    trees = []
    for which, _, columns, flip in cuts:
        trees += tree_scratch(sizes, flip, (wi, wu, wo)[which].shape[1], columns)
    flats = [(x.shape[1] * x.shape[2] // LANES, LANES) for x in (wi, wu, wo)]
    return pl.pallas_call(
        partial(attend_back_kernel, segments, sizes, cuts),
        grid=(pairs, 4),
        out_shape=[jax.ShapeDtypeStruct((count, width), BF16)] * 3
        + [jax.ShapeDtypeStruct((8, width), F32)]
        + [jax.ShapeDtypeStruct(flat, F32) for flat in flats],
        in_specs=[pl.BlockSpec((tile, 1), lambda h, i: (i, 0))] + [tile_spec] * 4 + [held_spec((count, 1)), all_spec, all_spec]
        + [anywhere] * 3,
        out_specs=[tile_spec, all_spec, all_spec, pl.BlockSpec((8, LANES), lambda h, i: (0, h))]
        + [full_spec(flat) for flat in flats],
        scratch_shapes=[pltpu.VMEM((count, LANES), BF16)] * 4 + [pltpu.VMEM((count, LANES), F32)] * 2
        + trees,
        compiler_params=params(60, "arbitrary", "arbitrary", collective_id=2, has_side_effects=True),
        cost_estimate=pl.CostEstimate(flops=20 * count * count * width, bytes_accessed=16 * MIB, transcendentals=count * count * 12),
        name="attend_back",
    )(segment_col, q, out, grad, lse, segment_col, k, v, *parts)


def normalize(hidden):
    centered = hidden - jnp.mean(hidden, axis=1, keepdims=True)
    variance = jnp.mean(centered * centered, axis=1, keepdims=True)
    inverse = lax.rsqrt(variance + EPSILON)
    return centered * inverse, inverse


def normalize_back(grad, normal, inverse):
    return inverse * (
        grad
        - jnp.mean(grad, axis=1, keepdims=True)
        - normal * jnp.mean(grad * normal, axis=1, keepdims=True)
    )


def column_sum(matrix):
    return jnp.sum(matrix.astype(F32), axis=0, keepdims=True)


def feed_kernel(sizes, tiles, chunk, where_ref, place_ref, rows_hbm, att_hbm, cot_hbm, early_hbm, w4_hbm, wi_hbm, wu_hbm, vec_ref, bi_ref,
                first_ref, agrad_ref, returned_hbm, dwi_ref, dwu_ref, dwo_ref, sums_ref, bisum_ref,
                act_ref, inner_ref, slope_ref, turned_ref, outer_ref, low_ref, normal1_ref, normal2_ref, inverse1_ref, inverse2_ref,
                cot_ref, result_ref, leaving_ref, rows_ref, att_ref, wo_ref, wi_ref, wu_ref, load_sems, early_sems, swap_sems, swap_local):
    count = att_ref.shape[0]
    tile = count // tiles
    hidden_width = wi_ref.shape[1]
    devices = sizes[0] * sizes[1] * sizes[2] * sizes[3]
    step, last = pl.program_id(0), pl.num_programs(0) - 1
    vec = vec_ref[...]
    bo, ga, sa, bu, gf, sf = (vec[i:i + 1] for i in range(2, 8))
    enter = Exchange(devices, cot_hbm, cot_ref, swap_sems.at[0], swap_local.at[0], (devices // 2, devices))
    early = Exchange(devices, early_hbm, cot_ref, None, None, (1, devices // 2))
    loads = [
        pltpu.make_async_copy(source, target, load_sems.at[i])
        for i, (source, target) in enumerate((
            (att_hbm, att_ref), (w4_hbm.at[3], wo_ref), (rows_hbm, rows_ref), (wi_hbm, wi_ref), (wu_hbm, wu_ref)
        ))
    ]

    def early_block(j):
        peer = (early.me + devices - j) % devices
        return pltpu.make_async_copy(early.block(early_hbm, peer), early.block(cot_ref, peer), early_sems.at[j])

    leave = Exchange(devices, leaving_ref, returned_hbm, swap_sems.at[1], swap_local.at[1])

    @pl.when(step == 0)
    def _():
        for load in loads:
            load.start()
        greet_all(devices)
        enter.start()
        early.over(lambda j: early_block(j).start())
        sums_ref[...] = jnp.zeros_like(sums_ref)
        bisum_ref[...] = jnp.zeros_like(bisum_ref)
        for load in loads:
            load.wait()

    @pl.when(step < tiles)
    def _():
        cut = pl.ds(pl.multiple_of(step * tile, tile), tile)
        first_sum = rows_ref[cut, :].astype(F32) + dot_nn(att_ref[cut, :], wo_ref[...]) + bo
        normal1, inverse1 = normalize(first_sum)
        normal1_ref[cut, :] = normal1
        inverse1_ref[cut, :] = inverse1
        normed = normal1 * ga + sa
        normed_low = normed.astype(BF16)
        turned_ref[:, cut] = normed.T.astype(BF16)
        second = normed + bu
        for at in range(0, hidden_width, chunk):
            pre = dot_nn(normed_low, wi_ref[:, at:at + chunk]) + bi_ref[:, at:at + chunk]
            share = 0.5 + 0.5 * lax.erf(pre * 0.7071067811865476)
            act = (pre * share).astype(BF16)
            act_ref[cut, at:at + chunk] = act
            slope_ref[cut, at:at + chunk] = (share + pre * (jnp.exp(pre * pre * -0.5) * 0.3989422804014327)).astype(BF16)
            second = second + dot_nn(act, wu_ref[at:at + chunk, :])
        normal2, inverse2 = normalize(second)
        normal2_ref[cut, :] = normal2
        inverse2_ref[cut, :] = inverse2
        result_ref[cut, :] = (normal2 * gf + sf).astype(BF16)

    @pl.when(step == tiles)
    def _():
        for at in range(0, count, tile):
            target = lax.broadcasted_iota(jnp.int32, (tile, count), 0) + at
            leaving_ref[at:at + tile] = select_rows(where_ref[...] == target, result_ref)
        early.over(lambda j: early_block(j).wait())
        enter.wait()
        leave.start()

    @pl.when((step >= tiles) & (step < 2 * tiles))
    def _():
        cut = pl.ds(pl.multiple_of((step - tiles) * tile, tile), tile)
        lane = lax.broadcasted_iota(jnp.int32, (tile, count), 1)
        chosen = jnp.where(place_ref[...] == lane, 1.0, 0.0).astype(BF16)
        cot = dot_nn(chosen, cot_ref[...])
        normal1, normal2 = normal1_ref[cut, :], normal2_ref[cut, :]
        second_grad = normalize_back(cot * gf, normal2, inverse2_ref[cut, :])
        outer_low = second_grad.astype(BF16)
        outer_ref[cut, :] = outer_low
        normed_grad = second_grad
        for at in range(0, hidden_width, chunk):
            act_grad = dot_nt(outer_low, wu_ref[at:at + chunk, :])
            inner_low = (act_grad * slope_ref[cut, at:at + chunk].astype(F32)).astype(BF16)
            inner_ref[cut, at:at + chunk] = inner_low
            bisum_ref[0:1, at:at + chunk] += column_sum(inner_low)
            normed_grad = normed_grad + dot_nt(inner_low, wi_ref[:, at:at + chunk])
        first_grad = normalize_back(normed_grad * ga, normal1, inverse1_ref[cut, :])
        first_ref[...] = first_grad
        branch_low = first_grad.astype(BF16)
        low_ref[cut, :] = branch_low
        agrad_ref[...] = dot_nt(branch_low, wo_ref[...]).astype(BF16)
        sums_ref[2:3, :] += column_sum(branch_low)
        sums_ref[3:4, :] += column_sum(normed_grad * normal1)
        sums_ref[4:5, :] += column_sum(normed_grad)
        sums_ref[5:6, :] += column_sum(outer_low)
        sums_ref[6:7, :] += column_sum(cot * normal2)
        sums_ref[7:8, :] += column_sum(cot)

    @pl.when(step >= 2 * tiles)
    def _():
        cut = pl.ds(pl.multiple_of((step - 2 * tiles) * chunk, chunk), chunk)
        dwi_ref[...] = dot_nn(turned_ref[...], inner_ref[:, cut]).astype(BF16)
        dwu_ref[...] = dot_tn(act_ref[:, cut], outer_ref[...]).astype(BF16)

    @pl.when(step == last)
    def _():
        dwo_ref[...] = dot_tn(att_ref[...], low_ref[...]).astype(BF16)
        leave.wait()


def feed_forward(devices, place_row, place_col, rows, attended, leaving_cot, early_cot, w4, wi, wu, vec, bi):
    count, width = rows.shape
    hidden_width = wi.shape[1]
    tiles, chunk = 4, 512
    tile = count // tiles
    anywhere = pl.BlockSpec(memory_space=pl.ANY)
    back_spec = pl.BlockSpec((tile, width), lambda i: (jnp.clip(i - tiles, 0, tiles - 1), 0))
    parts = hidden_width // chunk

    def part(i):
        return jnp.clip(i - 2 * tiles, 0, parts - 1)

    def held(n, dtype=BF16):
        return pltpu.VMEM((count, n), dtype)

    return pl.pallas_call(
        partial(feed_kernel, grid_of(devices), tiles, chunk),
        grid=(2 * tiles + parts,),
        out_shape=[
            jax.ShapeDtypeStruct((count, width), F32), jax.ShapeDtypeStruct((count, width), BF16), jax.ShapeDtypeStruct((count, width), BF16),
            jax.ShapeDtypeStruct((width, hidden_width), BF16), jax.ShapeDtypeStruct((hidden_width, width), BF16),
            jax.ShapeDtypeStruct((width, width), BF16), jax.ShapeDtypeStruct((8, width), F32), jax.ShapeDtypeStruct((8, hidden_width), F32),
        ],
        in_specs=[
            held_spec((1, count)), pl.BlockSpec((tile, 1), lambda i: (jnp.clip(i - tiles, 0, tiles - 1), 0)),
            anywhere, anywhere, anywhere, anywhere, anywhere, anywhere, anywhere, held_spec(vec.shape), held_spec(bi.shape),
        ],
        out_specs=[
            back_spec, back_spec, anywhere,
            pl.BlockSpec((width, chunk), lambda i: (0, part(i))), pl.BlockSpec((chunk, width), lambda i: (part(i), 0)),
            full_spec((width, width)), full_spec((8, width)), full_spec((8, hidden_width)),
        ],
        scratch_shapes=[
            held(hidden_width), held(hidden_width), held(hidden_width), pltpu.VMEM((width, count), BF16), held(width), held(width),
            held(width, F32), held(width, F32), held(1, F32), held(1, F32), held(width), held(width), held(width),
            held(width), held(width), pltpu.VMEM((width, width), BF16), pltpu.VMEM(wi.shape, BF16), pltpu.VMEM(wu.shape, BF16),
            pltpu.SemaphoreType.DMA((5,)), pltpu.SemaphoreType.DMA((devices,)), pltpu.SemaphoreType.DMA((2, 2, devices)), pltpu.SemaphoreType.DMA((2,)),
        ],
        compiler_params=params(62, "arbitrary", collective_id=5, has_side_effects=True),
        cost_estimate=pl.CostEstimate(flops=20 * count * width * hidden_width, bytes_accessed=36 * MIB, transcendentals=2 * count * hidden_width),
        name="feed_forward",
    )(place_row, place_col, rows, attended, leaving_cot, early_cot, w4, wi, wu, vec, bi)


def finish_kernel(sizes, share, where_ref, rank_ref, first_hbm, dq_hbm, dk_hbm, dv_hbm, w4_hbm, rows_hbm, returned_hbm, sums_ref, more_ref, bisum_ref,
                  layer_ref, back_ref, wq_out, wk_out, wv_out, *refs):
    finish_body(sizes, share, where_ref, rank_ref, first_hbm, dq_hbm, dk_hbm, dv_hbm, w4_hbm, rows_hbm, returned_hbm, sums_ref, more_ref, bisum_ref,
                layer_ref, back_ref, wq_out, wk_out, wv_out, refs[:9], *refs[9:])


def finish_body(sizes, share, where_ref, rank_ref, first_hbm, dq_hbm, dk_hbm, dv_hbm, w4_hbm, rows_hbm, returned_hbm, sums_ref, more_ref, bisum_ref,
                  layer_ref, back_ref, wq_out, wk_out, wv_out, small_outs,
                  first_ref, dq_ref, dk_ref, dv_ref, w_ref, rows_ref, returned_ref, load_sems,
                  total_ref, leaving_ref, wq_ref, wk_ref, wv_ref, lines_ref, small_ref, swap_sems, swap_local, *tree_refs):
    count, width = total_ref.shape
    devices = sizes[0] * sizes[1] * sizes[2] * sizes[3]
    na, nb, nc, nk = sizes
    tile = count // 4
    loads = [
        pltpu.make_async_copy(source, target, load_sems.at[i])
        for i, (source, target) in enumerate((
            (first_hbm, first_ref), (dq_hbm, dq_ref), (w4_hbm.at[pl.ds(0, 3)], w_ref), (dk_hbm, dk_ref), (dv_hbm, dv_ref),
            (rows_hbm, rows_ref), (returned_hbm, returned_ref),
        ))
    ]
    for load in loads:
        load.start()
    place = Place(sizes)
    swap = Exchange(devices, leaving_ref, back_ref, swap_sems, swap_local)
    parts = (wq_ref, wk_ref, wv_ref, small_ref)
    trees = [Tree(place, flip, ref, tree_refs[7 * i:7 * i + 7]) for i, (flip, ref) in enumerate(zip((False, True, False, True), parts))]
    greet_all(devices)
    for load in loads[:5]:
        load.wait()
    for at in range(0, count, tile):
        cut = slice(at, at + tile)
        total_ref[cut] = (
            first_ref[cut] + dot_nt(dq_ref[cut], w_ref[0]) + dot_nt(dk_ref[cut], w_ref[1]) + dot_nt(dv_ref[cut], w_ref[2])
        ).astype(BF16)
    for at in range(0, count, tile):
        target = lax.broadcasted_iota(jnp.int32, (tile, count), 0) + at
        chosen = jnp.where(where_ref[...] == target, 1.0, 0.0).astype(BF16)
        leaving_ref[at:at + tile] = dot_nn(chosen, total_ref[...]).astype(BF16)
    swap.start()

    def by_device(line, share):
        count = line.shape[1]
        start = lax.broadcasted_iota(jnp.int32, (devices, count), 0) * share
        lane = lax.broadcasted_iota(jnp.int32, (devices, count), 1)
        left = jnp.where((lane >= start) & (lane < start + share), line, 0.0).astype(BF16)
        at = lax.broadcasted_iota(jnp.int32, (count, LANES), 0).astype(F32)
        inside = at - jnp.floor((at + 0.5) * (1.0 / share)) * share
        right = jnp.where(inside == lax.broadcasted_iota(jnp.int32, (count, LANES), 1).astype(F32), 1.0, 0.0).astype(BF16)
        return dot_nn(left, right)

    lines_ref[...] = jnp.zeros_like(lines_ref)
    for i in range(8):
        lines_ref[i] = by_device(sums_ref[i:i + 1, :] + more_ref[i:i + 1, :], share)
    lines_ref[8] = by_device(bisum_ref[0:1, :], bisum_ref.shape[1] // devices)
    for d in range(devices):
        index = (d // (nk * nc * nb), d // (nk * nc) % nb, d // nk % nc, d % nk)
        small_ref[index] = lines_ref[:, d, :].astype(BF16)
    trees[3].start(0)
    loads[5].wait()
    group = 3 * LANES
    for grad_ref, out_ref, tree in zip((dq_ref, dk_ref, dv_ref), parts, trees):
        for at in range(0, width, group):
            value = dot_tn(rows_ref[:, at:at + group], grad_ref[...])
            for i in range(group // share):
                d = at // share + i
                index = (d // (nk * nc * nb), d // (nk * nc) % nb, d // nk % nc, d % nk)
                out_ref[index] = value[i * share:(i + 1) * share].astype(BF16)
        tree.start(0)
    loads[6].wait()

    def restore(out_ref, from_ref):
        for at in range(0, count, tile):
            lane = lax.broadcasted_iota(jnp.int32, (tile, count), 1)
            chosen = jnp.where(rank_ref[at:at + tile] == lane, 1.0, 0.0).astype(BF16)
            out_ref[at:at + tile] = dot_nn(chosen, from_ref[...]).astype(BF16)

    for stage in range(3):
        for tree in trees:
            tree.settle(stage)
            tree.start(stage + 1)
        if stage == 0:
            restore(layer_ref, returned_ref)
    for tree, out in zip(trees, (wq_out, wk_out, wv_out)):
        tree.settle(3, partial(store_flat, out, 0))

    def store_small(value):
        for i, out in enumerate(small_outs):
            out[...] = value[i:i + 1, :out.shape[1]]

    trees[3].settle(3, store_small)
    swap.wait()
    for tree in trees:
        tree.drain()


def emit_kernel(rank_ref, back_hbm, *refs):
    count = (len(refs) - 3) // 2
    given, tokens_ref, outs, (back_ref, sems) = refs[:count], refs[count], refs[count + 1:2 * count + 1], refs[2 * count + 1:]
    load = pltpu.make_async_copy(back_hbm, back_ref, sems.at[count])
    load.start()
    copies = [pltpu.make_async_copy(source, target, sems.at[i]) for i, (source, target) in enumerate(zip(given, outs))]
    for copy in copies:
        copy.start()
    load.wait()
    rows = back_ref.shape[0]
    tile = rows // 4
    for at in range(0, rows, tile):
        lane = lax.broadcasted_iota(jnp.int32, (tile, rows), 1)
        tokens_ref[at:at + tile] = select_rows(rank_ref[at:at + tile] == lane, back_ref)
    for copy in copies:
        copy.wait()


def emit(rank_col, back, others):
    anywhere = pl.BlockSpec(memory_space=pl.ANY)
    in_vmem = pl.BlockSpec(memory_space=pltpu.VMEM)
    return pl.pallas_call(
        emit_kernel,
        out_shape=[jax.ShapeDtypeStruct(x.shape, x.dtype) for x in (back, *others)],
        in_specs=[in_vmem] + [anywhere] * (1 + len(others)),
        out_specs=[in_vmem] * (1 + len(others)),
        scratch_shapes=[pltpu.VMEM(back.shape, BF16), pltpu.SemaphoreType.DMA((len(others) + 1,))],
        compiler_params=pltpu.CompilerParams(vmem_limit_bytes=56 * MIB),
        name="emit",
    )(rank_col, back, *others)


def finish(devices, place_row, rank_col, first_grad, dq, dk, dv, w4, rows, returned, sums, more, bi_sum):
    count, width = dq.shape
    sizes = grid_of(devices)
    share = width // devices
    anywhere = pl.BlockSpec(memory_space=pl.ANY)
    in_vmem = pl.BlockSpec(memory_space=pltpu.VMEM)
    whole = pltpu.VMEM((count, width), BF16)
    trees = []
    for flip, shape in zip((False, True, False, True), ((share, width),) * 3 + ((16, LANES),)):
        trees += tree_scratch(sizes, flip, *shape)
    return pl.pallas_call(
        partial(finish_kernel, sizes, share),
        out_shape=[jax.ShapeDtypeStruct((count, width), BF16)] * 2
        + [jax.ShapeDtypeStruct((share * width // LANES, LANES), F32)] * 3
        + [jax.ShapeDtypeStruct((1, share), F32)] * 8 + [jax.ShapeDtypeStruct((1, bi_sum.shape[1] // devices), F32)],
        in_specs=[in_vmem] * 2 + [anywhere] * 7 + [in_vmem] * 3,
        out_specs=[in_vmem] * 14,
        scratch_shapes=[pltpu.VMEM((count, width), F32)] + [whole] * 3 + [pltpu.VMEM((3, width, width), BF16)] + [whole] * 2
        + [pltpu.SemaphoreType.DMA((7,))] + [whole] * 2 + [pltpu.VMEM(sizes + (share, width), BF16)] * 3
        + [pltpu.VMEM((16, devices, LANES), F32), pltpu.VMEM(sizes + (16, LANES), BF16)]
        + [pltpu.SemaphoreType.DMA((2, devices)), pltpu.SemaphoreType.DMA(())] + trees,
        compiler_params=pltpu.CompilerParams(collective_id=3, has_side_effects=True, vmem_limit_bytes=60 * MIB),
        name="finish",
    )(place_row, rank_col, first_grad, dq, dk, dv, w4, rows, returned, sums, more, bi_sum)


def on_device(tokens, cotangent, packed_slot, seq_lengths, query_weight, query_bias, key_weight, value_weight,
              value_bias, output_weight, output_bias, attention_gain, attention_shift, inner_weight, inner_bias,
              outer_weight, outer_bias, final_gain, final_shift):
    devices = lax.axis_size("fsdp")
    count, width = tokens.shape
    hidden_width = inner_bias.shape[0] * devices
    segments = seq_lengths.shape[1]
    share = width // devices
    small = (query_bias, value_bias, output_bias, attention_gain, attention_shift, outer_bias, final_gain, final_shift, inner_bias)
    arrived, leaving_cot, g4, gv, gi, place_row, place_col, rank_col, segment_col, wu_own = arrive(
        seq_lengths, packed_slot.reshape(devices, count), tokens, cotangent,
        (query_weight, key_weight, value_weight, output_weight), inner_weight, outer_weight, small,
    )
    w4 = g4.reshape(4, width, width)
    flat = gv.reshape(devices, 16, LANES).astype(F32)
    vec = flat[:, :8, :share].transpose(1, 0, 2).reshape(8, width)
    bi = flat[:, 8, :hidden_width // devices].reshape(1, hidden_width)

    attended, lse, rows, q, k, v, gu, early_cot = attend(devices, segments, place_col, arrived, w4, vec, segment_col, wu_own, leaving_cot)
    wi = gi.reshape(width, hidden_width)
    wu = gu.reshape(hidden_width, width)
    first_grad, attended_grad, returned, inner_grad, outer_grad, wo_grad, sums, bi_sum = feed_forward(
        devices, place_row, place_col, rows, attended, leaving_cot, early_cot, w4, wi, wu, vec, bi
    )
    inner_grad, outer_grad, wo_grad = (x.reshape(devices, -1, x.shape[-1]) for x in (inner_grad, outer_grad, wo_grad))
    dq, dk, dv, more, inner_grad, outer_grad, wo_grad = attend_back(
        segments, segment_col, q, attended, attended_grad, lse, k, v, inner_grad, outer_grad, wo_grad
    )
    layer_out, back, wq_grad, wk_grad, wv_grad, *small = finish(
        devices, place_row, rank_col, first_grad, dq, dk, dv, w4, rows, returned, sums, more, bi_sum
    )
    tokens_grad, layer_out, wq_grad, wk_grad, wv_grad, wo_grad, inner_grad, outer_grad, *small = emit(
        rank_col, back, (layer_out, wq_grad, wk_grad, wv_grad, wo_grad, inner_grad, outer_grad, *small)
    )
    wq_grad, wk_grad, wv_grad, wo_grad, wi_grad, wu_grad = (
        x.reshape(-1) for x in (wq_grad, wk_grad, wv_grad, wo_grad, inner_grad, outer_grad)
    )
    bq, bv, bo, ga, sa, bu, gf, sf, bi = (x.reshape(-1) for x in small)
    return (layer_out, tokens_grad, wq_grad, bq, wk_grad, wv_grad, bv, wo_grad, bo, ga, sa, wi_grad, bi, wu_grad, bu, gf, sf)


def solution(mesh):
    split, rows = P("fsdp"), P("fsdp", None)
    return jax.shard_map(
        on_device,
        mesh=mesh,
        in_specs=(rows, rows, P(), rows) + (split,) * 15,
        out_specs=(rows, rows) + (split,) * 15,
        check_vma=False,
    )
```

```python
from functools import partial

import jax
import jax.numpy as jnp
from jax import lax
from jax.experimental import pallas as pl
from jax.experimental.pallas import tpu as pltpu
from jax.sharding import PartitionSpec as P

HD = 64
LANES = 128
EPSILON = 1e-12
NEG_LARGE = -1e30
MIB = 1 << 20
F32 = jnp.float32
BF16 = jnp.bfloat16
MESH = pl.DeviceIdType.MESH


def dot_nn(a, b):
    return lax.dot_general(a, b, (((1,), (0,)), ((), ())), preferred_element_type=F32)


def dot_nt(a, b):
    return lax.dot_general(a, b, (((1,), (1,)), ((), ())), preferred_element_type=F32)


def dot_tn(a, b):
    return lax.dot_general(a, b, (((0,), (0,)), ((), ())), preferred_element_type=F32)


def full_spec(shape, **kw):
    return pl.BlockSpec(shape, lambda *_: (0,) * len(shape), **kw)


def held_spec(shape):
    return full_spec(shape, pipeline_mode=pl.Buffered(1))


def params(mib, *axes, **kw):
    return pltpu.CompilerParams(
        dimension_semantics=axes or None, vmem_limit_bytes=mib * MIB, **kw
    )


def grid_of(devices):
    return {32: (4, 2, 2, 2), 128: (4, 4, 4, 2)}.get(devices, (devices, 1, 1, 1))


class Place:
    def __init__(self, sizes):
        na, nb, nc, nk = self.sizes = sizes
        self.me = me = lax.axis_index("fsdp")
        self.k = me % nk
        self.c = (me // nk) % nc
        self.b = (me // (nk * nc)) % nb
        self.a = me // (nk * nc * nb)

    def ahead(self, axis, step):
        own = (self.a, self.b, self.c, self.k)[axis]
        return (own + step) % self.sizes[axis]

    def device(self, axis, step):
        na, nb, nc, nk = self.sizes
        where = [self.a, self.b, self.c, self.k]
        where[axis] = self.ahead(axis, step)
        return ((where[0] * nb + where[1]) * nc + where[2]) * nk + where[3]


def remote(source, target, send_sem, recv_sem, peer):
    return pltpu.make_async_remote_copy(
        src_ref=source, dst_ref=target, send_sem=send_sem, recv_sem=recv_sem,
        device_id=(peer,), device_id_type=MESH,
    )


def greet_all(devices):
    me = lax.axis_index("fsdp")
    barrier = pltpu.get_barrier_semaphore()

    def signal(j, carry):
        pl.semaphore_signal(barrier, inc=1, device_id=((me + j) % devices,), device_id_type=MESH)
        return carry

    lax.fori_loop(1, devices, signal, 0)
    pl.semaphore_wait(barrier, devices - 1)


class Exchange:
    def __init__(self, devices, source, target, sems, local_sem, turns=None):
        self.devices, self.source, self.target, self.sems, self.local_sem = devices, source, target, sems, local_sem
        self.turns = turns or (1, devices)
        self.rows = source.shape[0] // devices
        self.me = lax.axis_index("fsdp")

    def block(self, ref, device):
        return ref.at[pl.ds(pl.multiple_of(device * self.rows, self.rows), self.rows)]

    def own(self):
        return pltpu.make_async_copy(self.block(self.source, self.me), self.block(self.target, self.me), self.local_sem)

    def outgoing(self, j):
        peer = (self.me + j) % self.devices
        return remote(self.block(self.source, peer), self.block(self.target, self.me), self.sems.at[0, j], self.sems.at[1, j], peer)

    def incoming(self, j):
        peer = (self.me + self.devices - j) % self.devices
        block = self.block(self.target, peer)
        return remote(block, block, self.sems.at[0, j], self.sems.at[1, j], peer)

    def over(self, act):
        def body(j, carry):
            act((j * 13) % self.devices)
            return carry

        lax.fori_loop(*self.turns, body, 0)

    def start(self):
        self.own().start()
        self.start_remote()

    def start_remote(self):
        self.over(lambda j: self.outgoing(j).start())

    def wait(self):
        self.wait_remote()
        self.own().wait()

    def wait_remote(self):
        self.over(lambda j: self.incoming(j).wait_recv())
        self.over(lambda j: self.outgoing(j).wait_send())


def greet_peers(place):
    barrier = pltpu.get_barrier_semaphore()
    count = 0
    for axis, size in enumerate(place.sizes):
        for j in range(1, size):
            pl.semaphore_signal(barrier, inc=1, device_id=(place.device(axis, j),), device_id_type=MESH)
            count += 1
    pl.semaphore_wait(barrier, count)


def spread_scratch(sizes):
    return [pltpu.SemaphoreType.DMA((2, 4, max(sizes))), pltpu.SemaphoreType.DMA(())]


class Spread:
    def __init__(self, place, flip, own, out, scratch, lead=()):
        self.place, self.flip, self.mine, self.out, self.lead = place, flip, own, out, lead
        self.sems, self.local_sem = scratch
        self.axes = (0, 1, 2, 3) if flip else (0, 2, 1, 3)

    def region(self, stage, step=0):
        place, every = self.place, slice(None)
        where = [place.a, place.b, place.c, place.k]
        axis = self.axes[stage]
        where[axis] = place.ahead(axis, step)
        for done in self.axes[:stage]:
            where[done] = every
        return self.out.at[self.lead + tuple(where)]

    def local(self):
        return pltpu.make_async_copy(self.mine, self.region(0), self.local_sem)

    def outgoing(self, stage):
        axis = self.axes[stage]
        source = self.mine if stage == 0 else self.region(stage)
        return [
            remote(source, self.region(stage), self.sems.at[0, stage, j], self.sems.at[1, stage, j], self.place.device(axis, j))
            for j in range(1, self.place.sizes[axis])
        ]

    def start(self, stage):
        for copy in self.outgoing(stage):
            copy.start()
        if stage == 0:
            self.local().start()

    def settle(self, stage):
        axis = self.axes[stage]
        if stage == 0:
            self.local().wait()
        for j in range(1, self.place.sizes[axis]):
            block = self.region(stage, self.place.sizes[axis] - j)
            remote(block, block, self.sems.at[0, stage, j], self.sems.at[1, stage, j], self.place.device(axis, j)).wait_recv()

    def drain(self):
        for stage in range(4):
            for copy in self.outgoing(stage):
                copy.wait_send()


def store_flat(ref, base, value):
    rows, columns = value.shape
    width = ref.shape[0] // rows
    for j in range(columns // LANES):
        ref[pl.ds(base + j, rows, stride=width), :] = value[:, j * LANES:(j + 1) * LANES]


def tree_scratch(sizes, flip, rows, columns):
    na, nb, nc, nk = sizes
    one, two = (nb, nc) if flip else (nc, nb)
    shapes = [(na, nb, nc), (nk - 1, na, nb, nc), (one - 1, na, two), (two - 1, na), (na - 1,)]
    return [pltpu.VMEM(shape + (rows, columns), BF16) for shape in shapes] + [
        pltpu.SemaphoreType.DMA((2, 4, max(sizes))),
        pltpu.SemaphoreType.DMA(()),
    ]


class Tree:
    def __init__(self, place, flip, parts, scratch):
        self.place, self.flip, self.parts = place, flip, parts
        self.held, *self.landing, self.sems, self.local_sem = scratch
        order = (3, 1, 2, 0) if flip else (3, 2, 1, 0)
        self.axes = order

    def own(self):
        return pltpu.make_async_copy(self.parts.at[:, :, :, self.place.k], self.held, self.local_sem)

    def outgoing(self, stage):
        place, held = self.place, self.held
        axis = self.axes[stage]
        copies = []
        for j in range(1, place.sizes[axis]):
            other = place.ahead(axis, j)
            if stage == 0:
                source = self.parts.at[:, :, :, other]
            elif stage == 1:
                source = held.at[:, other] if self.flip else held.at[:, :, other]
            elif stage == 2:
                source = held.at[:, place.b, other] if self.flip else held.at[:, other, place.c]
            else:
                source = held.at[other, place.b, place.c]
            copies.append(
                remote(source, self.landing[stage].at[j - 1], self.sems.at[0, stage, j], self.sems.at[1, stage, j], place.device(axis, j))
            )
        return copies

    def start(self, stage):
        if stage == 0:
            self.own().start()
        for copy in self.outgoing(stage):
            copy.start()

    def settle(self, stage, out=None):
        out = out if stage == 3 else None
        place, held, landing = self.place, self.held, self.landing[stage]
        na, nb, nc, nk = place.sizes
        if stage == 0:
            self.own().wait()
        for copy in self.outgoing(stage):
            copy.wait_recv()
        count = place.sizes[self.axes[stage]] - 1

        def total(own, index):
            if count == 1 and out is None:
                return own + landing[(0,) + index]
            value = own.astype(F32)
            for j in range(count):
                value = value + landing[(j,) + index].astype(F32)
            return value

        if stage == 0:
            def add(i, carry):
                held[i] = total(held[i], (i,)).astype(BF16)
                return carry
            lax.fori_loop(0, na, add, 0)
        elif stage == 1:
            two = nc if self.flip else nb
            def add(i, carry):
                for t in range(two):
                    at = (i, place.b, t) if self.flip else (i, t, place.c)
                    held[at] = total(held[at], (i, t)).astype(BF16)
                return carry
            lax.fori_loop(0, na, add, 0)
        elif stage == 2:
            def add(i, carry):
                at = (i, place.b, place.c)
                held[at] = total(held[at], (i,)).astype(BF16)
                return carry
            lax.fori_loop(0, na, add, 0)
        else:
            out(total(held[place.a, place.b, place.c], ()))

    def drain(self):
        for stage in range(4):
            for copy in self.outgoing(stage):
                copy.wait_send()


LOW = 32
EARLY = 2


def select_rows(chosen, rows_ref):
    return dot_nn(jnp.where(chosen, 1.0, 0.0).astype(BF16), rows_ref[...]).astype(BF16)


def count_true(mask, axis):
    return jnp.sum(jnp.where(mask, 1.0, 0.0), axis=axis, keepdims=True)


def load_flat(ref, base_ref, width, store):
    total = ref.shape[0]
    base_ref[0:total, :] = ref[...].astype(F32)
    per_row = width // LANES
    for j in range(per_row):
        store(j * LANES, base_ref[pl.ds(j, total // per_row, stride=per_row), :].astype(BF16))


def block_lanes(rows, columns, share):
    lane = lax.broadcasted_iota(jnp.int32, (rows, columns), 1).astype(F32)
    inside = lane - jnp.floor((lane + 0.5) * (1.0 / share)) * share
    return inside == lax.broadcasted_iota(jnp.int32, (rows, columns), 0).astype(F32)


def line_of(blocks, share):
    devices = blocks.shape[0]
    columns = devices * share
    spread = dot_nn(blocks, jnp.where(block_lanes(LANES, columns, share), 1.0, 0.0).astype(BF16))
    start = lax.broadcasted_iota(jnp.int32, (devices, columns), 0) * share
    lane = lax.broadcasted_iota(jnp.int32, (devices, columns), 1)
    return jnp.sum(jnp.where((lane >= start) & (lane < start + share), spread, 0.0), axis=0, keepdims=True)


def split3(column):
    high = column.astype(BF16).astype(F32)
    rest = column - high
    mid = rest.astype(BF16).astype(F32)
    return high, mid, rest - mid


def feature_lanes(rows):
    lane = lax.broadcasted_iota(jnp.int32, (rows, LANES), 1)
    return lane < HD, lane & (HD - 1)


def key_features(lane, segment, segments):
    return jnp.where(lane == segment, 1.0, jnp.where((lane >= segments) & (lane < segments + 3), 1.0, 0.0))


def query_features(lane, segment, segments):
    return jnp.where((lane < segments) & (lane != segment), NEG_LARGE, 0.0)


def with_column(features, lane, start, column):
    high, mid, last = split3(column)
    features = jnp.where(lane == start, high, features)
    features = jnp.where(lane == start + 1, mid, features)
    return jnp.where(lane == start + 2, last, features)


def front_kernel(segments, sizes, cuts, lengths_ref, *refs):
    given, outs, held = refs[:18], refs[18:35], refs[35:53]
    (out_ref, lse_ref, rows_hbm, q_hbm, k_hbm, v_hbm, g4, gi, gu, cot_hbm, cot_out,
     place_row, place_col, rank_out, segment_out, vec_out, bi_out) = outs
    (leaving_ref, arrived_ref, cot_leaving, flat_ref, w4_own, wi_own, wu_own, lines_ref, vec_own, gv, blocks_ref, w_ref, rows_ref, q_ref, k_ref, v_ref,
     load_sems, save_sems, w_sem, swap_sems, swap_local, *spread_refs) = refs[53:]
    w4_refs, small_refs = held[:4], held[4:13]
    slots_ref, tokens_ref, cot_ref, wi_ref, wu_ref = held[13:]
    loads = [pltpu.make_async_copy(source, target, load_sems.at[i]) for i, (source, target) in enumerate(zip(given, held))]
    count, width = tokens_ref.shape
    devices = slots_ref.shape[0]
    peer_rows = count // devices
    share = width // devices
    tile = count // 4
    now, last = pl.program_id(0), pl.num_programs(0) - 1
    place = Place(sizes)
    me = place.me
    spreads = [
        Spread(place, False, w4_own.at[pl.ds(0, 2)], g4, spread_refs[0:2], (pl.ds(0, 2),)),
        Spread(place, True, w4_own.at[pl.ds(2, 2)], g4, spread_refs[2:4], (pl.ds(2, 2),)),
        Spread(place, True, vec_own, gv, spread_refs[4:6]),
    ]
    wide = []
    for i, (which, base, columns, flip) in enumerate(cuts):
        own, whole = ((wi_own, gi), (wu_own, gu))[which]
        cut = pl.ds(base, columns)
        wide.append(Spread(place, flip, own.at[:, cut], whole.at[:, :, :, :, :, cut], spread_refs[6 + 2 * i:8 + 2 * i]))
    swap = Exchange(devices, leaving_ref, arrived_ref, swap_sems.at[0], swap_local)
    early = Exchange(devices, cot_leaving, cot_out, swap_sems.at[1], swap_local, (1, devices // EARLY))
    w_load = pltpu.make_async_copy(g4.at[pl.ds(0, 3)], w_ref, w_sem)
    saves = [
        pltpu.make_async_copy(source, target, save_sems.at[i])
        for i, (source, target) in enumerate(((rows_ref, rows_hbm), (q_ref, q_hbm), (k_ref, k_hbm), (v_ref, v_hbm), (cot_leaving, cot_hbm)))
    ]

    def onward(group, stage):
        for spread in group:
            spread.settle(stage)
            if stage < 3:
                spread.start(stage + 1)

    def pair(i):
        return wide[2 * i:2 * i + 2]

    def begin(i):
        for spread in pair(i):
            spread.start(0)

    @pl.when(now == 0)
    def _():
        for load in loads:
            load.start()
        for load in loads[:13]:
            load.wait()
        for i, ref in enumerate(w4_refs):
            def put(at, value, i=i):
                w4_own[i, :, at:at + LANES] = value
            load_flat(ref, flat_ref, width, put)
        lines_ref[...] = jnp.zeros_like(lines_ref)
        for i, ref in enumerate(small_refs):
            lines_ref[i:i + 1, 0:ref.shape[1]] = ref[...].astype(F32)
        vec_own[...] = lines_ref[...].astype(BF16)
        greet_all(devices)
        for spread in spreads:
            spread.start(0)
        for load in loads[13:]:
            load.wait()

        cuts = [(at, slice(at, at + tile)) for at in range(0, count, tile)]
        row_at = [lax.broadcasted_iota(jnp.int32, (tile, count), 0) + at for at, _ in cuts]
        lane = lax.broadcasted_iota(jnp.int32, (tile, count), 1)
        own_row = slots_ref[pl.ds(me, 1), :]
        own_float = own_row.astype(F32)
        own_col = [jnp.sum(jnp.where(lane == row, own_float, 0.0), axis=1, keepdims=True) for row in row_at]
        rank_row = sum(count_true(col < own_float, 0) for col in own_col).astype(jnp.int32)
        for (_, cut), row in zip(cuts, row_at):
            leaving_ref[cut] = select_rows(rank_row == row, tokens_ref)
        swap.start()
        onward(spreads, 0)

        def put_inner(at, value):
            wi_own[:, at:at + LANES] = value

        def put_outer(at, value):
            wu_own[:, at:at + LANES] = value

        load_flat(wi_ref, flat_ref, wi_own.shape[1], put_inner)
        load_flat(wu_ref, flat_ref, width, put_outer)
        for (_, cut), row, col in zip(cuts, row_at, own_col):
            cot_leaving[cut] = select_rows(rank_row == row, cot_ref)
            rank_out[cut] = count_true(own_float < col, 1).astype(jnp.int32)
        saves[4].start()
        row = lax.broadcasted_iota(jnp.int32, (count, 1), 0)
        end, segment = 0, jnp.zeros((count, 1), jnp.int32)
        for i in range(lengths_ref.shape[1]):
            end = end + lengths_ref[0, i]
            segment = segment + jnp.where(row >= end, 1, 0)
        segment_out[...] = segment
        onward(spreads, 1)
        begin(0)

        high = count // LOW

        def body(s, total):
            local = slots_ref[pl.ds(s, 1), :] - me * count
            in_high = lax.broadcasted_iota(jnp.int32, (high, count), 0) == (local >> 5)
            in_low = lax.broadcasted_iota(jnp.int32, (LOW, count), 0) == (local & (LOW - 1))
            weight = jnp.where(in_high, s.astype(F32), 0.0).astype(BF16)
            return total + dot_nt(weight, jnp.where(in_low, 1.0, 0.0).astype(BF16))

        source = lax.fori_loop(0, devices, body, jnp.zeros((high, LOW), F32)).astype(BF16)
        over = lax.broadcasted_iota(jnp.int32, (high, count), 1)
        picked = dot_tn(source, jnp.where((over >> 5) == lax.broadcasted_iota(jnp.int32, (high, count), 0), 1.0, 0.0).astype(BF16))
        low_row = lax.broadcasted_iota(jnp.int32, (LOW, count), 0)
        low_wide = lax.broadcasted_iota(jnp.int32, (LOW, count), 1) & (LOW - 1)
        source_row = jnp.sum(jnp.where(low_row == low_wide, picked, 0.0), axis=0, keepdims=True)
        onward(spreads, 2)
        places = source_row * peer_rows
        for (_, cut), row in zip(cuts, row_at):
            source_col = jnp.sum(jnp.where(lane == row, source_row, 0.0), axis=1, keepdims=True)
            same = source_col == source_row
            place_col[cut] = (source_col * peer_rows + count_true(same & (lane < row), 1)).astype(jnp.int32)
            places = places + count_true(same & (row < lane), 0)
        place_row[...] = places.astype(jnp.int32)
        onward(spreads, 3)
        w_load.start()
        for i, line in enumerate(small_refs):
            for d in range(devices):
                nk, nc, nb = sizes[3], sizes[2], sizes[1]
                blocks_ref[d:d + 1, :] = gv[d // (nk * nc * nb), d // (nk * nc) % nb, d // nk % nc, d % nk].astype(F32)[i:i + 1, :]
            value = line_of(blocks_ref[...].astype(BF16), line.shape[1])
            if i < 8:
                vec_out[i:i + 1, :] = value
            else:
                bi_out[...] = value
        w_load.wait()
        onward(pair(0), 0)
        begin(1)
        swap.wait()
        vec = vec_out[...]
        wq, wk, wv = (w_ref[i].astype(F32).reshape(width, width).astype(BF16) for i in range(3))
        for at, cut in cuts:
            rows = select_rows(place_col[cut] == lane, arrived_ref)
            rows_ref[cut] = rows
            q_ref[cut] = ((dot_nn(rows, wq) + vec[0:1]).astype(BF16).astype(F32) * 0.125).astype(BF16)
            k_ref[cut] = dot_nn(rows, wk).astype(BF16)
            v_ref[cut] = (dot_nn(rows, wv) + vec[1:2]).astype(BF16)
        for save in saves[:4]:
            save.start()

    columns = pl.ds(pl.multiple_of(jnp.maximum(now - 1, 0) * LANES, LANES), LANES)
    first, feature = feature_lanes(count)

    def head(mask):
        seg = segment_out[...]
        keys = jnp.where(mask, k_ref[:, columns], key_features(feature, seg, segments).astype(BF16))
        query = jnp.where(mask, q_ref[:, columns], query_features(feature, seg, segments).astype(BF16))
        scores = dot_nt(query, keys)
        top = jnp.max(scores, axis=1, keepdims=True)
        raised = jnp.exp(scores - top)
        total = jnp.sum(raised, axis=1, keepdims=True)
        return dot_nn(raised.astype(BF16), v_ref[:, columns]) * (1.0 / total), top + jnp.log(total)

    def hook(at, act):
        @pl.when(now == at)
        def _():
            act()

    @pl.when(now > 0)
    def _():
        out0, log0 = head(first)
        out1, log1 = head(~first)
        out_ref[...] = jnp.where(first, out0, out1).astype(BF16)
        lse_ref[...] = jnp.where(first, log0, log1)

    hook(0, lambda: (onward(pair(0), 1), begin(2)))
    hook(1, lambda: (onward(pair(1), 0), early.start_remote()))
    hook(2, lambda: onward(pair(2), 0))
    hook(3, lambda: (onward(pair(0), 2), onward(pair(1), 1)))
    hook(4, lambda: onward(pair(2), 1))
    hook(5, lambda: onward(pair(1), 2))

    @pl.when(now == last)
    def _():
        onward(pair(0), 3)
        onward(pair(2), 2)
        onward(pair(1), 3)
        onward(pair(2), 3)
        for spread in spreads + wide:
            spread.drain()
        early.wait_remote()
        for save in saves:
            save.wait()


def front(segments, seq_lengths, packed_slot, tokens, cotangent, w4, wi, wu, small):
    devices, count = packed_slot.shape
    width = tokens.shape[1]
    hidden_width = small[-1].shape[0] * devices
    sizes = grid_of(devices)
    share = width // devices
    pairs = width // LANES
    anywhere = pl.BlockSpec(memory_space=pl.ANY)
    pair_spec = pl.BlockSpec((count, LANES), lambda i: (0, jnp.maximum(i - 1, 0)))

    def shape(*dims, dtype=BF16):
        return jax.ShapeDtypeStruct(dims, dtype)

    def held(*dims, dtype=BF16):
        return pltpu.VMEM(dims, dtype)

    part = width // 6
    cuts = [(0, 0, hidden_width // 2, False), (0, hidden_width // 2, hidden_width // 2, True),
            (1, 0, 2 * part, False), (1, 2 * part, 2 * part, True), (1, 4 * part, part, False), (1, 5 * part, part, True)]
    flat = [w.reshape(-1, LANES) for w in w4]
    given = flat + [x.reshape(1, -1) for x in small] + [packed_slot, tokens, cotangent, wi.reshape(-1, LANES), wu.reshape(-1, LANES)]
    whole = shape(count, width)
    lines = [shape(1, count, dtype=jnp.int32)] + [shape(count, 1, dtype=jnp.int32)] * 3 + [shape(8, width, dtype=F32), shape(1, hidden_width, dtype=F32)]
    return pl.pallas_call(
        partial(front_kernel, segments, sizes, cuts),
        grid=(1 + pairs,),
        out_shape=[whole, shape(count, width, dtype=F32)] + [whole] * 4
        + [shape(4, *sizes, share, width), shape(*sizes, share, hidden_width), shape(*sizes, hidden_width // devices, width), whole, whole] + lines,
        in_specs=[pl.BlockSpec(memory_space=pltpu.SMEM)] + [anywhere] * len(given),
        out_specs=[pair_spec, pair_spec] + [anywhere] * 9 + [full_spec(x.shape) for x in lines],
        scratch_shapes=[pltpu.VMEM(x.shape, x.dtype) for x in given]
        + [held(count, width)] * 3 + [held(*given[-1].shape, dtype=F32), held(4, share, width), held(share, hidden_width),
           held(hidden_width // devices, width), held(16, LANES, dtype=F32), held(16, LANES), held(*sizes, 16, LANES), held(devices, LANES, dtype=F32),
           held(3, *sizes, share, width)] + [held(count, width)] * 4
        + [pltpu.SemaphoreType.DMA((len(given),)), pltpu.SemaphoreType.DMA((5,)), pltpu.SemaphoreType.DMA(()),
           pltpu.SemaphoreType.DMA((2, 2, devices)), pltpu.SemaphoreType.DMA(())] + spread_scratch(sizes) * (3 + len(cuts)),
        compiler_params=params(60, "arbitrary", collective_id=1, has_side_effects=True),
        cost_estimate=pl.CostEstimate(flops=16 * count * count * width, bytes_accessed=30 * MIB, transcendentals=count * count * 12),
        name="front",
    )(seq_lengths, *given)


def normalize(hidden):
    centered = hidden - jnp.mean(hidden, axis=1, keepdims=True)
    variance = jnp.mean(centered * centered, axis=1, keepdims=True)
    inverse = lax.rsqrt(variance + EPSILON)
    return centered * inverse, inverse


def normalize_back(grad, normal, inverse):
    return inverse * (
        grad
        - jnp.mean(grad, axis=1, keepdims=True)
        - normal * jnp.mean(grad * normal, axis=1, keepdims=True)
    )


def column_sum(matrix):
    return jnp.sum(matrix.astype(F32), axis=0, keepdims=True)


def feed_kernel(sizes, tiles, chunk, where_ref, place_ref, rows_hbm, att_hbm, cot_hbm, early_hbm, w4_hbm, wi_hbm, wu_hbm, vec_ref, bi_ref,
                first_ref, agrad_ref, returned_hbm, dwi_ref, dwu_ref, dwo_ref, sums_ref, bisum_ref,
                act_ref, inner_ref, slope_ref, turned_ref, outer_ref, low_ref, normal1_ref, normal2_ref, inverse1_ref, inverse2_ref,
                cot_ref, result_ref, leaving_ref, rows_ref, att_ref, wo_ref, wi_ref, wu_ref, load_sems, early_sems, swap_sems, swap_local):
    count = att_ref.shape[0]
    tile = count // tiles
    hidden_width = wi_ref.shape[1]
    devices = sizes[0] * sizes[1] * sizes[2] * sizes[3]
    step, last = pl.program_id(0), pl.num_programs(0) - 1
    vec = vec_ref[...]
    bo, ga, sa, bu, gf, sf = (vec[i:i + 1] for i in range(2, 8))
    enter = Exchange(devices, cot_hbm, cot_ref, swap_sems.at[0], swap_local.at[0], (devices // EARLY, devices))
    early = Exchange(devices, early_hbm, cot_ref, None, None, (1, devices // EARLY))
    loads = [
        pltpu.make_async_copy(source, target, load_sems.at[i])
        for i, (source, target) in enumerate((
            (att_hbm, att_ref), (w4_hbm.at[3], wo_ref), (rows_hbm, rows_ref), (wi_hbm, wi_ref), (wu_hbm, wu_ref)
        ))
    ]

    def early_block(j):
        peer = (early.me + devices - j) % devices
        return pltpu.make_async_copy(early.block(early_hbm, peer), early.block(cot_ref, peer), early_sems.at[j])

    leave = Exchange(devices, leaving_ref, returned_hbm, swap_sems.at[1], swap_local.at[1])

    @pl.when(step == 0)
    def _():
        for load in loads:
            load.start()
        greet_all(devices)
        enter.start()
        early.over(lambda j: early_block(j).start())
        sums_ref[...] = jnp.zeros_like(sums_ref)
        bisum_ref[...] = jnp.zeros_like(bisum_ref)
        for load in loads:
            load.wait()

    @pl.when(step < tiles)
    def _():
        cut = pl.ds(pl.multiple_of(step * tile, tile), tile)
        first_sum = rows_ref[cut, :].astype(F32) + dot_nn(att_ref[cut, :], wo_ref[...]) + bo
        normal1, inverse1 = normalize(first_sum)
        normal1_ref[cut, :] = normal1
        inverse1_ref[cut, :] = inverse1
        normed = normal1 * ga + sa
        normed_low = normed.astype(BF16)
        turned_ref[:, cut] = normed.T.astype(BF16)
        second = normed + bu
        for at in range(0, hidden_width, chunk):
            pre = dot_nn(normed_low, wi_ref[:, at:at + chunk]) + bi_ref[:, at:at + chunk]
            share = 0.5 + 0.5 * lax.erf(pre * 0.7071067811865476)
            act = (pre * share).astype(BF16)
            act_ref[cut, at:at + chunk] = act
            slope_ref[cut, at:at + chunk] = (share + pre * (jnp.exp(pre * pre * -0.5) * 0.3989422804014327)).astype(BF16)
            second = second + dot_nn(act, wu_ref[at:at + chunk, :])
        normal2, inverse2 = normalize(second)
        normal2_ref[cut, :] = normal2
        inverse2_ref[cut, :] = inverse2
        result_ref[cut, :] = (normal2 * gf + sf).astype(BF16)

    @pl.when(step == tiles)
    def _():
        for at in range(0, count, tile):
            target = lax.broadcasted_iota(jnp.int32, (tile, count), 0) + at
            leaving_ref[at:at + tile] = select_rows(where_ref[...] == target, result_ref)
        early.over(lambda j: early_block(j).wait())
        enter.wait()
        leave.start()

    @pl.when((step >= tiles) & (step < 2 * tiles))
    def _():
        cut = pl.ds(pl.multiple_of((step - tiles) * tile, tile), tile)
        lane = lax.broadcasted_iota(jnp.int32, (tile, count), 1)
        chosen = jnp.where(place_ref[...] == lane, 1.0, 0.0).astype(BF16)
        cot = dot_nn(chosen, cot_ref[...])
        normal1, normal2 = normal1_ref[cut, :], normal2_ref[cut, :]
        second_grad = normalize_back(cot * gf, normal2, inverse2_ref[cut, :])
        outer_low = second_grad.astype(BF16)
        outer_ref[cut, :] = outer_low
        normed_grad = second_grad
        for at in range(0, hidden_width, chunk):
            act_grad = dot_nt(outer_low, wu_ref[at:at + chunk, :])
            inner_low = (act_grad * slope_ref[cut, at:at + chunk].astype(F32)).astype(BF16)
            inner_ref[cut, at:at + chunk] = inner_low
            bisum_ref[0:1, at:at + chunk] += column_sum(inner_low)
            normed_grad = normed_grad + dot_nt(inner_low, wi_ref[:, at:at + chunk])
        first_grad = normalize_back(normed_grad * ga, normal1, inverse1_ref[cut, :])
        first_ref[...] = first_grad
        branch_low = first_grad.astype(BF16)
        low_ref[cut, :] = branch_low
        agrad_ref[...] = dot_nt(branch_low, wo_ref[...]).astype(BF16)
        sums_ref[2:3, :] += column_sum(branch_low)
        sums_ref[3:4, :] += column_sum(normed_grad * normal1)
        sums_ref[4:5, :] += column_sum(normed_grad)
        sums_ref[5:6, :] += column_sum(outer_low)
        sums_ref[6:7, :] += column_sum(cot * normal2)
        sums_ref[7:8, :] += column_sum(cot)

    @pl.when(step >= 2 * tiles)
    def _():
        cut = pl.ds(pl.multiple_of((step - 2 * tiles) * chunk, chunk), chunk)
        dwi_ref[...] = dot_nn(turned_ref[...], inner_ref[:, cut]).astype(BF16)
        dwu_ref[...] = dot_tn(act_ref[:, cut], outer_ref[...]).astype(BF16)

    @pl.when(step == last)
    def _():
        dwo_ref[...] = dot_tn(att_ref[...], low_ref[...]).astype(BF16)
        leave.wait()


def feed_forward(devices, place_row, place_col, rows, attended, leaving_cot, early_cot, w4, wi, wu, vec, bi):
    count, width = rows.shape
    hidden_width = wi.shape[1]
    tiles, chunk = 4, 768
    tile = count // tiles
    anywhere = pl.BlockSpec(memory_space=pl.ANY)
    back_spec = pl.BlockSpec((tile, width), lambda i: (jnp.clip(i - tiles, 0, tiles - 1), 0))
    parts = hidden_width // chunk

    def part(i):
        return jnp.clip(i - 2 * tiles, 0, parts - 1)

    def held(n, dtype=BF16):
        return pltpu.VMEM((count, n), dtype)

    return pl.pallas_call(
        partial(feed_kernel, grid_of(devices), tiles, chunk),
        grid=(2 * tiles + parts,),
        out_shape=[
            jax.ShapeDtypeStruct((count, width), F32), jax.ShapeDtypeStruct((count, width), BF16), jax.ShapeDtypeStruct((count, width), BF16),
            jax.ShapeDtypeStruct((width, hidden_width), BF16), jax.ShapeDtypeStruct((hidden_width, width), BF16),
            jax.ShapeDtypeStruct((width, width), BF16), jax.ShapeDtypeStruct((8, width), F32), jax.ShapeDtypeStruct((8, hidden_width), F32),
        ],
        in_specs=[
            held_spec((1, count)), pl.BlockSpec((tile, 1), lambda i: (jnp.clip(i - tiles, 0, tiles - 1), 0)),
            anywhere, anywhere, anywhere, anywhere, anywhere, anywhere, anywhere, held_spec(vec.shape), held_spec(bi.shape),
        ],
        out_specs=[
            back_spec, back_spec, anywhere,
            pl.BlockSpec((width, chunk), lambda i: (0, part(i))), pl.BlockSpec((chunk, width), lambda i: (part(i), 0)),
            full_spec((width, width)), full_spec((8, width)), full_spec((8, hidden_width)),
        ],
        scratch_shapes=[
            held(hidden_width), held(hidden_width), held(hidden_width), pltpu.VMEM((width, count), BF16), held(width), held(width),
            held(width, F32), held(width, F32), held(1, F32), held(1, F32), held(width), held(width), held(width),
            held(width), held(width), pltpu.VMEM((width, width), BF16), pltpu.VMEM(wi.shape, BF16), pltpu.VMEM(wu.shape, BF16),
            pltpu.SemaphoreType.DMA((5,)), pltpu.SemaphoreType.DMA((devices,)), pltpu.SemaphoreType.DMA((2, 2, devices)), pltpu.SemaphoreType.DMA((2,)),
        ],
        compiler_params=params(62, "arbitrary", collective_id=5, has_side_effects=True),
        cost_estimate=pl.CostEstimate(flops=20 * count * width * hidden_width, bytes_accessed=36 * MIB, transcendentals=2 * count * hidden_width),
        name="feed_forward",
    )(place_row, place_col, rows, attended, leaving_cot, early_cot, w4, wi, wu, vec, bi)


def by_device(line, devices, share):
    count = line.shape[1]
    start = lax.broadcasted_iota(jnp.int32, (devices, count), 0) * share
    lane = lax.broadcasted_iota(jnp.int32, (devices, count), 1)
    left = jnp.where((lane >= start) & (lane < start + share), line, 0.0).astype(BF16)
    return dot_nt(left, jnp.where(block_lanes(LANES, count, share), 1.0, 0.0).astype(BF16))


def back_kernel(segments, sizes, share, cuts, seg_ref, where_ref, q_ref, o_ref, g_ref, lse_ref, k_ref, v_ref, sums_ref, bisum_ref,
                wi_ref, wu_ref, wo_ref, first_hbm, w4_hbm, rows_hbm, *refs):
    back_ref, wi_out, wu_out, wo_out, wq_out, wk_out, wv_out, *small_outs = refs[:16]
    (dq_ref, dk_ref, dv_ref, first_ref, w_ref, rows_ref, load_sems, total_ref, leaving_ref, wq_part, wk_part, wv_part,
     lines_ref, small_part, swap_sems, swap_local, *tree_refs) = refs[16:]
    count, width = total_ref.shape
    na, nb, nc, nk = sizes
    devices = na * nb * nc * nk
    tile = count // 4
    now, last = pl.program_id(0), pl.num_programs(0) - 1
    place = Place(sizes)
    loads = [
        pltpu.make_async_copy(source, target, load_sems.at[i])
        for i, (source, target) in enumerate(((first_hbm, first_ref), (w4_hbm.at[pl.ds(0, 3)], w_ref), (rows_hbm, rows_ref)))
    ]
    swap = Exchange(devices, leaving_ref, back_ref, swap_sems, swap_local)
    outs = {0: wi_out, 1: wu_out, 2: wo_out}
    every = (slice(None),) * 5
    trees, ends = [], []
    for i, (which, base, columns, flip) in enumerate(cuts):
        parts = (wi_ref, wu_ref, wo_ref)[which].at[every + (pl.ds(base, columns),)]
        trees.append(Tree(place, flip, parts, tree_refs[7 * i:7 * i + 7]))
        ends.append(partial(store_flat, outs[which], base // LANES))
    late_parts = (wq_part, wk_part, wv_part, small_part)
    late = [
        Tree(place, i % 2 == 1, part, tree_refs[7 * (len(cuts) + i):7 * (len(cuts) + i) + 7])
        for i, part in enumerate(late_parts)
    ]

    @pl.when(now == 0)
    def _():
        greet_all(devices)
        for tree in trees[:3]:
            tree.start(0)
        for load in loads:
            load.start()

    groups = (slice(0, 3), slice(3, 5), slice(5, 7), slice(7, 9))

    def onward(group, stage, then=None):
        for tree, end in zip(trees[groups[group]], ends[groups[group]]):
            tree.settle(stage, end)
            if stage < 3:
                tree.start(stage + 1)
        if then is not None:
            for tree in trees[groups[then]]:
                tree.start(0)

    def hook(at, act):
        @pl.when(now == at)
        def _():
            act()

    first, lane = feature_lanes(count)
    columns = pl.ds(pl.multiple_of(now * LANES, LANES), LANES)

    def head(mask, at):
        seg, grads = seg_ref[...], g_ref[...]
        ones = key_features(lane, seg, segments).astype(BF16)
        keys = jnp.where(mask, k_ref[...], ones)
        values = jnp.where(mask, v_ref[...], ones)
        lse = lse_ref[:, at:at + 1]
        product = grads.astype(F32) * o_ref[...].astype(F32)
        delta = jnp.sum(jnp.where(mask, product, 0.0), axis=1, keepdims=True)
        hidden = query_features(lane, seg, segments)
        query = jnp.where(mask, q_ref[...], with_column(hidden, lane, segments, -lse).astype(BF16))
        grad = jnp.where(mask, grads, with_column(jnp.zeros_like(hidden), lane, segments, -delta).astype(BF16))
        dqs, dk, dv = [], 0.0, 0.0
        for top in range(0, count, count // PARTS):
            cut = slice(top, top + count // PARTS)
            probs = jnp.exp(dot_nt(keys, query[cut]))
            score = (probs * dot_nt(values, grad[cut])).astype(BF16)
            dv = dv + dot_nn(probs.astype(BF16), grad[cut])
            dk = dk + dot_nn(score, query[cut])
            dqs.append(dot_tn(score, keys))
        return (jnp.concatenate(dqs) * 0.125).astype(BF16), dk.astype(BF16), dv.astype(BF16)

    for ref, value in zip((dq_ref, dk_ref, dv_ref), head(first, 0)):
        ref[:, columns] = value

    hook(0, lambda: onward(0, 0, 1))
    hook(3, lambda: onward(0, 2))
    hook(4, lambda: (onward(1, 1), onward(2, 0, 3)))
    hook(5, lambda: (onward(1, 2), onward(2, 1), onward(3, 0)))

    for ref, value in zip((dq_ref, dk_ref, dv_ref), head(~first, HD)):
        ref[:, columns] = jnp.where(first, ref[:, columns], value)

    hook(1, lambda: (onward(0, 1), onward(1, 0, 2)))

    @pl.when(now == last)
    def _():
        for load in loads:
            load.wait()
        for at in range(0, count, tile):
            cut = slice(at, at + tile)
            total_ref[cut] = (
                first_ref[cut] + dot_nt(dq_ref[cut], w_ref[0]) + dot_nt(dk_ref[cut], w_ref[1]) + dot_nt(dv_ref[cut], w_ref[2])
            ).astype(BF16)
        onward(2, 2)
        onward(3, 1)
        for at in range(0, count, tile):
            target = lax.broadcasted_iota(jnp.int32, (tile, count), 0) + at
            leaving_ref[at:at + tile] = select_rows(where_ref[...] == target, total_ref)
        onward(0, 3)
        onward(3, 2)
        group = 3 * LANES
        for grad_ref, part, tree in zip((dq_ref, dk_ref, dv_ref), late_parts, late):
            for at in range(0, width, group):
                value = dot_tn(rows_ref[:, at:at + group], grad_ref[...])
                for i in range(group // share):
                    d = at // share + i
                    index = (d // (nk * nc * nb), d // (nk * nc) % nb, d // nk % nc, d % nk)
                    part[index] = value[i * share:(i + 1) * share].astype(BF16)
            tree.start(0)
        onward(1, 3)
        onward(2, 3)
        lines_ref[...] = jnp.zeros_like(lines_ref)
        lines_ref[0] = by_device(column_sum(dq_ref[...]), devices, share)
        lines_ref[1] = by_device(column_sum(dv_ref[...]), devices, share)
        for i in range(2, 8):
            lines_ref[i] = by_device(sums_ref[i:i + 1, :], devices, share)
        lines_ref[8] = by_device(bisum_ref[0:1, :], devices, bisum_ref.shape[1] // devices)
        for d in range(devices):
            index = (d // (nk * nc * nb), d // (nk * nc) % nb, d // nk % nc, d % nk)
            small_part[index] = lines_ref[:, d, :].astype(BF16)
        late[3].start(0)
        onward(3, 3)
        swap.start()
        for stage in range(3):
            for tree in late:
                tree.settle(stage)
                tree.start(stage + 1)
        for tree, out in zip(late, (wq_out, wk_out, wv_out)):
            tree.settle(3, partial(store_flat, out, 0))

        def store_small(value):
            for i, out in enumerate(small_outs):
                out[...] = value[i:i + 1, :out.shape[1]]

        late[3].settle(3, store_small)
        swap.wait()
        for tree in trees + late:
            tree.drain()


PARTS = 1


def backward(segments, segment_col, place_row, q, out, grad, lse, k, v, sums, bi_sum, wi, wu, wo, first_grad, w4, rows):
    count, width = q.shape
    pairs = width // LANES
    devices = wi.shape[0]
    share = width // devices
    sizes = grid_of(devices)
    pair_spec = pl.BlockSpec((count, LANES), lambda h: (0, h))
    anywhere = pl.BlockSpec(memory_space=pl.ANY)
    parts = [x.reshape(sizes + x.shape[1:]) for x in (wi, wu, wo)]
    cuts = []
    for base, size in ((0, 2), (2, 2), (4, 1), (5, 1)):
        for which, x in ((0, wi), (1, wu)):
            cuts.append((which, base * x.shape[2] // 6, size * x.shape[2] // 6, which == 1))
        if base == 0:
            cuts.append((2, 0, wo.shape[2], False))
    trees = []
    for which, _, columns, flip in cuts:
        trees += tree_scratch(sizes, flip, (wi, wu, wo)[which].shape[1], columns)
    for i, shape in enumerate(((share, width),) * 3 + ((16, LANES),)):
        trees += tree_scratch(sizes, i % 2 == 1, *shape)
    flats = [(x.shape[1] * x.shape[2] // LANES, LANES) for x in (wi, wu, wo)] + [(share * width // LANES, LANES)] * 3
    flats += [(1, share)] * 8 + [(1, bi_sum.shape[1] // devices)]
    whole = pltpu.VMEM((count, width), BF16)
    return pl.pallas_call(
        partial(back_kernel, segments, sizes, share, cuts),
        grid=(pairs,),
        out_shape=[jax.ShapeDtypeStruct((count, width), BF16)] + [jax.ShapeDtypeStruct(flat, F32) for flat in flats],
        in_specs=[held_spec((count, 1)), held_spec((1, count))] + [pair_spec] * 6 + [held_spec(sums.shape), held_spec(bi_sum.shape)]
        + [anywhere] * 6,
        out_specs=[anywhere] + [full_spec(flat) for flat in flats],
        scratch_shapes=[whole] * 3 + [pltpu.VMEM((count, width), F32), pltpu.VMEM((3, width, width), BF16), whole, pltpu.SemaphoreType.DMA((3,))]
        + [whole] * 2 + [pltpu.VMEM(sizes + (share, width), BF16)] * 3
        + [pltpu.VMEM((16, devices, LANES), F32), pltpu.VMEM(sizes + (16, LANES), BF16)]
        + [pltpu.SemaphoreType.DMA((2, devices)), pltpu.SemaphoreType.DMA(())] + trees,
        compiler_params=params(63, "arbitrary", collective_id=2, has_side_effects=True),
        cost_estimate=pl.CostEstimate(flops=20 * count * count * width, bytes_accessed=16 * MIB, transcendentals=count * count * 12),
        name="backward",
    )(segment_col, place_row, q, out, grad, lse, k, v, sums, bi_sum, *parts, first_grad, w4, rows)


def emit_kernel(rank_ref, back_hbm, layer_hbm, *refs):
    count = (len(refs) - 5) // 2
    given, tokens_ref, layer_ref, outs, (back_ref, held_ref, sems) = refs[:count], refs[count], refs[count + 1], refs[count + 2:2 * count + 2], refs[2 * count + 2:]
    moved = [
        pltpu.make_async_copy(source, target, sems.at[i])
        for i, (source, target) in enumerate(zip((back_hbm, layer_hbm, *given), (back_ref, held_ref, *outs)))
    ]
    for copy in moved:
        copy.start()
    rows = back_ref.shape[0]
    tile = rows // 4
    for copy in moved[:2]:
        copy.wait()
    for at in range(0, rows, tile):
        lane = lax.broadcasted_iota(jnp.int32, (tile, rows), 1)
        chosen = rank_ref[at:at + tile] == lane
        tokens_ref[at:at + tile] = select_rows(chosen, back_ref)
        layer_ref[at:at + tile] = select_rows(chosen, held_ref)
    for copy in moved[2:]:
        copy.wait()


def emit(rank_col, back, layer, others):
    anywhere = pl.BlockSpec(memory_space=pl.ANY)
    in_vmem = pl.BlockSpec(memory_space=pltpu.VMEM)
    return pl.pallas_call(
        emit_kernel,
        out_shape=[jax.ShapeDtypeStruct(x.shape, x.dtype) for x in (back, layer, *others)],
        in_specs=[in_vmem] + [anywhere] * (2 + len(others)),
        out_specs=[in_vmem] * (2 + len(others)),
        scratch_shapes=[pltpu.VMEM(back.shape, BF16)] * 2 + [pltpu.SemaphoreType.DMA((len(others) + 2,))],
        compiler_params=pltpu.CompilerParams(vmem_limit_bytes=56 * MIB),
        name="emit",
    )(rank_col, back, layer, *others)


def on_device(tokens, cotangent, packed_slot, seq_lengths, query_weight, query_bias, key_weight, value_weight,
              value_bias, output_weight, output_bias, attention_gain, attention_shift, inner_weight, inner_bias,
              outer_weight, outer_bias, final_gain, final_shift):
    devices = lax.axis_size("fsdp")
    count, width = tokens.shape
    hidden_width = inner_bias.shape[0] * devices
    segments = seq_lengths.shape[1]
    share = width // devices
    small = (query_bias, value_bias, output_bias, attention_gain, attention_shift, outer_bias, final_gain, final_shift, inner_bias)
    (attended, lse, rows, q, k, v, g4, gi, gu, leaving_cot, early_cot, place_row, place_col, rank_col, segment_col, vec, bi) = front(
        segments, seq_lengths, packed_slot.reshape(devices, count), tokens, cotangent,
        (query_weight, key_weight, value_weight, output_weight), inner_weight, outer_weight, small,
    )
    w4 = g4.reshape(4, width, width)
    wi = gi.reshape(width, hidden_width)
    wu = gu.reshape(hidden_width, width)
    first_grad, attended_grad, returned, inner_grad, outer_grad, wo_grad, sums, bi_sum = feed_forward(
        devices, place_row, place_col, rows, attended, leaving_cot, early_cot, w4, wi, wu, vec, bi
    )
    inner_grad, outer_grad, wo_grad = (x.reshape(devices, -1, x.shape[-1]) for x in (inner_grad, outer_grad, wo_grad))
    back, inner_grad, outer_grad, wo_grad, wq_grad, wk_grad, wv_grad, *small = backward(
        segments, segment_col, place_row, q, attended, attended_grad, lse, k, v, sums, bi_sum,
        inner_grad, outer_grad, wo_grad, first_grad, w4, rows,
    )
    tokens_grad, layer_out, wq_grad, wk_grad, wv_grad, wo_grad, inner_grad, outer_grad, *small = emit(
        rank_col, back, returned, (wq_grad, wk_grad, wv_grad, wo_grad, inner_grad, outer_grad, *small)
    )
    wq_grad, wk_grad, wv_grad, wo_grad, wi_grad, wu_grad = (
        x.reshape(-1) for x in (wq_grad, wk_grad, wv_grad, wo_grad, inner_grad, outer_grad)
    )
    bq, bv, bo, ga, sa, bu, gf, sf, bi = (x.reshape(-1) for x in small)
    return (layer_out, tokens_grad, wq_grad, bq, wk_grad, wv_grad, bv, wo_grad, bo, ga, sa, wi_grad, bi, wu_grad, bu, gf, sf)


def solution(mesh):
    split, rows = P("fsdp"), P("fsdp", None)
    return jax.shard_map(
        on_device,
        mesh=mesh,
        in_specs=(rows, rows, P(), rows) + (split,) * 15,
        out_specs=(rows, rows) + (split,) * 15,
        check_vma=False,
    )
```

```python
from functools import partial

import jax
import jax.numpy as jnp
from jax import lax
from jax.experimental import pallas as pl
from jax.experimental.pallas import tpu as pltpu
from jax.sharding import PartitionSpec as P

HD = 64
LANES = 128
EPSILON = 1e-12
NEG_LARGE = -1e30
MIB = 1 << 20
F32 = jnp.float32
BF16 = jnp.bfloat16
MESH = pl.DeviceIdType.MESH


def dot_nn(a, b):
    return lax.dot_general(a, b, (((1,), (0,)), ((), ())), preferred_element_type=F32)


def dot_nt(a, b):
    return lax.dot_general(a, b, (((1,), (1,)), ((), ())), preferred_element_type=F32)


def dot_tn(a, b):
    return lax.dot_general(a, b, (((0,), (0,)), ((), ())), preferred_element_type=F32)


def full_spec(shape, **kw):
    return pl.BlockSpec(shape, lambda *_: (0,) * len(shape), **kw)


def held_spec(shape):
    return full_spec(shape, pipeline_mode=pl.Buffered(1))


def params(mib, *axes, **kw):
    return pltpu.CompilerParams(
        dimension_semantics=axes or None, vmem_limit_bytes=mib * MIB, **kw
    )


def grid_of(devices):
    return {32: (4, 2, 2, 2), 128: (4, 4, 4, 2)}.get(devices, (devices, 1, 1, 1))


class Place:
    def __init__(self, sizes):
        na, nb, nc, nk = self.sizes = sizes
        self.me = me = lax.axis_index("fsdp")
        self.k = me % nk
        self.c = (me // nk) % nc
        self.b = (me // (nk * nc)) % nb
        self.a = me // (nk * nc * nb)

    def ahead(self, axis, step):
        own = (self.a, self.b, self.c, self.k)[axis]
        return (own + step) % self.sizes[axis]

    def device(self, axis, step):
        na, nb, nc, nk = self.sizes
        where = [self.a, self.b, self.c, self.k]
        where[axis] = self.ahead(axis, step)
        return ((where[0] * nb + where[1]) * nc + where[2]) * nk + where[3]


def remote(source, target, send_sem, recv_sem, peer):
    return pltpu.make_async_remote_copy(
        src_ref=source, dst_ref=target, send_sem=send_sem, recv_sem=recv_sem,
        device_id=(peer,), device_id_type=MESH,
    )


def greet_all(devices):
    me = lax.axis_index("fsdp")
    barrier = pltpu.get_barrier_semaphore()

    def signal(j, carry):
        pl.semaphore_signal(barrier, inc=1, device_id=((me + j) % devices,), device_id_type=MESH)
        return carry

    lax.fori_loop(1, devices, signal, 0)
    pl.semaphore_wait(barrier, devices - 1)


class Exchange:
    def __init__(self, devices, source, target, sems, local_sem, turns=None):
        self.devices, self.source, self.target, self.sems, self.local_sem = devices, source, target, sems, local_sem
        self.turns = turns or (1, devices)
        self.rows = source.shape[0] // devices
        self.me = lax.axis_index("fsdp")

    def block(self, ref, device):
        return ref.at[pl.ds(pl.multiple_of(device * self.rows, self.rows), self.rows)]

    def own(self):
        return pltpu.make_async_copy(self.block(self.source, self.me), self.block(self.target, self.me), self.local_sem)

    def outgoing(self, j):
        peer = (self.me + j) % self.devices
        return remote(self.block(self.source, peer), self.block(self.target, self.me), self.sems.at[0, j], self.sems.at[1, j], peer)

    def incoming(self, j):
        peer = (self.me + self.devices - j) % self.devices
        block = self.block(self.target, peer)
        return remote(block, block, self.sems.at[0, j], self.sems.at[1, j], peer)

    def over(self, act):
        def body(j, carry):
            act((j * 13) % self.devices)
            return carry

        lax.fori_loop(*self.turns, body, 0)

    def start(self):
        self.own().start()
        self.start_remote()

    def start_remote(self):
        self.over(lambda j: self.outgoing(j).start())

    def wait(self):
        self.wait_remote()
        self.own().wait()

    def wait_remote(self):
        self.over(lambda j: self.incoming(j).wait_recv())
        self.over(lambda j: self.outgoing(j).wait_send())


def greet_peers(place):
    barrier = pltpu.get_barrier_semaphore()
    count = 0
    for axis, size in enumerate(place.sizes):
        for j in range(1, size):
            pl.semaphore_signal(barrier, inc=1, device_id=(place.device(axis, j),), device_id_type=MESH)
            count += 1
    pl.semaphore_wait(barrier, count)


def spread_scratch(sizes):
    return [pltpu.SemaphoreType.DMA((2, 4, max(sizes))), pltpu.SemaphoreType.DMA(())]


class Spread:
    def __init__(self, place, flip, own, out, scratch, lead=()):
        self.place, self.flip, self.mine, self.out, self.lead = place, flip, own, out, lead
        self.sems, self.local_sem = scratch
        self.axes = (0, 1, 2, 3) if flip else (0, 2, 1, 3)

    def region(self, stage, step=0):
        place, every = self.place, slice(None)
        where = [place.a, place.b, place.c, place.k]
        axis = self.axes[stage]
        where[axis] = place.ahead(axis, step)
        for done in self.axes[:stage]:
            where[done] = every
        return self.out.at[self.lead + tuple(where)]

    def local(self):
        return pltpu.make_async_copy(self.mine, self.region(0), self.local_sem)

    def outgoing(self, stage):
        axis = self.axes[stage]
        source = self.mine if stage == 0 else self.region(stage)
        return [
            remote(source, self.region(stage), self.sems.at[0, stage, j], self.sems.at[1, stage, j], self.place.device(axis, j))
            for j in range(1, self.place.sizes[axis])
        ]

    def start(self, stage):
        for copy in self.outgoing(stage):
            copy.start()
        if stage == 0:
            self.local().start()

    def settle(self, stage):
        axis = self.axes[stage]
        if stage == 0:
            self.local().wait()
        for j in range(1, self.place.sizes[axis]):
            block = self.region(stage, self.place.sizes[axis] - j)
            remote(block, block, self.sems.at[0, stage, j], self.sems.at[1, stage, j], self.place.device(axis, j)).wait_recv()

    def drain(self):
        for stage in range(4):
            for copy in self.outgoing(stage):
                copy.wait_send()


def store_flat(ref, base, value):
    rows, columns = value.shape
    width = ref.shape[0] // rows
    for j in range(columns // LANES):
        ref[pl.ds(base + j, rows, stride=width), :] = value[:, j * LANES:(j + 1) * LANES]


def tree_scratch(sizes, flip, rows, columns):
    na, nb, nc, nk = sizes
    one, two = (nb, nc) if flip else (nc, nb)
    shapes = [(na, nb, nc), (nk - 1, na, nb, nc), (one - 1, na, two), (two - 1, na), (na - 1,)]
    return [pltpu.VMEM(shape + (rows, columns), BF16) for shape in shapes] + [
        pltpu.SemaphoreType.DMA((2, 4, max(sizes))),
        pltpu.SemaphoreType.DMA(()),
    ]


class Tree:
    def __init__(self, place, flip, parts, scratch):
        self.place, self.flip, self.parts = place, flip, parts
        self.held, *self.landing, self.sems, self.local_sem = scratch
        order = (3, 1, 2, 0) if flip else (3, 2, 1, 0)
        self.axes = order

    def own(self):
        return pltpu.make_async_copy(self.parts.at[:, :, :, self.place.k], self.held, self.local_sem)

    def outgoing(self, stage):
        place, held = self.place, self.held
        axis = self.axes[stage]
        copies = []
        for j in range(1, place.sizes[axis]):
            other = place.ahead(axis, j)
            if stage == 0:
                source = self.parts.at[:, :, :, other]
            elif stage == 1:
                source = held.at[:, other] if self.flip else held.at[:, :, other]
            elif stage == 2:
                source = held.at[:, place.b, other] if self.flip else held.at[:, other, place.c]
            else:
                source = held.at[other, place.b, place.c]
            copies.append(
                remote(source, self.landing[stage].at[j - 1], self.sems.at[0, stage, j], self.sems.at[1, stage, j], place.device(axis, j))
            )
        return copies

    def start(self, stage):
        if stage == 0:
            self.own().start()
        for copy in self.outgoing(stage):
            copy.start()

    def settle(self, stage, out=None):
        out = out if stage == 3 else None
        place, held, landing = self.place, self.held, self.landing[stage]
        na, nb, nc, nk = place.sizes
        if stage == 0:
            self.own().wait()
        for copy in self.outgoing(stage):
            copy.wait_recv()
        count = place.sizes[self.axes[stage]] - 1

        def total(own, index):
            if count == 1 and out is None:
                return own + landing[(0,) + index]
            value = own.astype(F32)
            for j in range(count):
                value = value + landing[(j,) + index].astype(F32)
            return value

        if stage == 0:
            def add(i, carry):
                held[i] = total(held[i], (i,)).astype(BF16)
                return carry
            lax.fori_loop(0, na, add, 0)
        elif stage == 1:
            two = nc if self.flip else nb
            def add(i, carry):
                for t in range(two):
                    at = (i, place.b, t) if self.flip else (i, t, place.c)
                    held[at] = total(held[at], (i, t)).astype(BF16)
                return carry
            lax.fori_loop(0, na, add, 0)
        elif stage == 2:
            def add(i, carry):
                at = (i, place.b, place.c)
                held[at] = total(held[at], (i,)).astype(BF16)
                return carry
            lax.fori_loop(0, na, add, 0)
        else:
            out(total(held[place.a, place.b, place.c], ()))

    def drain(self):
        for stage in range(4):
            for copy in self.outgoing(stage):
                copy.wait_send()


LOW = 32
EARLY = 2


def select_rows(chosen, rows_ref):
    return dot_nn(jnp.where(chosen, 1.0, 0.0).astype(BF16), rows_ref[...]).astype(BF16)


def count_true(mask, axis):
    return jnp.sum(jnp.where(mask, 1.0, 0.0), axis=axis, keepdims=True)


def each_tile(tile, count, act):
    def body(t, carry):
        at = pl.multiple_of(t * tile, tile)
        act(pl.ds(at, tile), lax.broadcasted_iota(jnp.int32, (tile, count), 0) + at)
        return carry

    lax.fori_loop(0, count // tile, body, 0)


def load_flat(ref, base_ref, width, store):
    total = ref.shape[0]
    base_ref[0:total, :] = ref[...].astype(F32)
    per_row = width // LANES
    for j in range(per_row):
        store(j * LANES, base_ref[pl.ds(j, total // per_row, stride=per_row), :].astype(BF16))


def block_lanes(rows, columns, share):
    lane = lax.broadcasted_iota(jnp.int32, (rows, columns), 1).astype(F32)
    inside = lane - jnp.floor((lane + 0.5) * (1.0 / share)) * share
    return inside == lax.broadcasted_iota(jnp.int32, (rows, columns), 0).astype(F32)


def line_of(blocks, share):
    devices = blocks.shape[0]
    columns = devices * share
    spread = dot_nn(blocks, jnp.where(block_lanes(LANES, columns, share), 1.0, 0.0).astype(BF16))
    start = lax.broadcasted_iota(jnp.int32, (devices, columns), 0) * share
    lane = lax.broadcasted_iota(jnp.int32, (devices, columns), 1)
    return jnp.sum(jnp.where((lane >= start) & (lane < start + share), spread, 0.0), axis=0, keepdims=True)


def split3(column):
    high = column.astype(BF16).astype(F32)
    rest = column - high
    mid = rest.astype(BF16).astype(F32)
    return high, mid, rest - mid


def feature_lanes(rows):
    lane = lax.broadcasted_iota(jnp.int32, (rows, LANES), 1)
    return lane < HD, lane & (HD - 1)


def key_features(lane, segment, segments):
    return jnp.where(lane == segment, 1.0, jnp.where((lane >= segments) & (lane < segments + 3), 1.0, 0.0))


def query_features(lane, segment, segments):
    return jnp.where((lane < segments) & (lane != segment), NEG_LARGE, 0.0)


def with_column(features, lane, start, column):
    high, mid, last = split3(column)
    features = jnp.where(lane == start, high, features)
    features = jnp.where(lane == start + 1, mid, features)
    return jnp.where(lane == start + 2, last, features)


def front_kernel(segments, sizes, cuts, lengths_ref, *refs):
    given, outs, held = refs[:18], refs[18:35], refs[35:53]
    (out_ref, lse_ref, rows_hbm, q_hbm, k_hbm, v_hbm, g4, gi, gu, cot_hbm, cot_out,
     place_row, place_col, rank_out, segment_out, vec_out, bi_out) = outs
    (leaving_ref, arrived_ref, cot_leaving, flat_ref, w4_own, wi_own, wu_own, lines_ref, vec_own, gv, blocks_ref, w_ref, flat_w, rows_ref, q_ref, k_ref, v_ref,
     load_sems, save_sems, w_sem, swap_sems, swap_local, *spread_refs) = refs[53:]
    w4_refs, small_refs = held[:4], held[4:13]
    slots_ref, tokens_ref, cot_ref, wi_ref, wu_ref = held[13:]
    loads = [pltpu.make_async_copy(source, target, load_sems.at[i]) for i, (source, target) in enumerate(zip(given, held))]
    count, width = tokens_ref.shape
    devices = slots_ref.shape[0]
    peer_rows = count // devices
    share = width // devices
    tile = count // 4
    now, last = pl.program_id(0), pl.num_programs(0) - 1
    place = Place(sizes)
    me = place.me
    spreads = [
        Spread(place, False, w4_own.at[pl.ds(0, 2)], g4, spread_refs[0:2], (pl.ds(0, 2),)),
        Spread(place, True, w4_own.at[pl.ds(2, 2)], g4, spread_refs[2:4], (pl.ds(2, 2),)),
        Spread(place, True, vec_own, gv, spread_refs[4:6]),
    ]
    wide = []
    for i, (which, base, columns, flip) in enumerate(cuts):
        own, whole = ((wi_own, gi), (wu_own, gu))[which]
        cut = pl.ds(base, columns)
        wide.append(Spread(place, flip, own.at[:, cut], whole.at[:, :, :, :, :, cut], spread_refs[6 + 2 * i:8 + 2 * i]))
    swap = Exchange(devices, leaving_ref, arrived_ref, swap_sems.at[0], swap_local)
    early = Exchange(devices, cot_leaving, cot_out, swap_sems.at[1], swap_local, (1, devices // EARLY))
    w_load = pltpu.make_async_copy(g4.at[pl.ds(0, 3)], w_ref, w_sem)
    saves = [
        pltpu.make_async_copy(source, target, save_sems.at[i])
        for i, (source, target) in enumerate(((rows_ref, rows_hbm), (q_ref, q_hbm), (k_ref, k_hbm), (v_ref, v_hbm), (cot_leaving, cot_hbm)))
    ]

    def onward(group, stage):
        for spread in group:
            spread.settle(stage)
            if stage < 3:
                spread.start(stage + 1)

    def pair(i):
        return wide[2 * i:2 * i + 2]

    def begin(i):
        for spread in pair(i):
            spread.start(0)

    @pl.when(now == 0)
    def _():
        for load in loads:
            load.start()
        for load in loads[:13]:
            load.wait()
        for i, ref in enumerate(w4_refs):
            def put(at, value, i=i):
                w4_own[i, :, at:at + LANES] = value
            load_flat(ref, flat_ref, width, put)
        lines_ref[...] = jnp.zeros_like(lines_ref)
        for i, ref in enumerate(small_refs):
            lines_ref[i:i + 1, 0:ref.shape[1]] = ref[...].astype(F32)
        vec_own[...] = lines_ref[...].astype(BF16)
        greet_all(devices)
        for spread in spreads:
            spread.start(0)
        for load in loads[13:]:
            load.wait()

        lane = lax.broadcasted_iota(jnp.int32, (tile, count), 1)
        own_row = slots_ref[pl.ds(me, 1), :]
        own_float = own_row.astype(F32)

        def column_of(row, line):
            return jnp.sum(jnp.where(lane == row, line, 0.0), axis=1, keepdims=True)

        def rank_tile(t, total):
            row = lax.broadcasted_iota(jnp.int32, (tile, count), 0) + t * tile
            return total + count_true(column_of(row, own_float) < own_float, 0)

        rank_row = lax.fori_loop(0, count // tile, rank_tile, jnp.zeros((1, count), F32)).astype(jnp.int32)

        def leave(cut, row):
            leaving_ref[cut, :] = select_rows(rank_row == row, tokens_ref)

        each_tile(tile, count, leave)
        swap.start()
        onward(spreads, 0)

        def put_inner(at, value):
            wi_own[:, at:at + LANES] = value

        def put_outer(at, value):
            wu_own[:, at:at + LANES] = value

        load_flat(wi_ref, flat_ref, wi_own.shape[1], put_inner)
        load_flat(wu_ref, flat_ref, width, put_outer)

        def leave_cot(cut, row):
            cot_leaving[cut, :] = select_rows(rank_row == row, cot_ref)
            rank_out[cut, :] = count_true(own_float < column_of(row, own_float), 1).astype(jnp.int32)

        each_tile(tile, count, leave_cot)
        saves[4].start()
        row = lax.broadcasted_iota(jnp.int32, (count, 1), 0)
        end, segment = 0, jnp.zeros((count, 1), jnp.int32)
        for i in range(lengths_ref.shape[1]):
            end = end + lengths_ref[0, i]
            segment = segment + jnp.where(row >= end, 1, 0)
        segment_out[...] = segment
        onward(spreads, 1)
        begin(0)

        high = count // LOW

        def body(s, total):
            local = slots_ref[pl.ds(s, 1), :] - me * count
            in_high = lax.broadcasted_iota(jnp.int32, (high, count), 0) == (local >> 5)
            in_low = lax.broadcasted_iota(jnp.int32, (LOW, count), 0) == (local & (LOW - 1))
            weight = jnp.where(in_high, s.astype(F32), 0.0).astype(BF16)
            return total + dot_nt(weight, jnp.where(in_low, 1.0, 0.0).astype(BF16))

        source = lax.fori_loop(0, devices, body, jnp.zeros((high, LOW), F32)).astype(BF16)
        over = lax.broadcasted_iota(jnp.int32, (high, count), 1)
        picked = dot_tn(source, jnp.where((over >> 5) == lax.broadcasted_iota(jnp.int32, (high, count), 0), 1.0, 0.0).astype(BF16))
        low_row = lax.broadcasted_iota(jnp.int32, (LOW, count), 0)
        low_wide = lax.broadcasted_iota(jnp.int32, (LOW, count), 1) & (LOW - 1)
        source_row = jnp.sum(jnp.where(low_row == low_wide, picked, 0.0), axis=0, keepdims=True)
        onward(spreads, 2)

        def place_tile(t, places):
            at = pl.multiple_of(t * tile, tile)
            row = lax.broadcasted_iota(jnp.int32, (tile, count), 0) + at
            source_col = column_of(row, source_row)
            same = source_col == source_row
            place_col[pl.ds(at, tile), :] = (source_col * peer_rows + count_true(same & (lane < row), 1)).astype(jnp.int32)
            return places + count_true(same & (row < lane), 0)

        place_row[...] = lax.fori_loop(0, count // tile, place_tile, source_row * peer_rows).astype(jnp.int32)
        onward(spreads, 3)
        w_load.start()
        for i, line in enumerate(small_refs):
            for d in range(devices):
                nk, nc, nb = sizes[3], sizes[2], sizes[1]
                blocks_ref[d:d + 1, :] = gv[d // (nk * nc * nb), d // (nk * nc) % nb, d // nk % nc, d % nk].astype(F32)[i:i + 1, :]
            value = line_of(blocks_ref[...].astype(BF16), line.shape[1])
            if i < 8:
                vec_out[i:i + 1, :] = value
            else:
                bi_out[...] = value
        w_load.wait()
        onward(pair(0), 0)
        begin(1)
        swap.wait()
        vec = vec_out[...]
        wq, wk, wv = (w_ref[i].astype(F32).reshape(width, width).astype(BF16) for i in range(3))
        for i, w in enumerate((wq, wk, wv)):
            flat_w[i] = w

        def project(cut, _):
            rows = select_rows(place_col[cut, :] == lane, arrived_ref)
            rows_ref[cut, :] = rows
            q_ref[cut, :] = ((dot_nn(rows, flat_w[0]) + vec[0:1]).astype(BF16).astype(F32) * 0.125).astype(BF16)
            k_ref[cut, :] = dot_nn(rows, flat_w[1]).astype(BF16)
            v_ref[cut, :] = (dot_nn(rows, flat_w[2]) + vec[1:2]).astype(BF16)

        each_tile(tile, count, project)
        for save in saves[:4]:
            save.start()

    columns = pl.ds(pl.multiple_of(jnp.maximum(now - 1, 0) * LANES, LANES), LANES)
    first, feature = feature_lanes(count)

    def head(mask):
        seg = segment_out[...]
        keys = jnp.where(mask, k_ref[:, columns], key_features(feature, seg, segments).astype(BF16))
        query = jnp.where(mask, q_ref[:, columns], query_features(feature, seg, segments).astype(BF16))
        scores = dot_nt(query, keys)
        top = jnp.max(scores, axis=1, keepdims=True)
        raised = jnp.exp(scores - top)
        total = jnp.sum(raised, axis=1, keepdims=True)
        return dot_nn(raised.astype(BF16), v_ref[:, columns]) * (1.0 / total), top + jnp.log(total)

    def hook(at, act):
        @pl.when(now == at)
        def _():
            act()

    @pl.when(now > 0)
    def _():
        out0, log0 = head(first)
        out1, log1 = head(~first)
        out_ref[...] = jnp.where(first, out0, out1).astype(BF16)
        lse_ref[...] = jnp.where(first, log0, log1)

    hook(0, lambda: (onward(pair(0), 1), begin(2)))
    hook(1, lambda: (onward(pair(1), 0), early.start_remote()))
    hook(2, lambda: onward(pair(2), 0))
    hook(3, lambda: (onward(pair(0), 2), onward(pair(1), 1)))
    hook(4, lambda: onward(pair(2), 1))
    hook(5, lambda: onward(pair(1), 2))

    @pl.when(now == last)
    def _():
        onward(pair(0), 3)
        onward(pair(2), 2)
        onward(pair(1), 3)
        onward(pair(2), 3)
        for spread in spreads + wide:
            spread.drain()
        early.wait_remote()
        for save in saves:
            save.wait()


def front(segments, seq_lengths, packed_slot, tokens, cotangent, w4, wi, wu, small):
    devices, count = packed_slot.shape
    width = tokens.shape[1]
    hidden_width = small[-1].shape[0] * devices
    sizes = grid_of(devices)
    share = width // devices
    pairs = width // LANES
    anywhere = pl.BlockSpec(memory_space=pl.ANY)
    pair_spec = pl.BlockSpec((count, LANES), lambda i: (0, jnp.maximum(i - 1, 0)))

    def shape(*dims, dtype=BF16):
        return jax.ShapeDtypeStruct(dims, dtype)

    def held(*dims, dtype=BF16):
        return pltpu.VMEM(dims, dtype)

    part = width // 6
    cuts = [(0, 0, hidden_width // 2, False), (0, hidden_width // 2, hidden_width // 2, True),
            (1, 0, 2 * part, False), (1, 2 * part, 2 * part, True), (1, 4 * part, part, False), (1, 5 * part, part, True)]
    flat = [w.reshape(-1, LANES) for w in w4]
    given = flat + [x.reshape(1, -1) for x in small] + [packed_slot, tokens, cotangent, wi.reshape(-1, LANES), wu.reshape(-1, LANES)]
    whole = shape(count, width)
    lines = [shape(1, count, dtype=jnp.int32)] + [shape(count, 1, dtype=jnp.int32)] * 3 + [shape(8, width, dtype=F32), shape(1, hidden_width, dtype=F32)]
    return pl.pallas_call(
        partial(front_kernel, segments, sizes, cuts),
        grid=(1 + pairs,),
        out_shape=[whole, shape(count, width, dtype=F32)] + [whole] * 4
        + [shape(4, *sizes, share, width), shape(*sizes, share, hidden_width), shape(*sizes, hidden_width // devices, width), whole, whole] + lines,
        in_specs=[pl.BlockSpec(memory_space=pltpu.SMEM)] + [anywhere] * len(given),
        out_specs=[pair_spec, pair_spec] + [anywhere] * 9 + [full_spec(x.shape) for x in lines],
        scratch_shapes=[pltpu.VMEM(x.shape, x.dtype) for x in given]
        + [held(count, width)] * 3 + [held(*given[-1].shape, dtype=F32), held(4, share, width), held(share, hidden_width),
           held(hidden_width // devices, width), held(16, LANES, dtype=F32), held(16, LANES), held(*sizes, 16, LANES), held(devices, LANES, dtype=F32),
           held(3, *sizes, share, width), held(3, width, width)] + [held(count, width)] * 4
        + [pltpu.SemaphoreType.DMA((len(given),)), pltpu.SemaphoreType.DMA((5,)), pltpu.SemaphoreType.DMA(()),
           pltpu.SemaphoreType.DMA((2, 2, devices)), pltpu.SemaphoreType.DMA(())] + spread_scratch(sizes) * (3 + len(cuts)),
        compiler_params=params(60, "arbitrary", collective_id=1, has_side_effects=True),
        cost_estimate=pl.CostEstimate(flops=16 * count * count * width, bytes_accessed=30 * MIB, transcendentals=count * count * 12),
        name="front",
    )(seq_lengths, *given)


def normalize(hidden):
    centered = hidden - jnp.mean(hidden, axis=1, keepdims=True)
    variance = jnp.mean(centered * centered, axis=1, keepdims=True)
    inverse = lax.rsqrt(variance + EPSILON)
    return centered * inverse, inverse


def normalize_back(grad, normal, inverse):
    return inverse * (
        grad
        - jnp.mean(grad, axis=1, keepdims=True)
        - normal * jnp.mean(grad * normal, axis=1, keepdims=True)
    )


def column_sum(matrix):
    return jnp.sum(matrix.astype(F32), axis=0, keepdims=True)


def feed_kernel(sizes, tiles, chunk, where_ref, place_ref, rows_hbm, att_hbm, cot_hbm, early_hbm, w4_hbm, wi_hbm, wu_hbm, vec_ref, bi_ref,
                first_ref, agrad_ref, returned_hbm, dwi_ref, dwu_ref, dwo_ref, sums_ref, bisum_ref,
                act_ref, inner_ref, slope_ref, turned_ref, outer_ref, low_ref, normal1_ref, normal2_ref, inverse1_ref, inverse2_ref,
                cot_ref, result_ref, leaving_ref, rows_ref, att_ref, wo_ref, wi_ref, wu_ref, load_sems, early_sems, swap_sems, swap_local):
    count = att_ref.shape[0]
    tile = count // tiles
    hidden_width = wi_ref.shape[1]
    devices = sizes[0] * sizes[1] * sizes[2] * sizes[3]
    step, last = pl.program_id(0), pl.num_programs(0) - 1
    vec = vec_ref[...]
    bo, ga, sa, bu, gf, sf = (vec[i:i + 1] for i in range(2, 8))
    enter = Exchange(devices, cot_hbm, cot_ref, swap_sems.at[0], swap_local.at[0], (devices // EARLY, devices))
    early = Exchange(devices, early_hbm, cot_ref, None, None, (1, devices // EARLY))
    loads = [
        pltpu.make_async_copy(source, target, load_sems.at[i])
        for i, (source, target) in enumerate((
            (att_hbm, att_ref), (w4_hbm.at[3], wo_ref), (rows_hbm, rows_ref), (wi_hbm, wi_ref), (wu_hbm, wu_ref)
        ))
    ]

    def early_block(j):
        peer = (early.me + devices - j) % devices
        return pltpu.make_async_copy(early.block(early_hbm, peer), early.block(cot_ref, peer), early_sems.at[j])

    leave = Exchange(devices, leaving_ref, returned_hbm, swap_sems.at[1], swap_local.at[1])

    @pl.when(step == 0)
    def _():
        for load in loads:
            load.start()
        greet_all(devices)
        enter.start()
        early.over(lambda j: early_block(j).start())
        sums_ref[...] = jnp.zeros_like(sums_ref)
        bisum_ref[...] = jnp.zeros_like(bisum_ref)
        for load in loads:
            load.wait()

    @pl.when(step < tiles)
    def _():
        cut = pl.ds(pl.multiple_of(step * tile, tile), tile)
        first_sum = rows_ref[cut, :].astype(F32) + dot_nn(att_ref[cut, :], wo_ref[...]) + bo
        normal1, inverse1 = normalize(first_sum)
        normal1_ref[cut, :] = normal1
        inverse1_ref[cut, :] = inverse1
        normed = normal1 * ga + sa
        normed_low = normed.astype(BF16)
        turned_ref[:, cut] = normed.T.astype(BF16)
        second = normed + bu
        for at in range(0, hidden_width, chunk):
            pre = dot_nn(normed_low, wi_ref[:, at:at + chunk]) + bi_ref[:, at:at + chunk]
            share = 0.5 + 0.5 * lax.erf(pre * 0.7071067811865476)
            act = (pre * share).astype(BF16)
            act_ref[cut, at:at + chunk] = act
            slope_ref[cut, at:at + chunk] = (share + pre * (jnp.exp(pre * pre * -0.5) * 0.3989422804014327)).astype(BF16)
            second = second + dot_nn(act, wu_ref[at:at + chunk, :])
        normal2, inverse2 = normalize(second)
        normal2_ref[cut, :] = normal2
        inverse2_ref[cut, :] = inverse2
        result_ref[cut, :] = (normal2 * gf + sf).astype(BF16)

    @pl.when(step == tiles)
    def _():
        def leave_tile(cut, target):
            leaving_ref[cut, :] = select_rows(where_ref[...] == target, result_ref)

        each_tile(tile, count, leave_tile)
        early.over(lambda j: early_block(j).wait())
        enter.wait()
        leave.start()

    @pl.when((step >= tiles) & (step < 2 * tiles))
    def _():
        cut = pl.ds(pl.multiple_of((step - tiles) * tile, tile), tile)
        lane = lax.broadcasted_iota(jnp.int32, (tile, count), 1)
        chosen = jnp.where(place_ref[...] == lane, 1.0, 0.0).astype(BF16)
        cot = dot_nn(chosen, cot_ref[...])
        normal1, normal2 = normal1_ref[cut, :], normal2_ref[cut, :]
        second_grad = normalize_back(cot * gf, normal2, inverse2_ref[cut, :])
        outer_low = second_grad.astype(BF16)
        outer_ref[cut, :] = outer_low
        normed_grad = second_grad
        for at in range(0, hidden_width, chunk):
            act_grad = dot_nt(outer_low, wu_ref[at:at + chunk, :])
            inner_low = (act_grad * slope_ref[cut, at:at + chunk].astype(F32)).astype(BF16)
            inner_ref[cut, at:at + chunk] = inner_low
            bisum_ref[0:1, at:at + chunk] += column_sum(inner_low)
            normed_grad = normed_grad + dot_nt(inner_low, wi_ref[:, at:at + chunk])
        first_grad = normalize_back(normed_grad * ga, normal1, inverse1_ref[cut, :])
        first_ref[...] = first_grad
        branch_low = first_grad.astype(BF16)
        low_ref[cut, :] = branch_low
        agrad_ref[...] = dot_nt(branch_low, wo_ref[...]).astype(BF16)
        sums_ref[2:3, :] += column_sum(branch_low)
        sums_ref[3:4, :] += column_sum(normed_grad * normal1)
        sums_ref[4:5, :] += column_sum(normed_grad)
        sums_ref[5:6, :] += column_sum(outer_low)
        sums_ref[6:7, :] += column_sum(cot * normal2)
        sums_ref[7:8, :] += column_sum(cot)

    @pl.when(step >= 2 * tiles)
    def _():
        cut = pl.ds(pl.multiple_of((step - 2 * tiles) * chunk, chunk), chunk)
        dwi_ref[...] = dot_nn(turned_ref[...], inner_ref[:, cut]).astype(BF16)
        dwu_ref[...] = dot_tn(act_ref[:, cut], outer_ref[...]).astype(BF16)

    @pl.when(step == last)
    def _():
        dwo_ref[...] = dot_tn(att_ref[...], low_ref[...]).astype(BF16)
        leave.wait()


def feed_forward(devices, place_row, place_col, rows, attended, leaving_cot, early_cot, w4, wi, wu, vec, bi):
    count, width = rows.shape
    hidden_width = wi.shape[1]
    tiles, chunk = 4, 768
    tile = count // tiles
    anywhere = pl.BlockSpec(memory_space=pl.ANY)
    back_spec = pl.BlockSpec((tile, width), lambda i: (jnp.clip(i - tiles, 0, tiles - 1), 0))
    parts = hidden_width // chunk

    def part(i):
        return jnp.clip(i - 2 * tiles, 0, parts - 1)

    def held(n, dtype=BF16):
        return pltpu.VMEM((count, n), dtype)

    return pl.pallas_call(
        partial(feed_kernel, grid_of(devices), tiles, chunk),
        grid=(2 * tiles + parts,),
        out_shape=[
            jax.ShapeDtypeStruct((count, width), F32), jax.ShapeDtypeStruct((count, width), BF16), jax.ShapeDtypeStruct((count, width), BF16),
            jax.ShapeDtypeStruct((width, hidden_width), BF16), jax.ShapeDtypeStruct((hidden_width, width), BF16),
            jax.ShapeDtypeStruct((width, width), BF16), jax.ShapeDtypeStruct((8, width), F32), jax.ShapeDtypeStruct((8, hidden_width), F32),
        ],
        in_specs=[
            held_spec((1, count)), pl.BlockSpec((tile, 1), lambda i: (jnp.clip(i - tiles, 0, tiles - 1), 0)),
            anywhere, anywhere, anywhere, anywhere, anywhere, anywhere, anywhere, held_spec(vec.shape), held_spec(bi.shape),
        ],
        out_specs=[
            back_spec, back_spec, anywhere,
            pl.BlockSpec((width, chunk), lambda i: (0, part(i))), pl.BlockSpec((chunk, width), lambda i: (part(i), 0)),
            full_spec((width, width)), full_spec((8, width)), full_spec((8, hidden_width)),
        ],
        scratch_shapes=[
            held(hidden_width), held(hidden_width), held(hidden_width), pltpu.VMEM((width, count), BF16), held(width), held(width),
            held(width, F32), held(width, F32), held(1, F32), held(1, F32), held(width), held(width), held(width),
            held(width), held(width), pltpu.VMEM((width, width), BF16), pltpu.VMEM(wi.shape, BF16), pltpu.VMEM(wu.shape, BF16),
            pltpu.SemaphoreType.DMA((5,)), pltpu.SemaphoreType.DMA((devices,)), pltpu.SemaphoreType.DMA((2, 2, devices)), pltpu.SemaphoreType.DMA((2,)),
        ],
        compiler_params=params(62, "arbitrary", collective_id=5, has_side_effects=True),
        cost_estimate=pl.CostEstimate(flops=20 * count * width * hidden_width, bytes_accessed=36 * MIB, transcendentals=2 * count * hidden_width),
        name="feed_forward",
    )(place_row, place_col, rows, attended, leaving_cot, early_cot, w4, wi, wu, vec, bi)


def by_device(line, devices, share):
    count = line.shape[1]
    start = lax.broadcasted_iota(jnp.int32, (devices, count), 0) * share
    lane = lax.broadcasted_iota(jnp.int32, (devices, count), 1)
    left = jnp.where((lane >= start) & (lane < start + share), line, 0.0).astype(BF16)
    return dot_nt(left, jnp.where(block_lanes(LANES, count, share), 1.0, 0.0).astype(BF16))


def back_kernel(segments, sizes, share, cuts, seg_ref, where_ref, q_ref, o_ref, g_ref, lse_ref, k_ref, v_ref, sums_ref, bisum_ref,
                wi_ref, wu_ref, wo_ref, first_hbm, w4_hbm, rows_hbm, *refs):
    back_ref, wi_out, wu_out, wo_out, wq_out, wk_out, wv_out, *small_outs = refs[:16]
    (dq_ref, dk_ref, dv_ref, first_ref, w_ref, rows_ref, load_sems, total_ref, leaving_ref, wq_part, wk_part, wv_part,
     lines_ref, small_part, swap_sems, swap_local, *tree_refs) = refs[16:]
    count, width = total_ref.shape
    na, nb, nc, nk = sizes
    devices = na * nb * nc * nk
    tile = count // 4
    now, last = pl.program_id(0), pl.num_programs(0) - 1
    place = Place(sizes)
    loads = [
        pltpu.make_async_copy(source, target, load_sems.at[i])
        for i, (source, target) in enumerate(((first_hbm, first_ref), (w4_hbm.at[pl.ds(0, 3)], w_ref), (rows_hbm, rows_ref)))
    ]
    swap = Exchange(devices, leaving_ref, back_ref, swap_sems, swap_local)
    outs = {0: wi_out, 1: wu_out, 2: wo_out}
    every = (slice(None),) * 5
    trees, ends = [], []
    for i, (which, base, columns, flip) in enumerate(cuts):
        parts = (wi_ref, wu_ref, wo_ref)[which].at[every + (pl.ds(base, columns),)]
        trees.append(Tree(place, flip, parts, tree_refs[7 * i:7 * i + 7]))
        ends.append(partial(store_flat, outs[which], base // LANES))
    late_parts = (wq_part, wk_part, wv_part, small_part)
    late = [
        Tree(place, i % 2 == 1, part, tree_refs[7 * (len(cuts) + i):7 * (len(cuts) + i) + 7])
        for i, part in enumerate(late_parts)
    ]

    groups = (slice(0, 3), slice(3, 5), slice(5, 7), slice(7, 9))

    def onward(group, stage, then=None):
        for tree, end in zip(trees[groups[group]], ends[groups[group]]):
            tree.settle(stage, end)
            if stage < 3:
                tree.start(stage + 1)
        if then is not None:
            for tree in trees[groups[then]]:
                tree.start(0)

    def hook(at, act):
        @pl.when(now == at)
        def _():
            act()

    @pl.when(now == 0)
    def _():
        greet_all(devices)
        for tree in trees[groups[0]]:
            tree.start(0)
        onward(0, 0, 1)

    first, lane = feature_lanes(count)
    columns = pl.ds(pl.multiple_of(now * LANES, LANES), LANES)

    def head(mask, at):
        seg, grads = seg_ref[...], g_ref[...]
        ones = key_features(lane, seg, segments).astype(BF16)
        keys = jnp.where(mask, k_ref[...], ones)
        values = jnp.where(mask, v_ref[...], ones)
        lse = lse_ref[:, at:at + 1]
        product = grads.astype(F32) * o_ref[...].astype(F32)
        delta = jnp.sum(jnp.where(mask, product, 0.0), axis=1, keepdims=True)
        hidden = query_features(lane, seg, segments)
        query = jnp.where(mask, q_ref[...], with_column(hidden, lane, segments, -lse).astype(BF16))
        grad = jnp.where(mask, grads, with_column(jnp.zeros_like(hidden), lane, segments, -delta).astype(BF16))
        dqs, dk, dv = [], 0.0, 0.0
        for top in range(0, count, count // PARTS):
            cut = slice(top, top + count // PARTS)
            probs = jnp.exp(dot_nt(keys, query[cut]))
            score = (probs * dot_nt(values, grad[cut])).astype(BF16)
            dv = dv + dot_nn(probs.astype(BF16), grad[cut])
            dk = dk + dot_nn(score, query[cut])
            dqs.append(dot_tn(score, keys))
        return (jnp.concatenate(dqs) * 0.125).astype(BF16), dk.astype(BF16), dv.astype(BF16)

    for ref, one, two in zip((dq_ref, dk_ref, dv_ref), head(first, 0), head(~first, HD)):
        ref[:, columns] = jnp.where(first, one, two)

    hook(1, lambda: (onward(0, 1), onward(1, 0, 2)))
    hook(3, lambda: (onward(0, 2), onward(1, 1), onward(2, 0, 3), [load.start() for load in loads]))
    hook(4, lambda: (onward(1, 2), onward(2, 1), onward(3, 0)))
    hook(5, lambda: (onward(2, 2), onward(3, 1)))

    @pl.when(now == last)
    def _():
        for load in loads:
            load.wait()

        def total_tile(cut, _):
            total_ref[cut, :] = (
                first_ref[cut, :] + dot_nt(dq_ref[cut, :], w_ref[0]) + dot_nt(dk_ref[cut, :], w_ref[1]) + dot_nt(dv_ref[cut, :], w_ref[2])
            ).astype(BF16)

        each_tile(tile, count, total_tile)
        onward(3, 2)
        onward(0, 3)

        def leave(cut, target):
            leaving_ref[cut, :] = select_rows(where_ref[...] == target, total_ref)

        each_tile(tile, count, leave)
        onward(1, 3)
        onward(2, 3)
        onward(3, 3)
        swap.start()
        group = 3 * LANES
        for grad_ref, part, tree in zip((dq_ref, dk_ref, dv_ref), late_parts, late):
            def weight_tile(t, carry, grad_ref=grad_ref, part=part):
                value = dot_tn(rows_ref[:, pl.ds(pl.multiple_of(t * group, group), group)], grad_ref[...])
                for i in range(group // share):
                    d = t * (group // share) + i
                    index = (d // (nk * nc * nb), d // (nk * nc) % nb, d // nk % nc, d % nk)
                    part[index] = value[i * share:(i + 1) * share].astype(BF16)
                return carry

            lax.fori_loop(0, width // group, weight_tile, 0)
            tree.start(0)
        lines_ref[...] = jnp.zeros_like(lines_ref)
        lines_ref[0] = by_device(column_sum(dq_ref[...]), devices, share)
        lines_ref[1] = by_device(column_sum(dv_ref[...]), devices, share)
        for i in range(2, 8):
            lines_ref[i] = by_device(sums_ref[i:i + 1, :], devices, share)
        lines_ref[8] = by_device(bisum_ref[0:1, :], devices, bisum_ref.shape[1] // devices)
        for d in range(devices):
            index = (d // (nk * nc * nb), d // (nk * nc) % nb, d // nk % nc, d % nk)
            small_part[index] = lines_ref[:, d, :].astype(BF16)
        late[3].start(0)
        for stage in range(3):
            for tree in late:
                tree.settle(stage)
                tree.start(stage + 1)
        for tree, out in zip(late, (wq_out, wk_out, wv_out)):
            tree.settle(3, partial(store_flat, out, 0))

        def store_small(value):
            for i, out in enumerate(small_outs):
                out[...] = value[i:i + 1, :out.shape[1]]

        late[3].settle(3, store_small)
        swap.wait()
        for tree in trees + late:
            tree.drain()


PARTS = 1


def backward(segments, segment_col, place_row, q, out, grad, lse, k, v, sums, bi_sum, wi, wu, wo, first_grad, w4, rows):
    count, width = q.shape
    pairs = width // LANES
    devices = wi.shape[0]
    share = width // devices
    sizes = grid_of(devices)
    pair_spec = pl.BlockSpec((count, LANES), lambda h: (0, h))
    anywhere = pl.BlockSpec(memory_space=pl.ANY)
    parts = [x.reshape(sizes + x.shape[1:]) for x in (wi, wu, wo)]
    cuts = []
    for base, size in ((0, 2), (2, 2), (4, 1), (5, 1)):
        for which, x in ((0, wi), (1, wu)):
            cuts.append((which, base * x.shape[2] // 6, size * x.shape[2] // 6, which == 1))
        if base == 0:
            cuts.append((2, 0, wo.shape[2], False))
    trees = []
    for which, _, columns, flip in cuts:
        trees += tree_scratch(sizes, flip, (wi, wu, wo)[which].shape[1], columns)
    for i, shape in enumerate(((share, width),) * 3 + ((16, LANES),)):
        trees += tree_scratch(sizes, i % 2 == 1, *shape)
    flats = [(x.shape[1] * x.shape[2] // LANES, LANES) for x in (wi, wu, wo)] + [(share * width // LANES, LANES)] * 3
    flats += [(1, share)] * 8 + [(1, bi_sum.shape[1] // devices)]
    whole = pltpu.VMEM((count, width), BF16)
    return pl.pallas_call(
        partial(back_kernel, segments, sizes, share, cuts),
        grid=(pairs,),
        out_shape=[jax.ShapeDtypeStruct((count, width), BF16)] + [jax.ShapeDtypeStruct(flat, F32) for flat in flats],
        in_specs=[held_spec((count, 1)), held_spec((1, count))] + [pair_spec] * 6 + [held_spec(sums.shape), held_spec(bi_sum.shape)]
        + [anywhere] * 6,
        out_specs=[anywhere] + [full_spec(flat) for flat in flats],
        scratch_shapes=[whole] * 3 + [pltpu.VMEM((count, width), F32), pltpu.VMEM((3, width, width), BF16), whole, pltpu.SemaphoreType.DMA((3,))]
        + [whole] * 2 + [pltpu.VMEM(sizes + (share, width), BF16)] * 3
        + [pltpu.VMEM((16, devices, LANES), F32), pltpu.VMEM(sizes + (16, LANES), BF16)]
        + [pltpu.SemaphoreType.DMA((2, devices)), pltpu.SemaphoreType.DMA(())] + trees,
        compiler_params=params(63, "arbitrary", collective_id=2, has_side_effects=True),
        cost_estimate=pl.CostEstimate(flops=20 * count * count * width, bytes_accessed=16 * MIB, transcendentals=count * count * 12),
        name="backward",
    )(segment_col, place_row, q, out, grad, lse, k, v, sums, bi_sum, *parts, first_grad, w4, rows)


def emit_kernel(rank_ref, back_hbm, layer_hbm, *refs):
    count = (len(refs) - 5) // 2
    given, tokens_ref, layer_ref, outs, (back_ref, held_ref, sems) = refs[:count], refs[count], refs[count + 1], refs[count + 2:2 * count + 2], refs[2 * count + 2:]
    moved = [
        pltpu.make_async_copy(source, target, sems.at[i])
        for i, (source, target) in enumerate(zip((back_hbm, layer_hbm, *given), (back_ref, held_ref, *outs)))
    ]
    for copy in moved:
        copy.start()
    rows = back_ref.shape[0]
    tile = rows // 4
    for copy in moved[:2]:
        copy.wait()
    lane = lax.broadcasted_iota(jnp.int32, (tile, rows), 1)

    def restore(cut, _):
        chosen = rank_ref[cut, :] == lane
        tokens_ref[cut, :] = select_rows(chosen, back_ref)
        layer_ref[cut, :] = select_rows(chosen, held_ref)

    each_tile(tile, rows, restore)
    for copy in moved[2:]:
        copy.wait()


def emit(rank_col, back, layer, others):
    anywhere = pl.BlockSpec(memory_space=pl.ANY)
    in_vmem = pl.BlockSpec(memory_space=pltpu.VMEM)
    return pl.pallas_call(
        emit_kernel,
        out_shape=[jax.ShapeDtypeStruct(x.shape, x.dtype) for x in (back, layer, *others)],
        in_specs=[in_vmem] + [anywhere] * (2 + len(others)),
        out_specs=[in_vmem] * (2 + len(others)),
        scratch_shapes=[pltpu.VMEM(back.shape, BF16)] * 2 + [pltpu.SemaphoreType.DMA((len(others) + 2,))],
        compiler_params=pltpu.CompilerParams(vmem_limit_bytes=56 * MIB),
        name="emit",
    )(rank_col, back, layer, *others)


def on_device(tokens, cotangent, packed_slot, seq_lengths, query_weight, query_bias, key_weight, value_weight,
              value_bias, output_weight, output_bias, attention_gain, attention_shift, inner_weight, inner_bias,
              outer_weight, outer_bias, final_gain, final_shift):
    devices = lax.axis_size("fsdp")
    count, width = tokens.shape
    hidden_width = inner_bias.shape[0] * devices
    segments = seq_lengths.shape[1]
    share = width // devices
    small = (query_bias, value_bias, output_bias, attention_gain, attention_shift, outer_bias, final_gain, final_shift, inner_bias)
    (attended, lse, rows, q, k, v, g4, gi, gu, leaving_cot, early_cot, place_row, place_col, rank_col, segment_col, vec, bi) = front(
        segments, seq_lengths, packed_slot.reshape(devices, count), tokens, cotangent,
        (query_weight, key_weight, value_weight, output_weight), inner_weight, outer_weight, small,
    )
    w4 = g4.reshape(4, width, width)
    wi = gi.reshape(width, hidden_width)
    wu = gu.reshape(hidden_width, width)
    first_grad, attended_grad, returned, inner_grad, outer_grad, wo_grad, sums, bi_sum = feed_forward(
        devices, place_row, place_col, rows, attended, leaving_cot, early_cot, w4, wi, wu, vec, bi
    )
    inner_grad, outer_grad, wo_grad = (x.reshape(devices, -1, x.shape[-1]) for x in (inner_grad, outer_grad, wo_grad))
    back, inner_grad, outer_grad, wo_grad, wq_grad, wk_grad, wv_grad, *small = backward(
        segments, segment_col, place_row, q, attended, attended_grad, lse, k, v, sums, bi_sum,
        inner_grad, outer_grad, wo_grad, first_grad, w4, rows,
    )
    tokens_grad, layer_out, wq_grad, wk_grad, wv_grad, wo_grad, inner_grad, outer_grad, *small = emit(
        rank_col, back, returned, (wq_grad, wk_grad, wv_grad, wo_grad, inner_grad, outer_grad, *small)
    )
    wq_grad, wk_grad, wv_grad, wo_grad, wi_grad, wu_grad = (
        x.reshape(-1) for x in (wq_grad, wk_grad, wv_grad, wo_grad, inner_grad, outer_grad)
    )
    bq, bv, bo, ga, sa, bu, gf, sf, bi = (x.reshape(-1) for x in small)
    return (layer_out, tokens_grad, wq_grad, bq, wk_grad, wv_grad, bv, wo_grad, bo, ga, sa, wi_grad, bi, wu_grad, bu, gf, sf)


def solution(mesh):
    split, rows = P("fsdp"), P("fsdp", None)
    return jax.shard_map(
        on_device,
        mesh=mesh,
        in_specs=(rows, rows, P(), rows) + (split,) * 15,
        out_specs=(rows, rows) + (split,) * 15,
        check_vma=False,
    )
```

```python
from functools import partial

import jax
import jax.numpy as jnp
from jax import lax
from jax.experimental import pallas as pl
from jax.experimental.pallas import tpu as pltpu
from jax.sharding import PartitionSpec as P

HD = 64
LANES = 128
EPSILON = 1e-12
NEG_LARGE = -1e30
MIB = 1 << 20
F32 = jnp.float32
BF16 = jnp.bfloat16
MESH = pl.DeviceIdType.MESH


def dot_nn(a, b):
    return lax.dot_general(a, b, (((1,), (0,)), ((), ())), preferred_element_type=F32)


def dot_nt(a, b):
    return lax.dot_general(a, b, (((1,), (1,)), ((), ())), preferred_element_type=F32)


def dot_tn(a, b):
    return lax.dot_general(a, b, (((0,), (0,)), ((), ())), preferred_element_type=F32)


def full_spec(shape, **kw):
    return pl.BlockSpec(shape, lambda *_: (0,) * len(shape), **kw)


def held_spec(shape):
    return full_spec(shape, pipeline_mode=pl.Buffered(1))


def params(mib, *axes, **kw):
    return pltpu.CompilerParams(
        dimension_semantics=axes or None, vmem_limit_bytes=mib * MIB, **kw
    )


def grid_of(devices):
    return {32: (4, 2, 2, 2), 128: (4, 4, 4, 2)}.get(devices, (devices, 1, 1, 1))


class Place:
    def __init__(self, sizes):
        na, nb, nc, nk = self.sizes = sizes
        self.me = me = lax.axis_index("fsdp")
        self.k = me % nk
        self.c = (me // nk) % nc
        self.b = (me // (nk * nc)) % nb
        self.a = me // (nk * nc * nb)

    def ahead(self, axis, step):
        own = (self.a, self.b, self.c, self.k)[axis]
        return (own + step) % self.sizes[axis]

    def device(self, axis, step):
        na, nb, nc, nk = self.sizes
        where = [self.a, self.b, self.c, self.k]
        where[axis] = self.ahead(axis, step)
        return ((where[0] * nb + where[1]) * nc + where[2]) * nk + where[3]


def remote(source, target, send_sem, recv_sem, peer):
    return pltpu.make_async_remote_copy(
        src_ref=source, dst_ref=target, send_sem=send_sem, recv_sem=recv_sem,
        device_id=(peer,), device_id_type=MESH,
    )


def greet_all(devices):
    me = lax.axis_index("fsdp")
    barrier = pltpu.get_barrier_semaphore()

    def signal(j, carry):
        pl.semaphore_signal(barrier, inc=1, device_id=((me + j) % devices,), device_id_type=MESH)
        return carry

    lax.fori_loop(1, devices, signal, 0)
    pl.semaphore_wait(barrier, devices - 1)


class Exchange:
    def __init__(self, devices, source, target, sems, local_sem, turns=None):
        self.devices, self.source, self.target, self.sems, self.local_sem = devices, source, target, sems, local_sem
        self.turns = turns or (1, devices)
        self.rows = source.shape[0] // devices
        self.me = lax.axis_index("fsdp")

    def block(self, ref, device):
        return ref.at[pl.ds(pl.multiple_of(device * self.rows, self.rows), self.rows)]

    def own(self):
        return pltpu.make_async_copy(self.block(self.source, self.me), self.block(self.target, self.me), self.local_sem)

    def outgoing(self, j):
        peer = (self.me + j) % self.devices
        return remote(self.block(self.source, peer), self.block(self.target, self.me), self.sems.at[0, j], self.sems.at[1, j], peer)

    def incoming(self, j):
        peer = (self.me + self.devices - j) % self.devices
        block = self.block(self.target, peer)
        return remote(block, block, self.sems.at[0, j], self.sems.at[1, j], peer)

    def over(self, act):
        def body(j, carry):
            act((j * 13) % self.devices)
            return carry

        lax.fori_loop(*self.turns, body, 0)

    def start(self):
        self.own().start()
        self.start_remote()

    def start_remote(self):
        self.over(lambda j: self.outgoing(j).start())

    def wait(self):
        self.wait_remote()
        self.own().wait()

    def wait_remote(self):
        self.over(lambda j: self.incoming(j).wait_recv())
        self.over(lambda j: self.outgoing(j).wait_send())


def greet_peers(place):
    barrier = pltpu.get_barrier_semaphore()
    count = 0
    for axis, size in enumerate(place.sizes):
        for j in range(1, size):
            pl.semaphore_signal(barrier, inc=1, device_id=(place.device(axis, j),), device_id_type=MESH)
            count += 1
    pl.semaphore_wait(barrier, count)


def spread_scratch(sizes):
    return [pltpu.SemaphoreType.DMA((2, 4, max(sizes))), pltpu.SemaphoreType.DMA(())]


class Spread:
    def __init__(self, place, flip, own, out, scratch, lead=()):
        self.place, self.flip, self.mine, self.out, self.lead = place, flip, own, out, lead
        self.sems, self.local_sem = scratch
        self.axes = (0, 1, 2, 3) if flip else (0, 2, 1, 3)

    def region(self, stage, step=0):
        place, every = self.place, slice(None)
        where = [place.a, place.b, place.c, place.k]
        axis = self.axes[stage]
        where[axis] = place.ahead(axis, step)
        for done in self.axes[:stage]:
            where[done] = every
        return self.out.at[self.lead + tuple(where)]

    def local(self):
        return pltpu.make_async_copy(self.mine, self.region(0), self.local_sem)

    def outgoing(self, stage):
        axis = self.axes[stage]
        source = self.mine if stage == 0 else self.region(stage)
        return [
            remote(source, self.region(stage), self.sems.at[0, stage, j], self.sems.at[1, stage, j], self.place.device(axis, j))
            for j in range(1, self.place.sizes[axis])
        ]

    def start(self, stage):
        for copy in self.outgoing(stage):
            copy.start()
        if stage == 0:
            self.local().start()

    def settle(self, stage):
        axis = self.axes[stage]
        if stage == 0:
            self.local().wait()
        for j in range(1, self.place.sizes[axis]):
            block = self.region(stage, self.place.sizes[axis] - j)
            remote(block, block, self.sems.at[0, stage, j], self.sems.at[1, stage, j], self.place.device(axis, j)).wait_recv()

    def drain(self):
        for stage in range(4):
            for copy in self.outgoing(stage):
                copy.wait_send()


def store_flat(ref, base, value):
    rows, columns = value.shape
    width = ref.shape[0] // rows
    for j in range(columns // LANES):
        ref[pl.ds(base + j, rows, stride=width), :] = value[:, j * LANES:(j + 1) * LANES]


def tree_scratch(sizes, flip, rows, columns):
    na, nb, nc, nk = sizes
    one, two = (nb, nc) if flip else (nc, nb)
    shapes = [(na, nb, nc), (nk - 1, na, nb, nc), (one - 1, na, two), (two - 1, na), (na - 1,)]
    return [pltpu.VMEM(shape + (rows, columns), BF16) for shape in shapes] + [
        pltpu.SemaphoreType.DMA((2, 4, max(sizes))),
        pltpu.SemaphoreType.DMA(()),
    ]


class Tree:
    def __init__(self, place, flip, parts, scratch):
        self.place, self.flip, self.parts = place, flip, parts
        self.held, *self.landing, self.sems, self.local_sem = scratch
        order = (3, 1, 2, 0) if flip else (3, 2, 1, 0)
        self.axes = order

    def own(self):
        return pltpu.make_async_copy(self.parts.at[:, :, :, self.place.k], self.held, self.local_sem)

    def outgoing(self, stage):
        place, held = self.place, self.held
        axis = self.axes[stage]
        copies = []
        for j in range(1, place.sizes[axis]):
            other = place.ahead(axis, j)
            if stage == 0:
                source = self.parts.at[:, :, :, other]
            elif stage == 1:
                source = held.at[:, other] if self.flip else held.at[:, :, other]
            elif stage == 2:
                source = held.at[:, place.b, other] if self.flip else held.at[:, other, place.c]
            else:
                source = held.at[other, place.b, place.c]
            copies.append(
                remote(source, self.landing[stage].at[j - 1], self.sems.at[0, stage, j], self.sems.at[1, stage, j], place.device(axis, j))
            )
        return copies

    def start(self, stage):
        if stage == 0:
            self.own().start()
        for copy in self.outgoing(stage):
            copy.start()

    def settle(self, stage, out=None):
        out = out if stage == 3 else None
        place, held, landing = self.place, self.held, self.landing[stage]
        na, nb, nc, nk = place.sizes
        if stage == 0:
            self.own().wait()
        for copy in self.outgoing(stage):
            copy.wait_recv()
        count = place.sizes[self.axes[stage]] - 1

        def total(own, index):
            if count == 1 and out is None:
                return own + landing[(0,) + index]
            value = own.astype(F32)
            for j in range(count):
                value = value + landing[(j,) + index].astype(F32)
            return value

        if stage == 0:
            def add(i, carry):
                held[i] = total(held[i], (i,)).astype(BF16)
                return carry
            lax.fori_loop(0, na, add, 0)
        elif stage == 1:
            two = nc if self.flip else nb
            def add(i, carry):
                for t in range(two):
                    at = (i, place.b, t) if self.flip else (i, t, place.c)
                    held[at] = total(held[at], (i, t)).astype(BF16)
                return carry
            lax.fori_loop(0, na, add, 0)
        elif stage == 2:
            def add(i, carry):
                at = (i, place.b, place.c)
                held[at] = total(held[at], (i,)).astype(BF16)
                return carry
            lax.fori_loop(0, na, add, 0)
        else:
            out(total(held[place.a, place.b, place.c], ()))

    def drain(self):
        for stage in range(4):
            for copy in self.outgoing(stage):
                copy.wait_send()


LOW = 32
EARLY = 2


def select_rows(chosen, rows_ref):
    return dot_nn(jnp.where(chosen, 1.0, 0.0).astype(BF16), rows_ref[...]).astype(BF16)


def count_true(mask, axis):
    return jnp.sum(jnp.where(mask, 1.0, 0.0), axis=axis, keepdims=True)


def each_tile(tile, count, act):
    def body(t, carry):
        at = pl.multiple_of(t * tile, tile)
        act(pl.ds(at, tile), lax.broadcasted_iota(jnp.int32, (tile, count), 0) + at)
        return carry

    lax.fori_loop(0, count // tile, body, 0)


def load_flat(ref, base_ref, width, store):
    total = ref.shape[0]
    base_ref[0:total, :] = ref[...].astype(F32)
    per_row = width // LANES
    for j in range(per_row):
        store(j * LANES, base_ref[pl.ds(j, total // per_row, stride=per_row), :].astype(BF16))


def block_lanes(rows, columns, share):
    lane = lax.broadcasted_iota(jnp.int32, (rows, columns), 1).astype(F32)
    inside = lane - jnp.floor((lane + 0.5) * (1.0 / share)) * share
    return inside == lax.broadcasted_iota(jnp.int32, (rows, columns), 0).astype(F32)


def line_of(blocks, share):
    devices = blocks.shape[0]
    columns = devices * share
    spread = dot_nn(blocks, jnp.where(block_lanes(LANES, columns, share), 1.0, 0.0).astype(BF16))
    start = lax.broadcasted_iota(jnp.int32, (devices, columns), 0) * share
    lane = lax.broadcasted_iota(jnp.int32, (devices, columns), 1)
    return jnp.sum(jnp.where((lane >= start) & (lane < start + share), spread, 0.0), axis=0, keepdims=True)


def split3(column):
    high = column.astype(BF16).astype(F32)
    rest = column - high
    mid = rest.astype(BF16).astype(F32)
    return high, mid, rest - mid


def feature_lanes(rows):
    lane = lax.broadcasted_iota(jnp.int32, (rows, LANES), 1)
    return lane < HD, lane & (HD - 1)


def key_features(lane, segment, segments):
    return jnp.where(lane == segment, 1.0, jnp.where((lane >= segments) & (lane < segments + 3), 1.0, 0.0))


def query_features(lane, segment, segments):
    return jnp.where((lane < segments) & (lane != segment), NEG_LARGE, 0.0)


def with_column(features, lane, start, column):
    high, mid, last = split3(column)
    features = jnp.where(lane == start, high, features)
    features = jnp.where(lane == start + 1, mid, features)
    return jnp.where(lane == start + 2, last, features)


def front_kernel(segments, sizes, cuts, lengths_ref, *refs):
    given, outs, held = refs[:18], refs[18:35], refs[35:53]
    (out_ref, lse_ref, rows_hbm, q_hbm, k_hbm, v_hbm, g4, gi, gu, cot_hbm, cot_out,
     place_row, place_col, rank_out, segment_out, vec_out, bi_out) = outs
    (leaving_ref, arrived_ref, cot_leaving, flat_ref, w4_own, wi_own, wu_own, lines_ref, vec_own, gv, blocks_ref, w_ref, flat_w, slots_ref, rows_ref, q_ref, k_ref, v_ref,
     load_sems, save_sems, w_sem, swap_sems, swap_local, *spread_refs) = refs[53:]
    w4_refs, small_refs = held[:4], held[4:13]
    slots_flat, tokens_ref, cot_ref, wi_ref, wu_ref = held[13:]
    loads = [pltpu.make_async_copy(source, target, load_sems.at[i]) for i, (source, target) in enumerate(zip(given, held))]
    count, width = tokens_ref.shape
    devices = slots_ref.shape[0]
    peer_rows = count // devices
    share = width // devices
    tile = count // 4
    now, last = pl.program_id(0), pl.num_programs(0) - 1
    place = Place(sizes)
    me = place.me
    spreads = [
        Spread(place, False, w4_own.at[pl.ds(0, 2)], g4, spread_refs[0:2], (pl.ds(0, 2),)),
        Spread(place, True, w4_own.at[pl.ds(2, 2)], g4, spread_refs[2:4], (pl.ds(2, 2),)),
        Spread(place, True, vec_own, gv, spread_refs[4:6]),
    ]
    wide = []
    for i, (which, base, columns, flip) in enumerate(cuts):
        own, whole = ((wi_own, gi), (wu_own, gu))[which]
        cut = pl.ds(base, columns)
        wide.append(Spread(place, flip, own.at[:, cut], whole.at[:, :, :, :, :, cut], spread_refs[6 + 2 * i:8 + 2 * i]))
    swap = Exchange(devices, leaving_ref, arrived_ref, swap_sems.at[0], swap_local)
    early = Exchange(devices, cot_leaving, cot_out, swap_sems.at[1], swap_local, (1, devices // EARLY))
    w_load = pltpu.make_async_copy(g4.at[pl.ds(0, 3)], w_ref, w_sem)
    saves = [
        pltpu.make_async_copy(source, target, save_sems.at[i])
        for i, (source, target) in enumerate(((rows_ref, rows_hbm), (q_ref, q_hbm), (k_ref, k_hbm), (v_ref, v_hbm), (cot_leaving, cot_hbm)))
    ]

    def onward(group, stage):
        for spread in group:
            spread.settle(stage)
            if stage < 3:
                spread.start(stage + 1)

    def pair(i):
        return wide[2 * i:2 * i + 2]

    def begin(i):
        for spread in pair(i):
            spread.start(0)

    @pl.when(now == 0)
    def _():
        for load in loads:
            load.start()
        for load in loads[:13]:
            load.wait()
        for i, ref in enumerate(w4_refs):
            def put(at, value, i=i):
                w4_own[i, :, at:at + LANES] = value
            load_flat(ref, flat_ref, width, put)
        lines_ref[...] = jnp.zeros_like(lines_ref)
        for i, ref in enumerate(small_refs):
            lines_ref[i:i + 1, 0:ref.shape[1]] = ref[...].astype(F32)
        vec_own[...] = lines_ref[...].astype(BF16)
        greet_all(devices)
        for spread in spreads:
            spread.start(0)
        for load in loads[13:]:
            load.wait()
        per_row = count // LANES
        for j in range(per_row):
            slots_ref[:, j * LANES:(j + 1) * LANES] = slots_flat[pl.ds(j, devices, stride=per_row), :]

        lane = lax.broadcasted_iota(jnp.int32, (tile, count), 1)
        own_row = slots_ref[pl.ds(me, 1), :]
        own_float = own_row.astype(F32)

        def column_of(row, line):
            return jnp.sum(jnp.where(lane == row, line, 0.0), axis=1, keepdims=True)

        def rank_tile(t, total):
            row = lax.broadcasted_iota(jnp.int32, (tile, count), 0) + t * tile
            return total + count_true(column_of(row, own_float) < own_float, 0)

        rank_row = lax.fori_loop(0, count // tile, rank_tile, jnp.zeros((1, count), F32)).astype(jnp.int32)

        def leave(cut, row):
            leaving_ref[cut, :] = select_rows(rank_row == row, tokens_ref)

        each_tile(tile, count, leave)
        swap.start()
        onward(spreads, 0)

        def put_inner(at, value):
            wi_own[:, at:at + LANES] = value

        def put_outer(at, value):
            wu_own[:, at:at + LANES] = value

        load_flat(wi_ref, flat_ref, wi_own.shape[1], put_inner)
        load_flat(wu_ref, flat_ref, width, put_outer)

        def leave_cot(cut, row):
            cot_leaving[cut, :] = select_rows(rank_row == row, cot_ref)
            rank_out[cut, :] = count_true(own_float < column_of(row, own_float), 1).astype(jnp.int32)

        each_tile(tile, count, leave_cot)
        saves[4].start()
        row = lax.broadcasted_iota(jnp.int32, (count, 1), 0)
        end, segment = 0, jnp.zeros((count, 1), jnp.int32)
        for i in range(lengths_ref.shape[1]):
            end = end + lengths_ref[0, i]
            segment = segment + jnp.where(row >= end, 1, 0)
        segment_out[...] = segment
        onward(spreads, 1)
        begin(0)

        high = count // LOW

        def body(s, total):
            local = slots_ref[pl.ds(s, 1), :] - me * count
            in_high = lax.broadcasted_iota(jnp.int32, (high, count), 0) == (local >> 5)
            in_low = lax.broadcasted_iota(jnp.int32, (LOW, count), 0) == (local & (LOW - 1))
            weight = jnp.where(in_high, s.astype(F32), 0.0).astype(BF16)
            return total + dot_nt(weight, jnp.where(in_low, 1.0, 0.0).astype(BF16))

        source = lax.fori_loop(0, devices, body, jnp.zeros((high, LOW), F32)).astype(BF16)
        over = lax.broadcasted_iota(jnp.int32, (high, count), 1)
        picked = dot_tn(source, jnp.where((over >> 5) == lax.broadcasted_iota(jnp.int32, (high, count), 0), 1.0, 0.0).astype(BF16))
        low_row = lax.broadcasted_iota(jnp.int32, (LOW, count), 0)
        low_wide = lax.broadcasted_iota(jnp.int32, (LOW, count), 1) & (LOW - 1)
        source_row = jnp.sum(jnp.where(low_row == low_wide, picked, 0.0), axis=0, keepdims=True)
        onward(spreads, 2)

        def place_tile(t, places):
            at = pl.multiple_of(t * tile, tile)
            row = lax.broadcasted_iota(jnp.int32, (tile, count), 0) + at
            source_col = column_of(row, source_row)
            same = source_col == source_row
            place_col[pl.ds(at, tile), :] = (source_col * peer_rows + count_true(same & (lane < row), 1)).astype(jnp.int32)
            return places + count_true(same & (row < lane), 0)

        place_row[...] = lax.fori_loop(0, count // tile, place_tile, source_row * peer_rows).astype(jnp.int32)
        onward(spreads, 3)
        w_load.start()
        for i, line in enumerate(small_refs):
            for d in range(devices):
                nk, nc, nb = sizes[3], sizes[2], sizes[1]
                blocks_ref[d:d + 1, :] = gv[d // (nk * nc * nb), d // (nk * nc) % nb, d // nk % nc, d % nk].astype(F32)[i:i + 1, :]
            value = line_of(blocks_ref[...].astype(BF16), line.shape[1])
            if i < 8:
                vec_out[i:i + 1, :] = value
            else:
                bi_out[...] = value
        w_load.wait()
        onward(pair(0), 0)
        begin(1)
        swap.wait()
        vec = vec_out[...]
        wq, wk, wv = (w_ref[i].astype(F32).reshape(width, width).astype(BF16) for i in range(3))
        for i, w in enumerate((wq, wk, wv)):
            flat_w[i] = w

        def project(cut, _):
            rows = select_rows(place_col[cut, :] == lane, arrived_ref)
            rows_ref[cut, :] = rows
            q_ref[cut, :] = ((dot_nn(rows, flat_w[0]) + vec[0:1]).astype(BF16).astype(F32) * 0.125).astype(BF16)
            k_ref[cut, :] = dot_nn(rows, flat_w[1]).astype(BF16)
            v_ref[cut, :] = (dot_nn(rows, flat_w[2]) + vec[1:2]).astype(BF16)

        each_tile(tile, count, project)
        for save in saves[:4]:
            save.start()

    columns = pl.ds(pl.multiple_of(jnp.maximum(now - 1, 0) * LANES, LANES), LANES)
    first, feature = feature_lanes(count)

    def head(mask):
        seg = segment_out[...]
        keys = jnp.where(mask, k_ref[:, columns], key_features(feature, seg, segments).astype(BF16))
        query = jnp.where(mask, q_ref[:, columns], query_features(feature, seg, segments).astype(BF16))
        scores = dot_nt(query, keys)
        top = jnp.max(scores, axis=1, keepdims=True)
        raised = jnp.exp(scores - top)
        total = jnp.sum(raised, axis=1, keepdims=True)
        return dot_nn(raised.astype(BF16), v_ref[:, columns]) * (1.0 / total), top + jnp.log(total)

    def hook(at, act):
        @pl.when(now == at)
        def _():
            act()

    @pl.when(now > 0)
    def _():
        out0, log0 = head(first)
        out1, log1 = head(~first)
        out_ref[...] = jnp.where(first, out0, out1).astype(BF16)
        lse_ref[...] = jnp.where(first, log0, log1)

    hook(0, lambda: (onward(pair(0), 1), begin(2)))
    hook(1, lambda: (onward(pair(1), 0), early.start_remote()))
    hook(2, lambda: onward(pair(2), 0))
    hook(3, lambda: (onward(pair(0), 2), onward(pair(1), 1)))
    hook(4, lambda: onward(pair(2), 1))
    hook(5, lambda: onward(pair(1), 2))

    @pl.when(now == last)
    def _():
        onward(pair(0), 3)
        onward(pair(2), 2)
        onward(pair(1), 3)
        onward(pair(2), 3)
        for spread in spreads + wide:
            spread.drain()
        early.wait_remote()
        for save in saves:
            save.wait()


def front(segments, seq_lengths, packed_slot, tokens, cotangent, w4, wi, wu, small):
    width = tokens.shape[1]
    count = tokens.shape[0]
    devices = packed_slot.shape[0] // count
    hidden_width = small[-1].shape[0] * devices
    sizes = grid_of(devices)
    share = width // devices
    pairs = width // LANES
    anywhere = pl.BlockSpec(memory_space=pl.ANY)
    pair_spec = pl.BlockSpec((count, LANES), lambda i: (0, jnp.maximum(i - 1, 0)))

    def shape(*dims, dtype=BF16):
        return jax.ShapeDtypeStruct(dims, dtype)

    def held(*dims, dtype=BF16):
        return pltpu.VMEM(dims, dtype)

    part = width // 6
    cuts = [(0, 0, hidden_width // 2, False), (0, hidden_width // 2, hidden_width // 2, True),
            (1, 0, 2 * part, False), (1, 2 * part, 2 * part, True), (1, 4 * part, part, False), (1, 5 * part, part, True)]
    flat = [w.reshape(-1, LANES) for w in w4]
    given = flat + [x.reshape(1, -1) for x in small] + [packed_slot.reshape(-1, LANES), tokens, cotangent, wi.reshape(-1, LANES), wu.reshape(-1, LANES)]
    whole = shape(count, width)
    lines = [shape(1, count, dtype=jnp.int32)] + [shape(count, 1, dtype=jnp.int32)] * 3 + [shape(8, width, dtype=F32), shape(1, hidden_width, dtype=F32)]
    return pl.pallas_call(
        partial(front_kernel, segments, sizes, cuts),
        grid=(1 + pairs,),
        out_shape=[whole, shape(count, width, dtype=F32)] + [whole] * 4
        + [shape(4, *sizes, share, width), shape(*sizes, share, hidden_width), shape(*sizes, hidden_width // devices, width), whole, whole] + lines,
        in_specs=[pl.BlockSpec(memory_space=pltpu.SMEM)] + [anywhere] * len(given),
        out_specs=[pair_spec, pair_spec] + [anywhere] * 9 + [full_spec(x.shape) for x in lines],
        scratch_shapes=[pltpu.VMEM(x.shape, x.dtype) for x in given]
        + [held(count, width)] * 3 + [held(*given[-1].shape, dtype=F32), held(4, share, width), held(share, hidden_width),
           held(hidden_width // devices, width), held(16, LANES, dtype=F32), held(16, LANES), held(*sizes, 16, LANES), held(devices, LANES, dtype=F32),
           held(3, *sizes, share, width), held(3, width, width), held(devices, count, dtype=jnp.int32)] + [held(count, width)] * 4
        + [pltpu.SemaphoreType.DMA((len(given),)), pltpu.SemaphoreType.DMA((5,)), pltpu.SemaphoreType.DMA(()),
           pltpu.SemaphoreType.DMA((2, 2, devices)), pltpu.SemaphoreType.DMA(())] + spread_scratch(sizes) * (3 + len(cuts)),
        compiler_params=params(60, "arbitrary", collective_id=1, has_side_effects=True),
        cost_estimate=pl.CostEstimate(flops=16 * count * count * width, bytes_accessed=30 * MIB, transcendentals=count * count * 12),
        name="front",
    )(seq_lengths, *given)


def normalize(hidden):
    centered = hidden - jnp.mean(hidden, axis=1, keepdims=True)
    variance = jnp.mean(centered * centered, axis=1, keepdims=True)
    inverse = lax.rsqrt(variance + EPSILON)
    return centered * inverse, inverse


def normalize_back(grad, normal, inverse):
    return inverse * (
        grad
        - jnp.mean(grad, axis=1, keepdims=True)
        - normal * jnp.mean(grad * normal, axis=1, keepdims=True)
    )


def column_sum(matrix):
    return jnp.sum(matrix.astype(F32), axis=0, keepdims=True)


def feed_kernel(sizes, tiles, chunk, where_ref, place_ref, rows_hbm, att_hbm, cot_hbm, early_hbm, w4_hbm, wi_hbm, wu_hbm, vec_ref, bi_ref,
                first_ref, agrad_ref, returned_hbm, dwi_ref, dwu_ref, dwo_ref, sums_ref, bisum_ref,
                act_ref, inner_ref, slope_ref, turned_ref, outer_ref, low_ref, normal1_ref, normal2_ref, inverse1_ref, inverse2_ref,
                cot_ref, result_ref, leaving_ref, rows_ref, att_ref, wo_ref, wi_ref, wu_ref, load_sems, early_sems, swap_sems, swap_local):
    count = att_ref.shape[0]
    tile = count // tiles
    hidden_width = wi_ref.shape[1]
    devices = sizes[0] * sizes[1] * sizes[2] * sizes[3]
    step, last = pl.program_id(0), pl.num_programs(0) - 1
    vec = vec_ref[...]
    bo, ga, sa, bu, gf, sf = (vec[i:i + 1] for i in range(2, 8))
    enter = Exchange(devices, cot_hbm, cot_ref, swap_sems.at[0], swap_local.at[0], (devices // EARLY, devices))
    early = Exchange(devices, early_hbm, cot_ref, None, None, (1, devices // EARLY))
    loads = [
        pltpu.make_async_copy(source, target, load_sems.at[i])
        for i, (source, target) in enumerate((
            (att_hbm, att_ref), (w4_hbm.at[3], wo_ref), (rows_hbm, rows_ref), (wi_hbm, wi_ref), (wu_hbm, wu_ref)
        ))
    ]

    def early_block(j):
        peer = (early.me + devices - j) % devices
        return pltpu.make_async_copy(early.block(early_hbm, peer), early.block(cot_ref, peer), early_sems.at[j])

    leave = Exchange(devices, leaving_ref, returned_hbm, swap_sems.at[1], swap_local.at[1])

    @pl.when(step == 0)
    def _():
        for load in loads:
            load.start()
        greet_all(devices)
        enter.start()
        early.over(lambda j: early_block(j).start())
        sums_ref[...] = jnp.zeros_like(sums_ref)
        bisum_ref[...] = jnp.zeros_like(bisum_ref)
        for load in loads:
            load.wait()

    @pl.when(step < tiles)
    def _():
        cut = pl.ds(pl.multiple_of(step * tile, tile), tile)
        first_sum = rows_ref[cut, :].astype(F32) + dot_nn(att_ref[cut, :], wo_ref[...]) + bo
        normal1, inverse1 = normalize(first_sum)
        normal1_ref[cut, :] = normal1
        inverse1_ref[cut, :] = inverse1
        normed = normal1 * ga + sa
        normed_low = normed.astype(BF16)
        turned_ref[:, cut] = normed.T.astype(BF16)
        second = normed + bu
        for at in range(0, hidden_width, chunk):
            pre = dot_nn(normed_low, wi_ref[:, at:at + chunk]) + bi_ref[:, at:at + chunk]
            share = 0.5 + 0.5 * lax.erf(pre * 0.7071067811865476)
            act = (pre * share).astype(BF16)
            act_ref[cut, at:at + chunk] = act
            slope_ref[cut, at:at + chunk] = (share + pre * (jnp.exp(pre * pre * -0.5) * 0.3989422804014327)).astype(BF16)
            second = second + dot_nn(act, wu_ref[at:at + chunk, :])
        normal2, inverse2 = normalize(second)
        normal2_ref[cut, :] = normal2
        inverse2_ref[cut, :] = inverse2
        result_ref[cut, :] = (normal2 * gf + sf).astype(BF16)

    @pl.when(step == tiles)
    def _():
        def leave_tile(cut, target):
            leaving_ref[cut, :] = select_rows(where_ref[...] == target, result_ref)

        each_tile(tile, count, leave_tile)
        leave.start()
        early.over(lambda j: early_block(j).wait())
        enter.wait()

    @pl.when((step >= tiles) & (step < 2 * tiles))
    def _():
        cut = pl.ds(pl.multiple_of((step - tiles) * tile, tile), tile)
        lane = lax.broadcasted_iota(jnp.int32, (tile, count), 1)
        chosen = jnp.where(place_ref[...] == lane, 1.0, 0.0).astype(BF16)
        cot = dot_nn(chosen, cot_ref[...])
        normal1, normal2 = normal1_ref[cut, :], normal2_ref[cut, :]
        second_grad = normalize_back(cot * gf, normal2, inverse2_ref[cut, :])
        outer_low = second_grad.astype(BF16)
        outer_ref[cut, :] = outer_low
        normed_grad = second_grad
        for at in range(0, hidden_width, chunk):
            act_grad = dot_nt(outer_low, wu_ref[at:at + chunk, :])
            inner_low = (act_grad * slope_ref[cut, at:at + chunk].astype(F32)).astype(BF16)
            inner_ref[cut, at:at + chunk] = inner_low
            bisum_ref[0:1, at:at + chunk] += column_sum(inner_low)
            normed_grad = normed_grad + dot_nt(inner_low, wi_ref[:, at:at + chunk])
        first_grad = normalize_back(normed_grad * ga, normal1, inverse1_ref[cut, :])
        first_ref[...] = first_grad
        branch_low = first_grad.astype(BF16)
        low_ref[cut, :] = branch_low
        agrad_ref[...] = dot_nt(branch_low, wo_ref[...]).astype(BF16)
        sums_ref[2:3, :] += column_sum(branch_low)
        sums_ref[3:4, :] += column_sum(normed_grad * normal1)
        sums_ref[4:5, :] += column_sum(normed_grad)
        sums_ref[5:6, :] += column_sum(outer_low)
        sums_ref[6:7, :] += column_sum(cot * normal2)
        sums_ref[7:8, :] += column_sum(cot)

    @pl.when(step >= 2 * tiles)
    def _():
        cut = pl.ds(pl.multiple_of((step - 2 * tiles) * chunk, chunk), chunk)
        dwi_ref[...] = dot_nn(turned_ref[...], inner_ref[:, cut]).astype(BF16)
        dwu_ref[...] = dot_tn(act_ref[:, cut], outer_ref[...]).astype(BF16)

    @pl.when(step == last)
    def _():
        dwo_ref[...] = dot_tn(att_ref[...], low_ref[...]).astype(BF16)
        leave.wait()


def feed_forward(devices, place_row, place_col, rows, attended, leaving_cot, early_cot, w4, wi, wu, vec, bi):
    count, width = rows.shape
    hidden_width = wi.shape[1]
    tiles, chunk = 4, 768
    tile = count // tiles
    anywhere = pl.BlockSpec(memory_space=pl.ANY)
    back_spec = pl.BlockSpec((tile, width), lambda i: (jnp.clip(i - tiles, 0, tiles - 1), 0))
    parts = hidden_width // chunk

    def part(i):
        return jnp.clip(i - 2 * tiles, 0, parts - 1)

    def held(n, dtype=BF16):
        return pltpu.VMEM((count, n), dtype)

    return pl.pallas_call(
        partial(feed_kernel, grid_of(devices), tiles, chunk),
        grid=(2 * tiles + parts,),
        out_shape=[
            jax.ShapeDtypeStruct((count, width), F32), jax.ShapeDtypeStruct((count, width), BF16), jax.ShapeDtypeStruct((count, width), BF16),
            jax.ShapeDtypeStruct((width, hidden_width), BF16), jax.ShapeDtypeStruct((hidden_width, width), BF16),
            jax.ShapeDtypeStruct((width, width), BF16), jax.ShapeDtypeStruct((8, width), F32), jax.ShapeDtypeStruct((8, hidden_width), F32),
        ],
        in_specs=[
            held_spec((1, count)), pl.BlockSpec((tile, 1), lambda i: (jnp.clip(i - tiles, 0, tiles - 1), 0)),
            anywhere, anywhere, anywhere, anywhere, anywhere, anywhere, anywhere, held_spec(vec.shape), held_spec(bi.shape),
        ],
        out_specs=[
            back_spec, back_spec, anywhere,
            pl.BlockSpec((width, chunk), lambda i: (0, part(i))), pl.BlockSpec((chunk, width), lambda i: (part(i), 0)),
            full_spec((width, width)), full_spec((8, width)), full_spec((8, hidden_width)),
        ],
        scratch_shapes=[
            held(hidden_width), held(hidden_width), held(hidden_width), pltpu.VMEM((width, count), BF16), held(width), held(width),
            held(width, F32), held(width, F32), held(1, F32), held(1, F32), held(width), held(width), held(width),
            held(width), held(width), pltpu.VMEM((width, width), BF16), pltpu.VMEM(wi.shape, BF16), pltpu.VMEM(wu.shape, BF16),
            pltpu.SemaphoreType.DMA((5,)), pltpu.SemaphoreType.DMA((devices,)), pltpu.SemaphoreType.DMA((2, 2, devices)), pltpu.SemaphoreType.DMA((2,)),
        ],
        compiler_params=params(62, "arbitrary", collective_id=5, has_side_effects=True),
        cost_estimate=pl.CostEstimate(flops=20 * count * width * hidden_width, bytes_accessed=36 * MIB, transcendentals=2 * count * hidden_width),
        name="feed_forward",
    )(place_row, place_col, rows, attended, leaving_cot, early_cot, w4, wi, wu, vec, bi)


def by_device(line, devices, share):
    count = line.shape[1]
    start = lax.broadcasted_iota(jnp.int32, (devices, count), 0) * share
    lane = lax.broadcasted_iota(jnp.int32, (devices, count), 1)
    left = jnp.where((lane >= start) & (lane < start + share), line, 0.0).astype(BF16)
    return dot_nt(left, jnp.where(block_lanes(LANES, count, share), 1.0, 0.0).astype(BF16))


def back_kernel(segments, sizes, share, cuts, seg_ref, where_ref, q_ref, o_ref, g_ref, lse_ref, k_ref, v_ref, sums_ref, bisum_ref,
                wi_ref, wu_ref, wo_ref, first_hbm, w4_hbm, rows_hbm, *refs):
    back_ref, wi_out, wu_out, wo_out, wq_out, wk_out, wv_out, *small_outs = refs[:16]
    (dq_ref, dk_ref, dv_ref, first_ref, w_ref, rows_ref, load_sems, total_ref, leaving_ref, wq_part, wk_part, wv_part,
     lines_ref, small_part, swap_sems, swap_local, *tree_refs) = refs[16:]
    count, width = total_ref.shape
    na, nb, nc, nk = sizes
    devices = na * nb * nc * nk
    tile = count // 4
    now, last = pl.program_id(0), pl.num_programs(0) - 1
    place = Place(sizes)
    loads = [
        pltpu.make_async_copy(source, target, load_sems.at[i])
        for i, (source, target) in enumerate(((first_hbm, first_ref), (w4_hbm.at[pl.ds(0, 3)], w_ref), (rows_hbm, rows_ref)))
    ]
    swap = Exchange(devices, leaving_ref, back_ref, swap_sems, swap_local)
    outs = {0: wi_out, 1: wu_out, 2: wo_out}
    every = (slice(None),) * 5
    trees, ends = [], []
    for i, (which, base, columns, flip) in enumerate(cuts):
        parts = (wi_ref, wu_ref, wo_ref)[which].at[every + (pl.ds(base, columns),)]
        trees.append(Tree(place, flip, parts, tree_refs[7 * i:7 * i + 7]))
        ends.append(partial(store_flat, outs[which], base // LANES))
    late_parts = (wq_part, wk_part, wv_part, small_part)
    late = [
        Tree(place, i % 2 == 1, part, tree_refs[7 * (len(cuts) + i):7 * (len(cuts) + i) + 7])
        for i, part in enumerate(late_parts)
    ]

    groups = (slice(0, 3), slice(3, 5), slice(5, 7), slice(7, 9))

    def onward(group, stage, then=None):
        for tree, end in zip(trees[groups[group]], ends[groups[group]]):
            tree.settle(stage, end)
            if stage < 3:
                tree.start(stage + 1)
        if then is not None:
            for tree in trees[groups[then]]:
                tree.start(0)

    def hook(at, act):
        @pl.when(now == at)
        def _():
            act()

    @pl.when(now == 0)
    def _():
        greet_all(devices)
        for tree in trees[groups[0]]:
            tree.start(0)
        onward(0, 0, 1)

    first, lane = feature_lanes(count)
    columns = pl.ds(pl.multiple_of(now * LANES, LANES), LANES)

    def head(mask, at):
        seg, grads = seg_ref[...], g_ref[...]
        ones = key_features(lane, seg, segments).astype(BF16)
        keys = jnp.where(mask, k_ref[...], ones)
        values = jnp.where(mask, v_ref[...], ones)
        lse = lse_ref[:, at:at + 1]
        product = grads.astype(F32) * o_ref[...].astype(F32)
        delta = jnp.sum(jnp.where(mask, product, 0.0), axis=1, keepdims=True)
        hidden = query_features(lane, seg, segments)
        query = jnp.where(mask, q_ref[...], with_column(hidden, lane, segments, -lse).astype(BF16))
        grad = jnp.where(mask, grads, with_column(jnp.zeros_like(hidden), lane, segments, -delta).astype(BF16))
        dqs, dk, dv = [], 0.0, 0.0
        for top in range(0, count, count // PARTS):
            cut = slice(top, top + count // PARTS)
            probs = jnp.exp(dot_nt(keys, query[cut]))
            score = (probs * dot_nt(values, grad[cut])).astype(BF16)
            dv = dv + dot_nn(probs.astype(BF16), grad[cut])
            dk = dk + dot_nn(score, query[cut])
            dqs.append(dot_tn(score, keys))
        return (jnp.concatenate(dqs) * 0.125).astype(BF16), dk.astype(BF16), dv.astype(BF16)

    for ref, one, two in zip((dq_ref, dk_ref, dv_ref), head(first, 0), head(~first, HD)):
        ref[:, columns] = jnp.where(first, one, two)

    hook(1, lambda: (onward(0, 1), onward(1, 0, 2)))
    hook(3, lambda: (onward(0, 2), onward(1, 1), onward(2, 0, 3), [load.start() for load in loads]))
    hook(4, lambda: (onward(1, 2), onward(2, 1), onward(3, 0)))
    hook(5, lambda: (onward(2, 2), onward(3, 1)))

    @pl.when(now == last)
    def _():
        for load in loads:
            load.wait()

        def total_tile(cut, _):
            total_ref[cut, :] = (
                first_ref[cut, :] + dot_nt(dq_ref[cut, :], w_ref[0]) + dot_nt(dk_ref[cut, :], w_ref[1]) + dot_nt(dv_ref[cut, :], w_ref[2])
            ).astype(BF16)

        each_tile(tile, count, total_tile)
        onward(3, 2)
        onward(0, 3)

        def leave(cut, target):
            leaving_ref[cut, :] = select_rows(where_ref[...] == target, total_ref)

        each_tile(tile, count, leave)
        onward(1, 3)
        onward(2, 3)
        onward(3, 3)
        swap.start()
        group = 3 * LANES
        for grad_ref, part, tree in zip((dq_ref, dk_ref, dv_ref), late_parts, late):
            def weight_tile(t, carry, grad_ref=grad_ref, part=part):
                value = dot_tn(rows_ref[:, pl.ds(pl.multiple_of(t * group, group), group)], grad_ref[...])
                for i in range(group // share):
                    d = t * (group // share) + i
                    index = (d // (nk * nc * nb), d // (nk * nc) % nb, d // nk % nc, d % nk)
                    part[index] = value[i * share:(i + 1) * share].astype(BF16)
                return carry

            lax.fori_loop(0, width // group, weight_tile, 0)
            tree.start(0)
        lines_ref[...] = jnp.zeros_like(lines_ref)
        lines_ref[0] = by_device(column_sum(dq_ref[...]), devices, share)
        lines_ref[1] = by_device(column_sum(dv_ref[...]), devices, share)
        for i in range(2, 8):
            lines_ref[i] = by_device(sums_ref[i:i + 1, :], devices, share)
        lines_ref[8] = by_device(bisum_ref[0:1, :], devices, bisum_ref.shape[1] // devices)
        for d in range(devices):
            index = (d // (nk * nc * nb), d // (nk * nc) % nb, d // nk % nc, d % nk)
            small_part[index] = lines_ref[:, d, :].astype(BF16)
        late[3].start(0)
        for stage in range(3):
            for tree in late:
                tree.settle(stage)
                tree.start(stage + 1)
        for tree, out in zip(late, (wq_out, wk_out, wv_out)):
            tree.settle(3, partial(store_flat, out, 0))

        def store_small(value):
            for i, out in enumerate(small_outs):
                out[...] = value[i:i + 1, :out.shape[1]]

        late[3].settle(3, store_small)
        swap.wait()
        for tree in trees + late:
            tree.drain()


PARTS = 1


def backward(segments, segment_col, place_row, q, out, grad, lse, k, v, sums, bi_sum, wi, wu, wo, first_grad, w4, rows):
    count, width = q.shape
    pairs = width // LANES
    devices = wi.shape[0]
    share = width // devices
    sizes = grid_of(devices)
    pair_spec = pl.BlockSpec((count, LANES), lambda h: (0, h))
    anywhere = pl.BlockSpec(memory_space=pl.ANY)
    parts = [x.reshape(sizes + x.shape[1:]) for x in (wi, wu, wo)]
    cuts = []
    for base, size in ((0, 2), (2, 2), (4, 1), (5, 1)):
        for which, x in ((0, wi), (1, wu)):
            cuts.append((which, base * x.shape[2] // 6, size * x.shape[2] // 6, which == 1))
        if base == 0:
            cuts.append((2, 0, wo.shape[2], False))
    trees = []
    for which, _, columns, flip in cuts:
        trees += tree_scratch(sizes, flip, (wi, wu, wo)[which].shape[1], columns)
    for i, shape in enumerate(((share, width),) * 3 + ((16, LANES),)):
        trees += tree_scratch(sizes, i % 2 == 1, *shape)
    flats = [(x.shape[1] * x.shape[2] // LANES, LANES) for x in (wi, wu, wo)] + [(share * width // LANES, LANES)] * 3
    flats += [(1, share)] * 8 + [(1, bi_sum.shape[1] // devices)]
    whole = pltpu.VMEM((count, width), BF16)
    return pl.pallas_call(
        partial(back_kernel, segments, sizes, share, cuts),
        grid=(pairs,),
        out_shape=[jax.ShapeDtypeStruct((count, width), BF16)] + [jax.ShapeDtypeStruct(flat, F32) for flat in flats],
        in_specs=[held_spec((count, 1)), held_spec((1, count))] + [pair_spec] * 6 + [held_spec(sums.shape), held_spec(bi_sum.shape)]
        + [anywhere] * 6,
        out_specs=[anywhere] + [full_spec(flat) for flat in flats],
        scratch_shapes=[whole] * 3 + [pltpu.VMEM((count, width), F32), pltpu.VMEM((3, width, width), BF16), whole, pltpu.SemaphoreType.DMA((3,))]
        + [whole] * 2 + [pltpu.VMEM(sizes + (share, width), BF16)] * 3
        + [pltpu.VMEM((16, devices, LANES), F32), pltpu.VMEM(sizes + (16, LANES), BF16)]
        + [pltpu.SemaphoreType.DMA((2, devices)), pltpu.SemaphoreType.DMA(())] + trees,
        compiler_params=params(63, "arbitrary", collective_id=2, has_side_effects=True),
        cost_estimate=pl.CostEstimate(flops=20 * count * count * width, bytes_accessed=16 * MIB, transcendentals=count * count * 12),
        name="backward",
    )(segment_col, place_row, q, out, grad, lse, k, v, sums, bi_sum, *parts, first_grad, w4, rows)


def emit_kernel(rank_ref, back_hbm, layer_hbm, *refs):
    count = (len(refs) - 5) // 2
    given, tokens_ref, layer_ref, outs, (back_ref, held_ref, sems) = refs[:count], refs[count], refs[count + 1], refs[count + 2:2 * count + 2], refs[2 * count + 2:]
    moved = [
        pltpu.make_async_copy(source, target, sems.at[i])
        for i, (source, target) in enumerate(zip((back_hbm, layer_hbm, *given), (back_ref, held_ref, *outs)))
    ]
    for copy in moved:
        copy.start()
    rows = back_ref.shape[0]
    tile = rows // 4
    for copy in moved[:2]:
        copy.wait()
    lane = lax.broadcasted_iota(jnp.int32, (tile, rows), 1)

    def restore(cut, _):
        chosen = rank_ref[cut, :] == lane
        tokens_ref[cut, :] = select_rows(chosen, back_ref)
        layer_ref[cut, :] = select_rows(chosen, held_ref)

    each_tile(tile, rows, restore)
    for copy in moved[2:]:
        copy.wait()


def emit(rank_col, back, layer, others):
    anywhere = pl.BlockSpec(memory_space=pl.ANY)
    in_vmem = pl.BlockSpec(memory_space=pltpu.VMEM)
    return pl.pallas_call(
        emit_kernel,
        out_shape=[jax.ShapeDtypeStruct(x.shape, x.dtype) for x in (back, layer, *others)],
        in_specs=[in_vmem] + [anywhere] * (2 + len(others)),
        out_specs=[in_vmem] * (2 + len(others)),
        scratch_shapes=[pltpu.VMEM(back.shape, BF16)] * 2 + [pltpu.SemaphoreType.DMA((len(others) + 2,))],
        compiler_params=pltpu.CompilerParams(vmem_limit_bytes=56 * MIB),
        name="emit",
    )(rank_col, back, layer, *others)


def on_device(tokens, cotangent, packed_slot, seq_lengths, query_weight, query_bias, key_weight, value_weight,
              value_bias, output_weight, output_bias, attention_gain, attention_shift, inner_weight, inner_bias,
              outer_weight, outer_bias, final_gain, final_shift):
    devices = lax.axis_size("fsdp")
    count, width = tokens.shape
    hidden_width = inner_bias.shape[0] * devices
    segments = seq_lengths.shape[1]
    share = width // devices
    small = (query_bias, value_bias, output_bias, attention_gain, attention_shift, outer_bias, final_gain, final_shift, inner_bias)
    (attended, lse, rows, q, k, v, g4, gi, gu, leaving_cot, early_cot, place_row, place_col, rank_col, segment_col, vec, bi) = front(
        segments, seq_lengths, packed_slot, tokens, cotangent,
        (query_weight, key_weight, value_weight, output_weight), inner_weight, outer_weight, small,
    )
    w4 = g4.reshape(4, width, width)
    wi = gi.reshape(width, hidden_width)
    wu = gu.reshape(hidden_width, width)
    first_grad, attended_grad, returned, inner_grad, outer_grad, wo_grad, sums, bi_sum = feed_forward(
        devices, place_row, place_col, rows, attended, leaving_cot, early_cot, w4, wi, wu, vec, bi
    )
    inner_grad, outer_grad, wo_grad = (x.reshape(devices, -1, x.shape[-1]) for x in (inner_grad, outer_grad, wo_grad))
    back, inner_grad, outer_grad, wo_grad, wq_grad, wk_grad, wv_grad, *small = backward(
        segments, segment_col, place_row, q, attended, attended_grad, lse, k, v, sums, bi_sum,
        inner_grad, outer_grad, wo_grad, first_grad, w4, rows,
    )
    tokens_grad, layer_out, wq_grad, wk_grad, wv_grad, wo_grad, inner_grad, outer_grad, *small = emit(
        rank_col, back, returned, (wq_grad, wk_grad, wv_grad, wo_grad, inner_grad, outer_grad, *small)
    )
    wq_grad, wk_grad, wv_grad, wo_grad, wi_grad, wu_grad = (
        x.reshape(-1) for x in (wq_grad, wk_grad, wv_grad, wo_grad, inner_grad, outer_grad)
    )
    bq, bv, bo, ga, sa, bu, gf, sf, bi = (x.reshape(-1) for x in small)
    return (layer_out, tokens_grad, wq_grad, bq, wk_grad, wv_grad, bv, wo_grad, bo, ga, sa, wi_grad, bi, wu_grad, bu, gf, sf)


def solution(mesh):
    split, rows = P("fsdp"), P("fsdp", None)
    return jax.shard_map(
        on_device,
        mesh=mesh,
        in_specs=(rows, rows, P(), rows) + (split,) * 15,
        out_specs=(rows, rows) + (split,) * 15,
        check_vma=False,
    )
```

```python
from functools import partial

import jax
import jax.numpy as jnp
from jax import lax
from jax.experimental import pallas as pl
from jax.experimental.pallas import tpu as pltpu
from jax.sharding import PartitionSpec as P

HD = 64
LANES = 128
EPSILON = 1e-12
NEG_LARGE = -1e30
MIB = 1 << 20
F32 = jnp.float32
BF16 = jnp.bfloat16
MESH = pl.DeviceIdType.MESH


def dot_nn(a, b):
    return lax.dot_general(a, b, (((1,), (0,)), ((), ())), preferred_element_type=F32)


def dot_nt(a, b):
    return lax.dot_general(a, b, (((1,), (1,)), ((), ())), preferred_element_type=F32)


def dot_tn(a, b):
    return lax.dot_general(a, b, (((0,), (0,)), ((), ())), preferred_element_type=F32)


def full_spec(shape, **kw):
    return pl.BlockSpec(shape, lambda *_: (0,) * len(shape), **kw)


def held_spec(shape):
    return full_spec(shape, pipeline_mode=pl.Buffered(1))


def params(mib, *axes, **kw):
    return pltpu.CompilerParams(
        dimension_semantics=axes or None, vmem_limit_bytes=mib * MIB, **kw
    )


def grid_of(devices):
    return {32: (4, 2, 2, 2), 128: (4, 4, 4, 2)}.get(devices, (devices, 1, 1, 1))


class Place:
    def __init__(self, sizes):
        na, nb, nc, nk = self.sizes = sizes
        self.me = me = lax.axis_index("fsdp")
        self.k = me % nk
        self.c = (me // nk) % nc
        self.b = (me // (nk * nc)) % nb
        self.a = me // (nk * nc * nb)

    def ahead(self, axis, step):
        own = (self.a, self.b, self.c, self.k)[axis]
        return (own + step) % self.sizes[axis]

    def device(self, axis, step):
        na, nb, nc, nk = self.sizes
        where = [self.a, self.b, self.c, self.k]
        where[axis] = self.ahead(axis, step)
        return ((where[0] * nb + where[1]) * nc + where[2]) * nk + where[3]


def remote(source, target, send_sem, recv_sem, peer):
    return pltpu.make_async_remote_copy(
        src_ref=source, dst_ref=target, send_sem=send_sem, recv_sem=recv_sem,
        device_id=(peer,), device_id_type=MESH,
    )


def greet_all(devices):
    me = lax.axis_index("fsdp")
    barrier = pltpu.get_barrier_semaphore()

    def signal(j, carry):
        pl.semaphore_signal(barrier, inc=1, device_id=((me + j) % devices,), device_id_type=MESH)
        return carry

    lax.fori_loop(1, devices, signal, 0)
    pl.semaphore_wait(barrier, devices - 1)


class Exchange:
    def __init__(self, devices, source, target, sems, local_sem, turns=None):
        self.devices, self.source, self.target, self.sems, self.local_sem = devices, source, target, sems, local_sem
        self.turns = turns or (1, devices)
        self.rows = source.shape[0] // devices
        self.me = lax.axis_index("fsdp")

    def block(self, ref, device):
        return ref.at[pl.ds(pl.multiple_of(device * self.rows, self.rows), self.rows)]

    def own(self):
        return pltpu.make_async_copy(self.block(self.source, self.me), self.block(self.target, self.me), self.local_sem)

    def outgoing(self, j):
        peer = (self.me + j) % self.devices
        return remote(self.block(self.source, peer), self.block(self.target, self.me), self.sems.at[0, j], self.sems.at[1, j], peer)

    def incoming(self, j):
        peer = (self.me + self.devices - j) % self.devices
        block = self.block(self.target, peer)
        return remote(block, block, self.sems.at[0, j], self.sems.at[1, j], peer)

    def over(self, act):
        def body(j, carry):
            act((j * 13) % self.devices)
            return carry

        lax.fori_loop(*self.turns, body, 0)

    def start(self):
        self.own().start()
        self.start_remote()

    def start_remote(self):
        self.over(lambda j: self.outgoing(j).start())

    def wait(self):
        self.wait_remote()
        self.own().wait()

    def wait_remote(self):
        self.over(lambda j: self.incoming(j).wait_recv())
        self.over(lambda j: self.outgoing(j).wait_send())


def greet_peers(place):
    barrier = pltpu.get_barrier_semaphore()
    count = 0
    for axis, size in enumerate(place.sizes):
        for j in range(1, size):
            pl.semaphore_signal(barrier, inc=1, device_id=(place.device(axis, j),), device_id_type=MESH)
            count += 1
    pl.semaphore_wait(barrier, count)


def spread_scratch(sizes):
    return [pltpu.SemaphoreType.DMA((2, 4, max(sizes))), pltpu.SemaphoreType.DMA(())]


class Spread:
    def __init__(self, place, flip, own, out, scratch, lead=()):
        self.place, self.flip, self.mine, self.out, self.lead = place, flip, own, out, lead
        self.sems, self.local_sem = scratch
        self.axes = (0, 1, 2, 3) if flip else (0, 2, 1, 3)

    def region(self, stage, step=0):
        place, every = self.place, slice(None)
        where = [place.a, place.b, place.c, place.k]
        axis = self.axes[stage]
        where[axis] = place.ahead(axis, step)
        for done in self.axes[:stage]:
            where[done] = every
        return self.out.at[self.lead + tuple(where)]

    def local(self):
        return pltpu.make_async_copy(self.mine, self.region(0), self.local_sem)

    def outgoing(self, stage):
        axis = self.axes[stage]
        source = self.mine if stage == 0 else self.region(stage)
        return [
            remote(source, self.region(stage), self.sems.at[0, stage, j], self.sems.at[1, stage, j], self.place.device(axis, j))
            for j in range(1, self.place.sizes[axis])
        ]

    def start(self, stage):
        for copy in self.outgoing(stage):
            copy.start()
        if stage == 0:
            self.local().start()

    def settle(self, stage):
        axis = self.axes[stage]
        if stage == 0:
            self.local().wait()
        for j in range(1, self.place.sizes[axis]):
            block = self.region(stage, self.place.sizes[axis] - j)
            remote(block, block, self.sems.at[0, stage, j], self.sems.at[1, stage, j], self.place.device(axis, j)).wait_recv()

    def drain(self):
        for stage in range(4):
            for copy in self.outgoing(stage):
                copy.wait_send()


def store_flat(ref, base, value):
    rows, columns = value.shape
    width = ref.shape[0] // rows
    for j in range(columns // LANES):
        ref[pl.ds(base + j, rows, stride=width), :] = value[:, j * LANES:(j + 1) * LANES]


def tree_scratch(sizes, flip, rows, columns):
    na, nb, nc, nk = sizes
    one, two = (nb, nc) if flip else (nc, nb)
    shapes = [(na, nb, nc), (nk - 1, na, nb, nc), (one - 1, na, two), (two - 1, na), (na - 1,)]
    return [pltpu.VMEM(shape + (rows, columns), BF16) for shape in shapes] + [
        pltpu.SemaphoreType.DMA((2, 4, max(sizes))),
        pltpu.SemaphoreType.DMA(()),
    ]


class Tree:
    def __init__(self, place, flip, parts, scratch):
        self.place, self.flip, self.parts = place, flip, parts
        self.held, *self.landing, self.sems, self.local_sem = scratch
        order = (3, 1, 2, 0) if flip else (3, 2, 1, 0)
        self.axes = order

    def own(self):
        return pltpu.make_async_copy(self.parts.at[:, :, :, self.place.k], self.held, self.local_sem)

    def outgoing(self, stage):
        place, held = self.place, self.held
        axis = self.axes[stage]
        copies = []
        for j in range(1, place.sizes[axis]):
            other = place.ahead(axis, j)
            if stage == 0:
                source = self.parts.at[:, :, :, other]
            elif stage == 1:
                source = held.at[:, other] if self.flip else held.at[:, :, other]
            elif stage == 2:
                source = held.at[:, place.b, other] if self.flip else held.at[:, other, place.c]
            else:
                source = held.at[other, place.b, place.c]
            copies.append(
                remote(source, self.landing[stage].at[j - 1], self.sems.at[0, stage, j], self.sems.at[1, stage, j], place.device(axis, j))
            )
        return copies

    def start(self, stage):
        if stage == 0:
            self.own().start()
        for copy in self.outgoing(stage):
            copy.start()

    def settle(self, stage, out=None):
        out = out if stage == 3 else None
        place, held, landing = self.place, self.held, self.landing[stage]
        na, nb, nc, nk = place.sizes
        if stage == 0:
            self.own().wait()
        for copy in self.outgoing(stage):
            copy.wait_recv()
        count = place.sizes[self.axes[stage]] - 1

        def total(own, index):
            if count == 1 and out is None:
                return own + landing[(0,) + index]
            value = own.astype(F32)
            for j in range(count):
                value = value + landing[(j,) + index].astype(F32)
            return value

        if stage == 0:
            def add(i, carry):
                held[i] = total(held[i], (i,)).astype(BF16)
                return carry
            lax.fori_loop(0, na, add, 0)
        elif stage == 1:
            two = nc if self.flip else nb
            def add(i, carry):
                for t in range(two):
                    at = (i, place.b, t) if self.flip else (i, t, place.c)
                    held[at] = total(held[at], (i, t)).astype(BF16)
                return carry
            lax.fori_loop(0, na, add, 0)
        elif stage == 2:
            def add(i, carry):
                at = (i, place.b, place.c)
                held[at] = total(held[at], (i,)).astype(BF16)
                return carry
            lax.fori_loop(0, na, add, 0)
        else:
            out(total(held[place.a, place.b, place.c], ()))

    def drain(self):
        for stage in range(4):
            for copy in self.outgoing(stage):
                copy.wait_send()


LOW = 32
EARLY = 2


def select_rows(chosen, rows_ref):
    return dot_nn(jnp.where(chosen, 1.0, 0.0).astype(BF16), rows_ref[...]).astype(BF16)


def count_true(mask, axis):
    return jnp.sum(jnp.where(mask, 1.0, 0.0), axis=axis, keepdims=True)


def each_tile(tile, count, act):
    def body(t, carry):
        at = pl.multiple_of(t * tile, tile)
        act(pl.ds(at, tile), lax.broadcasted_iota(jnp.int32, (tile, count), 0) + at)
        return carry

    lax.fori_loop(0, count // tile, body, 0)


def load_flat(ref, base_ref, width, store):
    total = ref.shape[0]
    base_ref[0:total, :] = ref[...].astype(F32)
    per_row = width // LANES
    for j in range(per_row):
        store(j * LANES, base_ref[pl.ds(j, total // per_row, stride=per_row), :].astype(BF16))


def block_lanes(rows, columns, share):
    lane = lax.broadcasted_iota(jnp.int32, (rows, columns), 1).astype(F32)
    inside = lane - jnp.floor((lane + 0.5) * (1.0 / share)) * share
    return inside == lax.broadcasted_iota(jnp.int32, (rows, columns), 0).astype(F32)


def line_of(blocks, share):
    devices = blocks.shape[0]
    columns = devices * share
    spread = dot_nn(blocks, jnp.where(block_lanes(LANES, columns, share), 1.0, 0.0).astype(BF16))
    start = lax.broadcasted_iota(jnp.int32, (devices, columns), 0) * share
    lane = lax.broadcasted_iota(jnp.int32, (devices, columns), 1)
    return jnp.sum(jnp.where((lane >= start) & (lane < start + share), spread, 0.0), axis=0, keepdims=True)


def split3(column):
    high = column.astype(BF16).astype(F32)
    rest = column - high
    mid = rest.astype(BF16).astype(F32)
    return high, mid, rest - mid


def feature_lanes(rows):
    lane = lax.broadcasted_iota(jnp.int32, (rows, LANES), 1)
    return lane < HD, lane & (HD - 1)


def key_features(lane, segment, segments):
    return jnp.where(lane == segment, 1.0, jnp.where((lane >= segments) & (lane < segments + 3), 1.0, 0.0))


def query_features(lane, segment, segments):
    return jnp.where((lane < segments) & (lane != segment), NEG_LARGE, 0.0)


def with_column(features, lane, start, column):
    high, mid, last = split3(column)
    features = jnp.where(lane == start, high, features)
    features = jnp.where(lane == start + 1, mid, features)
    return jnp.where(lane == start + 2, last, features)


def front_kernel(segments, sizes, cuts, lengths_ref, *refs):
    given, outs, held = refs[:18], refs[18:35], refs[35:53]
    (out_ref, lse_ref, rows_hbm, q_hbm, k_hbm, v_hbm, g4, gi, gu, cot_hbm, cot_out,
     place_row, place_col, rank_out, segment_out, vec_out, bi_out) = outs
    (leaving_ref, arrived_ref, cot_leaving, flat_ref, w4_own, wi_own, wu_own, lines_ref, vec_own, gv, blocks_ref, w_ref, flat_w, slots_ref, rows_ref, q_ref, k_ref, v_ref,
     load_sems, save_sems, w_sem, swap_sems, swap_local, *spread_refs) = refs[53:]
    w4_refs, small_refs = held[:4], held[4:13]
    slots_flat, tokens_ref, cot_ref, wi_ref, wu_ref = held[13:]
    loads = [pltpu.make_async_copy(source, target, load_sems.at[i]) for i, (source, target) in enumerate(zip(given, held))]
    count, width = tokens_ref.shape
    devices = slots_ref.shape[0]
    peer_rows = count // devices
    share = width // devices
    tile = count // 4
    now, last = pl.program_id(0), pl.num_programs(0) - 1
    place = Place(sizes)
    me = place.me
    spreads = [
        Spread(place, False, w4_own.at[pl.ds(0, 2)], g4, spread_refs[0:2], (pl.ds(0, 2),)),
        Spread(place, True, w4_own.at[pl.ds(2, 2)], g4, spread_refs[2:4], (pl.ds(2, 2),)),
        Spread(place, True, vec_own, gv, spread_refs[4:6]),
    ]
    wide = []
    for i, (which, base, columns, flip) in enumerate(cuts):
        own, whole = ((wi_own, gi), (wu_own, gu))[which]
        cut = pl.ds(base, columns)
        wide.append(Spread(place, flip, own.at[:, cut], whole.at[:, :, :, :, :, cut], spread_refs[6 + 2 * i:8 + 2 * i]))
    swap = Exchange(devices, leaving_ref, arrived_ref, swap_sems.at[0], swap_local)
    early = Exchange(devices, cot_leaving, cot_out, swap_sems.at[1], swap_local, (1, devices // EARLY))
    w_load = pltpu.make_async_copy(g4.at[pl.ds(0, 3)], w_ref, w_sem)
    saves = [
        pltpu.make_async_copy(source, target, save_sems.at[i])
        for i, (source, target) in enumerate(((rows_ref, rows_hbm), (q_ref, q_hbm), (k_ref, k_hbm), (v_ref, v_hbm), (cot_leaving, cot_hbm)))
    ]

    def onward(group, stage):
        for spread in group:
            spread.settle(stage)
            if stage < 3:
                spread.start(stage + 1)

    def pair(i):
        return wide[2 * i:2 * i + 2]

    def begin(i):
        for spread in pair(i):
            spread.start(0)

    @pl.when(now == 0)
    def _():
        for load in loads:
            load.start()
        for load in loads[:13]:
            load.wait()
        for i, ref in enumerate(w4_refs):
            def put(at, value, i=i):
                w4_own[i, :, at:at + LANES] = value
            load_flat(ref, flat_ref, width, put)
        lines_ref[...] = jnp.zeros_like(lines_ref)
        for i, ref in enumerate(small_refs):
            lines_ref[i:i + 1, 0:ref.shape[1]] = ref[...].astype(F32)
        vec_own[...] = lines_ref[...].astype(BF16)
        greet_all(devices)
        for spread in spreads:
            spread.start(0)
        for load in loads[13:]:
            load.wait()
        per_row = count // LANES
        for j in range(per_row):
            slots_ref[:, j * LANES:(j + 1) * LANES] = slots_flat[pl.ds(j, devices, stride=per_row), :]

        lane = lax.broadcasted_iota(jnp.int32, (tile, count), 1)
        own_row = slots_ref[pl.ds(me, 1), :]
        own_float = own_row.astype(F32)

        def column_of(row, line):
            return jnp.sum(jnp.where(lane == row, line, 0.0), axis=1, keepdims=True)

        def rank_tile(t, total):
            row = lax.broadcasted_iota(jnp.int32, (tile, count), 0) + t * tile
            return total + count_true(column_of(row, own_float) < own_float, 0)

        rank_row = lax.fori_loop(0, count // tile, rank_tile, jnp.zeros((1, count), F32)).astype(jnp.int32)

        def leave(cut, row):
            leaving_ref[cut, :] = select_rows(rank_row == row, tokens_ref)

        each_tile(tile, count, leave)
        swap.start()
        onward(spreads, 0)

        def put_inner(at, value):
            wi_own[:, at:at + LANES] = value

        def put_outer(at, value):
            wu_own[:, at:at + LANES] = value

        load_flat(wi_ref, flat_ref, wi_own.shape[1], put_inner)
        load_flat(wu_ref, flat_ref, width, put_outer)

        def leave_cot(cut, row):
            cot_leaving[cut, :] = select_rows(rank_row == row, cot_ref)
            rank_out[cut, :] = count_true(own_float < column_of(row, own_float), 1).astype(jnp.int32)

        each_tile(tile, count, leave_cot)
        saves[4].start()
        row = lax.broadcasted_iota(jnp.int32, (count, 1), 0)
        end, segment = 0, jnp.zeros((count, 1), jnp.int32)
        for i in range(lengths_ref.shape[1]):
            end = end + lengths_ref[0, i]
            segment = segment + jnp.where(row >= end, 1, 0)
        segment_out[...] = segment
        onward(spreads, 1)
        begin(0)

        high = count // LOW

        def body(s, total):
            local = slots_ref[pl.ds(s, 1), :] - me * count
            in_high = lax.broadcasted_iota(jnp.int32, (high, count), 0) == (local >> 5)
            in_low = lax.broadcasted_iota(jnp.int32, (LOW, count), 0) == (local & (LOW - 1))
            weight = jnp.where(in_high, s.astype(F32), 0.0).astype(BF16)
            return total + dot_nt(weight, jnp.where(in_low, 1.0, 0.0).astype(BF16))

        source = lax.fori_loop(0, devices, body, jnp.zeros((high, LOW), F32)).astype(BF16)
        over = lax.broadcasted_iota(jnp.int32, (high, count), 1)
        picked = dot_tn(source, jnp.where((over >> 5) == lax.broadcasted_iota(jnp.int32, (high, count), 0), 1.0, 0.0).astype(BF16))
        low_row = lax.broadcasted_iota(jnp.int32, (LOW, count), 0)
        low_wide = lax.broadcasted_iota(jnp.int32, (LOW, count), 1) & (LOW - 1)
        source_row = jnp.sum(jnp.where(low_row == low_wide, picked, 0.0), axis=0, keepdims=True)
        onward(spreads, 2)

        def place_tile(t, places):
            at = pl.multiple_of(t * tile, tile)
            row = lax.broadcasted_iota(jnp.int32, (tile, count), 0) + at
            source_col = column_of(row, source_row)
            same = source_col == source_row
            place_col[pl.ds(at, tile), :] = (source_col * peer_rows + count_true(same & (lane < row), 1)).astype(jnp.int32)
            return places + count_true(same & (row < lane), 0)

        place_row[...] = lax.fori_loop(0, count // tile, place_tile, source_row * peer_rows).astype(jnp.int32)
        onward(spreads, 3)
        w_load.start()
        for i, line in enumerate(small_refs):
            for d in range(devices):
                nk, nc, nb = sizes[3], sizes[2], sizes[1]
                blocks_ref[d:d + 1, :] = gv[d // (nk * nc * nb), d // (nk * nc) % nb, d // nk % nc, d % nk].astype(F32)[i:i + 1, :]
            value = line_of(blocks_ref[...].astype(BF16), line.shape[1])
            if i < 8:
                vec_out[i:i + 1, :] = value
            else:
                bi_out[...] = value
        w_load.wait()
        onward(pair(0), 0)
        begin(1)
        swap.wait()
        vec = vec_out[...]
        wq, wk, wv = (w_ref[i].astype(F32).reshape(width, width).astype(BF16) for i in range(3))
        for i, w in enumerate((wq, wk, wv)):
            flat_w[i] = w

        def project(cut, _):
            rows = select_rows(place_col[cut, :] == lane, arrived_ref)
            rows_ref[cut, :] = rows
            q_ref[cut, :] = ((dot_nn(rows, flat_w[0]) + vec[0:1]).astype(BF16).astype(F32) * 0.125).astype(BF16)
            k_ref[cut, :] = dot_nn(rows, flat_w[1]).astype(BF16)
            v_ref[cut, :] = (dot_nn(rows, flat_w[2]) + vec[1:2]).astype(BF16)

        each_tile(tile, count, project)
        for save in saves[:4]:
            save.start()

    columns = pl.ds(pl.multiple_of(jnp.maximum(now - 1, 0) * LANES, LANES), LANES)
    first, feature = feature_lanes(count)

    def head(mask):
        seg = segment_out[...]
        keys = jnp.where(mask, k_ref[:, columns], key_features(feature, seg, segments).astype(BF16))
        query = jnp.where(mask, q_ref[:, columns], query_features(feature, seg, segments).astype(BF16))
        scores = dot_nt(query, keys)
        top = jnp.max(scores, axis=1, keepdims=True)
        raised = jnp.exp(scores - top)
        total = jnp.sum(raised, axis=1, keepdims=True)
        return dot_nn(raised.astype(BF16), v_ref[:, columns]) * (1.0 / total), top + jnp.log(total)

    def hook(at, act):
        @pl.when(now == at)
        def _():
            act()

    @pl.when(now > 0)
    def _():
        out0, log0 = head(first)
        out1, log1 = head(~first)
        out_ref[...] = jnp.where(first, out0, out1).astype(BF16)
        lse_ref[...] = jnp.where(first, log0, log1)

    hook(0, lambda: (onward(pair(0), 1), begin(2)))
    hook(1, lambda: (onward(pair(1), 0), early.start_remote()))
    hook(2, lambda: onward(pair(2), 0))
    hook(3, lambda: (onward(pair(0), 2), onward(pair(1), 1)))
    hook(4, lambda: onward(pair(2), 1))
    hook(5, lambda: onward(pair(1), 2))

    @pl.when(now == last)
    def _():
        onward(pair(0), 3)
        onward(pair(2), 2)
        onward(pair(1), 3)
        onward(pair(2), 3)
        for spread in spreads + wide:
            spread.drain()
        early.wait_remote()
        for save in saves:
            save.wait()


def front(segments, seq_lengths, packed_slot, tokens, cotangent, w4, wi, wu, small):
    width = tokens.shape[1]
    count = tokens.shape[0]
    devices = packed_slot.shape[0] // count
    hidden_width = small[-1].shape[0] * devices
    sizes = grid_of(devices)
    share = width // devices
    pairs = width // LANES
    anywhere = pl.BlockSpec(memory_space=pl.ANY)
    pair_spec = pl.BlockSpec((count, LANES), lambda i: (0, jnp.maximum(i - 1, 0)))

    def shape(*dims, dtype=BF16):
        return jax.ShapeDtypeStruct(dims, dtype)

    def held(*dims, dtype=BF16):
        return pltpu.VMEM(dims, dtype)

    part = width // 6
    cuts = [(0, 0, hidden_width // 2, False), (0, hidden_width // 2, hidden_width // 2, True),
            (1, 0, 2 * part, False), (1, 2 * part, 2 * part, True), (1, 4 * part, part, False), (1, 5 * part, part, True)]
    flat = [w.reshape(-1, LANES) for w in w4]
    given = flat + [x.reshape(1, -1) for x in small] + [packed_slot.reshape(-1, LANES), tokens, cotangent, wi.reshape(-1, LANES), wu.reshape(-1, LANES)]
    whole = shape(count, width)
    lines = [shape(1, count, dtype=jnp.int32)] + [shape(count, 1, dtype=jnp.int32)] * 3 + [shape(8, width, dtype=F32), shape(1, hidden_width, dtype=F32)]
    return pl.pallas_call(
        partial(front_kernel, segments, sizes, cuts),
        grid=(1 + pairs,),
        out_shape=[whole, shape(count, width, dtype=F32)] + [whole] * 4
        + [shape(4, *sizes, share, width), shape(*sizes, share, hidden_width), shape(*sizes, hidden_width // devices, width), whole, whole] + lines,
        in_specs=[pl.BlockSpec(memory_space=pltpu.SMEM)] + [anywhere] * len(given),
        out_specs=[pair_spec, pair_spec] + [anywhere] * 9 + [full_spec(x.shape) for x in lines],
        scratch_shapes=[pltpu.VMEM(x.shape, x.dtype) for x in given]
        + [held(count, width)] * 3 + [held(*given[-1].shape, dtype=F32), held(4, share, width), held(share, hidden_width),
           held(hidden_width // devices, width), held(16, LANES, dtype=F32), held(16, LANES), held(*sizes, 16, LANES), held(devices, LANES, dtype=F32),
           held(3, *sizes, share, width), held(3, width, width), held(devices, count, dtype=jnp.int32)] + [held(count, width)] * 4
        + [pltpu.SemaphoreType.DMA((len(given),)), pltpu.SemaphoreType.DMA((5,)), pltpu.SemaphoreType.DMA(()),
           pltpu.SemaphoreType.DMA((2, 2, devices)), pltpu.SemaphoreType.DMA(())] + spread_scratch(sizes) * (3 + len(cuts)),
        compiler_params=params(60, "arbitrary", collective_id=1, has_side_effects=True),
        cost_estimate=pl.CostEstimate(flops=16 * count * count * width, bytes_accessed=30 * MIB, transcendentals=count * count * 12),
        name="front",
    )(seq_lengths, *given)


def normalize(hidden):
    centered = hidden - jnp.mean(hidden, axis=1, keepdims=True)
    variance = jnp.mean(centered * centered, axis=1, keepdims=True)
    inverse = lax.rsqrt(variance + EPSILON)
    return centered * inverse, inverse


def normalize_back(grad, normal, inverse):
    return inverse * (
        grad
        - jnp.mean(grad, axis=1, keepdims=True)
        - normal * jnp.mean(grad * normal, axis=1, keepdims=True)
    )


def column_sum(matrix):
    return jnp.sum(matrix.astype(F32), axis=0, keepdims=True)


def feed_kernel(sizes, tiles, chunk, where_ref, place_ref, rows_hbm, att_hbm, cot_hbm, early_hbm, w4_hbm, wi_hbm, wu_hbm, vec_ref, bi_ref,
                first_ref, agrad_ref, returned_hbm, dwi_ref, dwu_ref, dwo_ref, sums_ref, bisum_ref,
                act_ref, inner_ref, slope_ref, turned_ref, outer_ref, low_ref, normal1_ref, normal2_ref, inverse1_ref, inverse2_ref,
                cot_ref, result_ref, leaving_ref, rows_ref, att_ref, wo_ref, wi_ref, wu_ref, load_sems, early_sems, swap_sems, swap_local):
    count = att_ref.shape[0]
    tile = count // tiles
    hidden_width = wi_ref.shape[1]
    devices = sizes[0] * sizes[1] * sizes[2] * sizes[3]
    step, last = pl.program_id(0), pl.num_programs(0) - 1
    vec = vec_ref[...]
    bo, ga, sa, bu, gf, sf = (vec[i:i + 1] for i in range(2, 8))
    enter = Exchange(devices, cot_hbm, cot_ref, swap_sems.at[0], swap_local.at[0], (devices // EARLY, devices))
    early = Exchange(devices, early_hbm, cot_ref, None, None, (1, devices // EARLY))
    loads = [
        pltpu.make_async_copy(source, target, load_sems.at[i])
        for i, (source, target) in enumerate((
            (att_hbm, att_ref), (w4_hbm.at[3], wo_ref), (rows_hbm, rows_ref), (wi_hbm, wi_ref), (wu_hbm, wu_ref)
        ))
    ]

    def early_block(j):
        peer = (early.me + devices - j) % devices
        return pltpu.make_async_copy(early.block(early_hbm, peer), early.block(cot_ref, peer), early_sems.at[j])

    leave = Exchange(devices, leaving_ref, returned_hbm, swap_sems.at[1], swap_local.at[1])

    @pl.when(step == 0)
    def _():
        for load in loads:
            load.start()
        greet_all(devices)
        enter.start()
        early.over(lambda j: early_block(j).start())
        sums_ref[...] = jnp.zeros_like(sums_ref)
        bisum_ref[...] = jnp.zeros_like(bisum_ref)
        for load in loads:
            load.wait()

    @pl.when(step < tiles)
    def _():
        cut = pl.ds(pl.multiple_of(step * tile, tile), tile)
        first_sum = rows_ref[cut, :].astype(F32) + dot_nn(att_ref[cut, :], wo_ref[...]) + bo
        normal1, inverse1 = normalize(first_sum)
        normal1_ref[cut, :] = normal1
        inverse1_ref[cut, :] = inverse1
        normed = normal1 * ga + sa
        normed_low = normed.astype(BF16)
        turned_ref[:, cut] = normed.T.astype(BF16)
        second = normed + bu
        for at in range(0, hidden_width, chunk):
            pre = dot_nn(normed_low, wi_ref[:, at:at + chunk]) + bi_ref[:, at:at + chunk]
            share = 0.5 + 0.5 * lax.erf(pre * 0.7071067811865476)
            act = (pre * share).astype(BF16)
            act_ref[cut, at:at + chunk] = act
            slope_ref[cut, at:at + chunk] = (share + pre * (jnp.exp(pre * pre * -0.5) * 0.3989422804014327)).astype(BF16)
            second = second + dot_nn(act, wu_ref[at:at + chunk, :])
        normal2, inverse2 = normalize(second)
        normal2_ref[cut, :] = normal2
        inverse2_ref[cut, :] = inverse2
        result_ref[cut, :] = (normal2 * gf + sf).astype(BF16)

    @pl.when(step == tiles)
    def _():
        def leave_tile(cut, target):
            leaving_ref[cut, :] = select_rows(where_ref[...] == target, result_ref)

        each_tile(tile, count, leave_tile)
        leave.start()
        early.over(lambda j: early_block(j).wait())
        enter.wait()

    @pl.when((step >= tiles) & (step < 2 * tiles))
    def _():
        cut = pl.ds(pl.multiple_of((step - tiles) * tile, tile), tile)
        lane = lax.broadcasted_iota(jnp.int32, (tile, count), 1)
        chosen = jnp.where(place_ref[...] == lane, 1.0, 0.0).astype(BF16)
        cot = dot_nn(chosen, cot_ref[...])
        normal1, normal2 = normal1_ref[cut, :], normal2_ref[cut, :]
        second_grad = normalize_back(cot * gf, normal2, inverse2_ref[cut, :])
        outer_low = second_grad.astype(BF16)
        outer_ref[cut, :] = outer_low
        normed_grad = second_grad
        for at in range(0, hidden_width, chunk):
            act_grad = dot_nt(outer_low, wu_ref[at:at + chunk, :])
            inner_low = (act_grad * slope_ref[cut, at:at + chunk].astype(F32)).astype(BF16)
            inner_ref[cut, at:at + chunk] = inner_low
            bisum_ref[0:1, at:at + chunk] += column_sum(inner_low)
            normed_grad = normed_grad + dot_nt(inner_low, wi_ref[:, at:at + chunk])
        first_grad = normalize_back(normed_grad * ga, normal1, inverse1_ref[cut, :])
        first_ref[...] = first_grad
        branch_low = first_grad.astype(BF16)
        low_ref[cut, :] = branch_low
        agrad_ref[...] = dot_nt(branch_low, wo_ref[...]).astype(BF16)
        sums_ref[2:3, :] += column_sum(branch_low)
        sums_ref[3:4, :] += column_sum(normed_grad * normal1)
        sums_ref[4:5, :] += column_sum(normed_grad)
        sums_ref[5:6, :] += column_sum(outer_low)
        sums_ref[6:7, :] += column_sum(cot * normal2)
        sums_ref[7:8, :] += column_sum(cot)

    @pl.when(step >= 2 * tiles)
    def _():
        cut = pl.ds(pl.multiple_of((step - 2 * tiles) * chunk, chunk), chunk)
        dwi_ref[...] = dot_nn(turned_ref[...], inner_ref[:, cut]).astype(BF16)
        dwu_ref[...] = dot_tn(act_ref[:, cut], outer_ref[...]).astype(BF16)

    @pl.when(step == last)
    def _():
        dwo_ref[...] = dot_tn(att_ref[...], low_ref[...]).astype(BF16)
        leave.wait()


def feed_forward(devices, place_row, place_col, rows, attended, leaving_cot, early_cot, w4, wi, wu, vec, bi):
    count, width = rows.shape
    hidden_width = wi.shape[1]
    tiles, chunk = 4, 768
    tile = count // tiles
    anywhere = pl.BlockSpec(memory_space=pl.ANY)
    back_spec = pl.BlockSpec((tile, width), lambda i: (jnp.clip(i - tiles, 0, tiles - 1), 0))
    parts = hidden_width // chunk

    def part(i):
        return jnp.clip(i - 2 * tiles, 0, parts - 1)

    def held(n, dtype=BF16):
        return pltpu.VMEM((count, n), dtype)

    return pl.pallas_call(
        partial(feed_kernel, grid_of(devices), tiles, chunk),
        grid=(2 * tiles + parts,),
        out_shape=[
            jax.ShapeDtypeStruct((count, width), F32), jax.ShapeDtypeStruct((count, width), BF16), jax.ShapeDtypeStruct((count, width), BF16),
            jax.ShapeDtypeStruct((width, hidden_width), BF16), jax.ShapeDtypeStruct((hidden_width, width), BF16),
            jax.ShapeDtypeStruct((width, width), BF16), jax.ShapeDtypeStruct((8, width), F32), jax.ShapeDtypeStruct((8, hidden_width), F32),
        ],
        in_specs=[
            held_spec((1, count)), pl.BlockSpec((tile, 1), lambda i: (jnp.clip(i - tiles, 0, tiles - 1), 0)),
            anywhere, anywhere, anywhere, anywhere, anywhere, anywhere, anywhere, held_spec(vec.shape), held_spec(bi.shape),
        ],
        out_specs=[
            back_spec, back_spec, anywhere,
            pl.BlockSpec((width, chunk), lambda i: (0, part(i))), pl.BlockSpec((chunk, width), lambda i: (part(i), 0)),
            full_spec((width, width)), full_spec((8, width)), full_spec((8, hidden_width)),
        ],
        scratch_shapes=[
            held(hidden_width), held(hidden_width), held(hidden_width), pltpu.VMEM((width, count), BF16), held(width), held(width),
            held(width, F32), held(width, F32), held(1, F32), held(1, F32), held(width), held(width), held(width),
            held(width), held(width), pltpu.VMEM((width, width), BF16), pltpu.VMEM(wi.shape, BF16), pltpu.VMEM(wu.shape, BF16),
            pltpu.SemaphoreType.DMA((5,)), pltpu.SemaphoreType.DMA((devices,)), pltpu.SemaphoreType.DMA((2, 2, devices)), pltpu.SemaphoreType.DMA((2,)),
        ],
        compiler_params=params(62, "arbitrary", collective_id=5, has_side_effects=True),
        cost_estimate=pl.CostEstimate(flops=20 * count * width * hidden_width, bytes_accessed=36 * MIB, transcendentals=2 * count * hidden_width),
        name="feed_forward",
    )(place_row, place_col, rows, attended, leaving_cot, early_cot, w4, wi, wu, vec, bi)


def by_device(line, devices, share):
    count = line.shape[1]
    start = lax.broadcasted_iota(jnp.int32, (devices, count), 0) * share
    lane = lax.broadcasted_iota(jnp.int32, (devices, count), 1)
    left = jnp.where((lane >= start) & (lane < start + share), line, 0.0).astype(BF16)
    return dot_nt(left, jnp.where(block_lanes(LANES, count, share), 1.0, 0.0).astype(BF16))


def back_kernel(segments, sizes, share, cuts, seg_ref, where_ref, q_ref, o_ref, g_ref, lse_ref, k_ref, v_ref, sums_ref, bisum_ref,
                wi_ref, wu_ref, wo_ref, first_hbm, w4_hbm, rows_hbm, *refs):
    back_ref, wi_out, wu_out, wo_out, wq_out, wk_out, wv_out, *small_outs = refs[:16]
    (dq_ref, dk_ref, dv_ref, first_ref, w_ref, rows_ref, load_sems, total_ref, leaving_ref, wq_part, wk_part, wv_part,
     lines_ref, small_part, swap_sems, swap_local, *tree_refs) = refs[16:]
    count, width = total_ref.shape
    na, nb, nc, nk = sizes
    devices = na * nb * nc * nk
    tile = count // 4
    now, last = pl.program_id(0), pl.num_programs(0) - 1
    place = Place(sizes)
    loads = [
        pltpu.make_async_copy(source, target, load_sems.at[i])
        for i, (source, target) in enumerate(((first_hbm, first_ref), (w4_hbm.at[pl.ds(0, 3)], w_ref), (rows_hbm, rows_ref)))
    ]
    swap = Exchange(devices, leaving_ref, back_ref, swap_sems, swap_local)
    outs = {0: wi_out, 1: wu_out, 2: wo_out}
    every = (slice(None),) * 5
    trees, ends = [], []
    for i, (which, base, columns, flip) in enumerate(cuts):
        parts = (wi_ref, wu_ref, wo_ref)[which].at[every + (pl.ds(base, columns),)]
        trees.append(Tree(place, flip, parts, tree_refs[7 * i:7 * i + 7]))
        ends.append(partial(store_flat, outs[which], base // LANES))
    late_parts = (wq_part, wk_part, wv_part, small_part)
    late = [
        Tree(place, i % 2 == 1, part, tree_refs[7 * (len(cuts) + i):7 * (len(cuts) + i) + 7])
        for i, part in enumerate(late_parts)
    ]

    groups = (slice(0, 3), slice(3, 5), slice(5, 7), slice(7, 9))

    def onward(group, stage, then=None):
        for tree, end in zip(trees[groups[group]], ends[groups[group]]):
            tree.settle(stage, end)
            if stage < 3:
                tree.start(stage + 1)
        if then is not None:
            for tree in trees[groups[then]]:
                tree.start(0)

    def hook(at, act):
        @pl.when(now == at)
        def _():
            act()

    @pl.when(now == 0)
    def _():
        greet_all(devices)
        for tree in trees[groups[0]]:
            tree.start(0)
        onward(0, 0, 1)

    first, lane = feature_lanes(count)
    columns = pl.ds(pl.multiple_of(now * LANES, LANES), LANES)

    def head(mask, at):
        seg, grads = seg_ref[...], g_ref[...]
        ones = key_features(lane, seg, segments).astype(BF16)
        keys = jnp.where(mask, k_ref[...], ones)
        values = jnp.where(mask, v_ref[...], ones)
        lse = lse_ref[:, at:at + 1]
        product = grads.astype(F32) * o_ref[...].astype(F32)
        delta = jnp.sum(jnp.where(mask, product, 0.0), axis=1, keepdims=True)
        hidden = query_features(lane, seg, segments)
        query = jnp.where(mask, q_ref[...], with_column(hidden, lane, segments, -lse).astype(BF16))
        grad = jnp.where(mask, grads, with_column(jnp.zeros_like(hidden), lane, segments, -delta).astype(BF16))
        dqs, dk, dv = [], 0.0, 0.0
        for top in range(0, count, count // PARTS):
            cut = slice(top, top + count // PARTS)
            probs = jnp.exp(dot_nt(keys, query[cut]))
            score = (probs * dot_nt(values, grad[cut])).astype(BF16)
            dv = dv + dot_nn(probs.astype(BF16), grad[cut])
            dk = dk + dot_nn(score, query[cut])
            dqs.append(dot_tn(score, keys))
        return (jnp.concatenate(dqs) * 0.125).astype(BF16), dk.astype(BF16), dv.astype(BF16)

    for ref, one, two in zip((dq_ref, dk_ref, dv_ref), head(first, 0), head(~first, HD)):
        ref[:, columns] = jnp.where(first, one, two)

    hook(1, lambda: (onward(0, 1), onward(1, 0, 2)))
    hook(3, lambda: (onward(0, 2), onward(1, 1), onward(2, 0, 3), [load.start() for load in loads]))
    hook(4, lambda: (onward(1, 2), onward(2, 1), onward(3, 0)))
    hook(5, lambda: (onward(2, 2), onward(3, 1)))

    @pl.when(now == last)
    def _():
        for load in loads:
            load.wait()

        def total_tile(cut, _):
            total_ref[cut, :] = (
                first_ref[cut, :] + dot_nt(dq_ref[cut, :], w_ref[0]) + dot_nt(dk_ref[cut, :], w_ref[1]) + dot_nt(dv_ref[cut, :], w_ref[2])
            ).astype(BF16)

        each_tile(tile, count, total_tile)
        onward(3, 2)
        onward(0, 3)

        def leave(cut, target):
            leaving_ref[cut, :] = select_rows(where_ref[...] == target, total_ref)

        each_tile(tile, count, leave)
        onward(1, 3)
        onward(2, 3)
        onward(3, 3)
        swap.start()
        group = 3 * LANES
        for grad_ref, part, tree in zip((dq_ref, dk_ref, dv_ref), late_parts, late):
            def weight_tile(t, carry, grad_ref=grad_ref, part=part):
                value = dot_tn(rows_ref[:, pl.ds(pl.multiple_of(t * group, group), group)], grad_ref[...])
                for i in range(group // share):
                    d = t * (group // share) + i
                    index = (d // (nk * nc * nb), d // (nk * nc) % nb, d // nk % nc, d % nk)
                    part[index] = value[i * share:(i + 1) * share].astype(BF16)
                return carry

            lax.fori_loop(0, width // group, weight_tile, 0)
            tree.start(0)
        lines_ref[...] = jnp.zeros_like(lines_ref)
        lines_ref[0] = by_device(column_sum(dq_ref[...]), devices, share)
        lines_ref[1] = by_device(column_sum(dv_ref[...]), devices, share)
        for i in range(2, 8):
            lines_ref[i] = by_device(sums_ref[i:i + 1, :], devices, share)
        lines_ref[8] = by_device(bisum_ref[0:1, :], devices, bisum_ref.shape[1] // devices)
        for d in range(devices):
            index = (d // (nk * nc * nb), d // (nk * nc) % nb, d // nk % nc, d % nk)
            small_part[index] = lines_ref[:, d, :].astype(BF16)
        late[3].start(0)
        for stage in range(3):
            for tree in late:
                tree.settle(stage)
                tree.start(stage + 1)
        for tree, out in zip(late, (wq_out, wk_out, wv_out)):
            tree.settle(3, partial(store_flat, out, 0))

        def store_small(value):
            for i, out in enumerate(small_outs):
                out[...] = value[i:i + 1, :out.shape[1]]

        late[3].settle(3, store_small)
        swap.wait()
        for tree in trees + late:
            tree.drain()


PARTS = 1


def backward(segments, segment_col, place_row, q, out, grad, lse, k, v, sums, bi_sum, wi, wu, wo, first_grad, w4, rows):
    count, width = q.shape
    pairs = width // LANES
    devices = wi.shape[0]
    share = width // devices
    sizes = grid_of(devices)
    pair_spec = pl.BlockSpec((count, LANES), lambda h: (0, h))
    anywhere = pl.BlockSpec(memory_space=pl.ANY)
    parts = [x.reshape(sizes + x.shape[1:]) for x in (wi, wu, wo)]
    cuts = []
    for base, size in ((0, 2), (2, 2), (4, 1), (5, 1)):
        for which, x in ((0, wi), (1, wu)):
            cuts.append((which, base * x.shape[2] // 6, size * x.shape[2] // 6, which == 1))
        if base == 0:
            cuts.append((2, 0, wo.shape[2], False))
    trees = []
    for which, _, columns, flip in cuts:
        trees += tree_scratch(sizes, flip, (wi, wu, wo)[which].shape[1], columns)
    for i, shape in enumerate(((share, width),) * 3 + ((16, LANES),)):
        trees += tree_scratch(sizes, i % 2 == 1, *shape)
    flats = [(x.shape[1] * x.shape[2] // LANES, LANES) for x in (wi, wu, wo)] + [(share * width // LANES, LANES)] * 3
    flats += [(1, share)] * 8 + [(1, bi_sum.shape[1] // devices)]
    whole = pltpu.VMEM((count, width), BF16)
    return pl.pallas_call(
        partial(back_kernel, segments, sizes, share, cuts),
        grid=(pairs,),
        out_shape=[jax.ShapeDtypeStruct((count, width), BF16)] + [jax.ShapeDtypeStruct(flat, F32) for flat in flats],
        in_specs=[held_spec((count, 1)), held_spec((1, count))] + [pair_spec] * 6 + [held_spec(sums.shape), held_spec(bi_sum.shape)]
        + [anywhere] * 6,
        out_specs=[anywhere] + [full_spec(flat) for flat in flats],
        scratch_shapes=[whole] * 3 + [pltpu.VMEM((count, width), F32), pltpu.VMEM((3, width, width), BF16), whole, pltpu.SemaphoreType.DMA((3,))]
        + [whole] * 2 + [pltpu.VMEM(sizes + (share, width), BF16)] * 3
        + [pltpu.VMEM((16, devices, LANES), F32), pltpu.VMEM(sizes + (16, LANES), BF16)]
        + [pltpu.SemaphoreType.DMA((2, devices)), pltpu.SemaphoreType.DMA(())] + trees,
        compiler_params=params(63, "arbitrary", collective_id=2, has_side_effects=True),
        cost_estimate=pl.CostEstimate(flops=20 * count * count * width, bytes_accessed=16 * MIB, transcendentals=count * count * 12),
        name="backward",
    )(segment_col, place_row, q, out, grad, lse, k, v, sums, bi_sum, *parts, first_grad, w4, rows)


def emit_kernel(count, rank_ref, back_hbm, layer_hbm, *refs):
    given, tokens_hbm, layer_out, outs = refs[:count], refs[count], refs[count + 1], refs[count + 2:2 * count + 2]
    back_ref, held_ref, tokens_ref, layer_ref, *staged, sems, save_sems = refs[2 * count + 2:]
    moved = [
        pltpu.make_async_copy(source, target, sems.at[i])
        for i, (source, target) in enumerate(zip((back_hbm, layer_hbm, *given), (back_ref, held_ref, *staged)))
    ]
    saves = [
        pltpu.make_async_copy(source, target, save_sems.at[i])
        for i, (source, target) in enumerate(zip((tokens_ref, layer_ref, *staged), (tokens_hbm, layer_out, *outs)))
    ]
    for copy in moved:
        copy.start()
    rows = back_ref.shape[0]
    tile = rows // 4
    lane = lax.broadcasted_iota(jnp.int32, (tile, rows), 1)

    def restore(source, target):
        def act(cut, _):
            target[cut, :] = select_rows(rank_ref[cut, :] == lane, source)
        return act

    moved[0].wait()
    each_tile(tile, rows, restore(back_ref, tokens_ref))
    saves[0].start()
    for copy, save in zip(moved[2:], saves[2:]):
        copy.wait()
        save.start()
    moved[1].wait()
    each_tile(tile, rows, restore(held_ref, layer_ref))
    saves[1].start()
    for save in saves:
        save.wait()


def emit(rank_col, back, layer, others):
    anywhere = pl.BlockSpec(memory_space=pl.ANY)
    in_vmem = pl.BlockSpec(memory_space=pltpu.VMEM)
    return pl.pallas_call(
        partial(emit_kernel, len(others)),
        out_shape=[jax.ShapeDtypeStruct(x.shape, x.dtype) for x in (back, layer, *others)],
        in_specs=[in_vmem] + [anywhere] * (2 + len(others)),
        out_specs=[anywhere] * (2 + len(others)),
        scratch_shapes=[pltpu.VMEM(back.shape, BF16)] * 4 + [pltpu.VMEM(x.shape, x.dtype) for x in others]
        + [pltpu.SemaphoreType.DMA((len(others) + 2,))] * 2,
        compiler_params=pltpu.CompilerParams(vmem_limit_bytes=56 * MIB),
        name="emit",
    )(rank_col, back, layer, *others)


def on_device(tokens, cotangent, packed_slot, seq_lengths, query_weight, query_bias, key_weight, value_weight,
              value_bias, output_weight, output_bias, attention_gain, attention_shift, inner_weight, inner_bias,
              outer_weight, outer_bias, final_gain, final_shift):
    devices = lax.axis_size("fsdp")
    count, width = tokens.shape
    hidden_width = inner_bias.shape[0] * devices
    segments = seq_lengths.shape[1]
    share = width // devices
    small = (query_bias, value_bias, output_bias, attention_gain, attention_shift, outer_bias, final_gain, final_shift, inner_bias)
    (attended, lse, rows, q, k, v, g4, gi, gu, leaving_cot, early_cot, place_row, place_col, rank_col, segment_col, vec, bi) = front(
        segments, seq_lengths, packed_slot, tokens, cotangent,
        (query_weight, key_weight, value_weight, output_weight), inner_weight, outer_weight, small,
    )
    w4 = g4.reshape(4, width, width)
    wi = gi.reshape(width, hidden_width)
    wu = gu.reshape(hidden_width, width)
    first_grad, attended_grad, returned, inner_grad, outer_grad, wo_grad, sums, bi_sum = feed_forward(
        devices, place_row, place_col, rows, attended, leaving_cot, early_cot, w4, wi, wu, vec, bi
    )
    inner_grad, outer_grad, wo_grad = (x.reshape(devices, -1, x.shape[-1]) for x in (inner_grad, outer_grad, wo_grad))
    back, inner_grad, outer_grad, wo_grad, wq_grad, wk_grad, wv_grad, *small = backward(
        segments, segment_col, place_row, q, attended, attended_grad, lse, k, v, sums, bi_sum,
        inner_grad, outer_grad, wo_grad, first_grad, w4, rows,
    )
    tokens_grad, layer_out, wq_grad, wk_grad, wv_grad, wo_grad, inner_grad, outer_grad, *small = emit(
        rank_col, back, returned, (wq_grad, wk_grad, wv_grad, wo_grad, inner_grad, outer_grad, *small)
    )
    wq_grad, wk_grad, wv_grad, wo_grad, wi_grad, wu_grad = (
        x.reshape(-1) for x in (wq_grad, wk_grad, wv_grad, wo_grad, inner_grad, outer_grad)
    )
    bq, bv, bo, ga, sa, bu, gf, sf, bi = (x.reshape(-1) for x in small)
    return (layer_out, tokens_grad, wq_grad, bq, wk_grad, wv_grad, bv, wo_grad, bo, ga, sa, wi_grad, bi, wu_grad, bu, gf, sf)


def solution(mesh):
    split, rows = P("fsdp"), P("fsdp", None)
    return jax.shard_map(
        on_device,
        mesh=mesh,
        in_specs=(rows, rows, P(), rows) + (split,) * 15,
        out_specs=(rows, rows) + (split,) * 15,
        check_vma=False,
    )
```
